32 devices in a mesh: seq: 8 (over z, x), head: 4 (over y, core).
Axes of the slice: x: 2, y: 2, z: 4, core: 2. Of those that a mesh axis runs over, the one named last changes fastest.
Arguments:
- block_input: bfloat16 [4096, 1024], P('seq'), may hold values from -6 to 6
- norm1_gain: float32 [1024], replicated, may hold values from 0.5 to 1.5
- w_in: bfloat16 [1024, 8, 768], P(None, 'head'), may hold values from -0.1875 to 0.1875
- w_ba: bfloat16 [1024, 2, 8], P(None, None, 'head'), may hold values from -0.1875 to 0.1875
- conv_weight: float32 [512, 8, 4], P(None, 'head'), may hold values from -2.5 to 2.5
- decay_log: float32 [8], P('head'), may hold values from -9 to -3.5
- gnorm_gain: float32 [256], replicated, may hold values from 0.5 to 1.5
- w_out: bfloat16 [256, 8, 1024], P(None, 'head'), may hold values from -0.1875 to 0.1875
- norm2_gain: float32 [1024], replicated, may hold values from 0.5 to 1.5
- w_up: bfloat16 [1024, 2, 2816], P(None, None, 'head'), may hold values from -0.1875 to 0.1875
- w_down: bfloat16 [1024, 2816], P(None, 'head'), may hold values from -0.15625 to 0.15625
- grad_out: bfloat16 [4096, 1024], P('seq'), may hold values from -6 to 6
Outputs:
- result: float32 [4096, 1024], P('seq')
- input_grad: float32 [4096, 1024], P('seq')
- norm1_gain_grad: float32 [1024], replicated
- input_weight_gradient: float32 [1024, 8, 768], P('seq', 'head')
- w_ba_grad: float32 [1024, 2, 8], P('seq', None, 'head')
- conv_grad: float32 [512, 8, 4], P('seq', 'head')
- log_decay_gradient: float32 [8], P('head')
- gnorm_gain_grad: float32 [256], replicated
- w_out_grad: float32 [256, 8, 1024], P('seq', 'head')
- norm2_gain_grad: float32 [1024], replicated
- w_up_grad: float32 [1024, 2, 2816], P('seq', None, 'head')
- w_down_grad: float32 [1024, 2816], P('seq', 'head')
The draws below stay inside these ranges and needn't reach their ends.
All inputs are finite; a program needn't handle non-finite values.
Results may differ from the reference program's by a relative error of at most 0.025.
The reference program's roundings to bfloat16 on the way (of `normed`, `projected`, `gated_out`, `hidden_n`, `swish`, `gate_up_grad`, `stream_b` and `proj_grad`) count: a program that leaves them out, or rounds other values in their place, can miss the bound.
Values may be sent and summed in bfloat16 or wider, within the bound.
A program may use at most 128 MiB of HBM per device.

```python
import jax
import jax.numpy as jnp
from jax import lax

D = 1024
H = 8
DK = 128
DV = 256
FF = 2816
CONV = 4
STRETCH = 64
TOKENS = 4096
N_HEAD = 4


def level_of(own_key, shape, cuts, low, largest):
    def one(position, blocks):
        draws = jax.random.uniform(jax.random.fold_in(jax.random.fold_in(own_key, 6), position), (blocks,), jnp.float32, low / len(cuts), largest / len(cuts))
        return jnp.repeat(jnp.exp(draws), shape[position] // blocks).reshape((-1,) + (1,) * (len(shape) - position - 1))

    factor_of = one(*cuts[0])
    for cut in cuts[1:]:
        factor_of = factor_of * one(*cut)
    return factor_of


def gaussian(stream_key, extent, scale, most, cuts=(), kind=jnp.bfloat16):
    drawn = scale * jax.random.normal(stream_key, extent, jnp.float32)
    if cuts:
        drawn = drawn * level_of(stream_key, extent, cuts, -0.22, 0.18)
    return jnp.clip(drawn, -most, most).astype(kind)


def setup_inputs(seed: int = 0) -> dict:
    seeds = jax.random.split(jax.random.key(seed), 13)
    block_input = gaussian(seeds[0], (TOKENS, D), 1.0, 6.0, ((0, 8),))
    norm1_gain = jnp.clip(1.0 + 0.1 * jax.random.normal(seeds[1], (D,), jnp.float32), 0.5, 1.5)
    w_in = gaussian(seeds[2], (D, H, 2 * DK + 2 * DV), D ** -0.5, 0.1875, ((1, 4),))
    w_ba = gaussian(seeds[3], (D, 2, H), D ** -0.5, 0.1875, ((2, 4),))
    conv_weight = gaussian(seeds[4], (2 * DK + DV, H, CONV), 0.5, 2.5, ((1, 4),), jnp.float32)
    decay_log = jnp.clip(-9.0 + 5.5 * jax.random.uniform(seeds[5], (H,), jnp.float32) ** level_of(seeds[5], (H,), ((0, 4),), -0.2, 0.2), -9.0, -3.5)
    gnorm_gain = jnp.clip(1.0 + 0.1 * jax.random.normal(seeds[6], (DV,), jnp.float32), 0.5, 1.5)
    w_out = gaussian(seeds[7], (DV, H, D), (H * DV // 2) ** -0.5, 0.1875, ((1, 4),))
    norm2_gain = jnp.clip(1.0 + 0.1 * jax.random.normal(seeds[8], (D,), jnp.float32), 0.5, 1.5)
    w_up = gaussian(seeds[9], (D, 2, FF), D ** -0.5, 0.1875, ((2, 4),))
    w_down = gaussian(seeds[10], (D, FF), (FF // 2) ** -0.5, 0.15625, ((1, 4),))
    grad_out = gaussian(seeds[11], (TOKENS, D), 1.0, 6.0, ((0, 8),))
    return {"block_input": block_input, "norm1_gain": norm1_gain, "w_in": w_in, "w_ba": w_ba, "conv_weight": conv_weight, "decay_log": decay_log, "gnorm_gain": gnorm_gain, "w_out": w_out, "norm2_gain": norm2_gain, "w_up": w_up, "w_down": w_down, "grad_out": grad_out}


EPSILON = 1e-06
NEGATIVE = -1e+30
MATMUL_ACCURACY = lax.Precision.HIGHEST

def dot_high(left, right):
    return jnp.dot(left, right, precision=MATMUL_ACCURACY)

def rms_apply(values, gain):
    return values * lax.rsqrt(lax.optimization_barrier(jnp.mean(values * values, axis=-1, keepdims=True)) + EPSILON) * gain

def features(edged, mixer_in, conv_weight, decay_log):
    length = edged.shape[0] - (CONV - 1)
    mixed = edged[0:length] * conv_weight[:, :, 0].T
    for index in range(1, CONV):
        mixed = mixed + edged[index:index + length] * conv_weight[:, :, index].T
    active = jax.nn.silu(mixed)
    query = active[..., :DK]
    key = active[..., DK:2 * DK]
    value = active[..., 2 * DK:]
    query = query * lax.rsqrt(lax.optimization_barrier(jnp.sum(query * query, axis=-1, keepdims=True)) + EPSILON) * DK ** (-0.5)
    key = key * lax.rsqrt(lax.optimization_barrier(jnp.sum(key * key, axis=-1, keepdims=True)) + EPSILON)
    beta = jax.nn.sigmoid(mixer_in[:, 0])
    logdecay = -jnp.exp(decay_log) * jax.nn.softplus(mixer_in[:, 1])
    return (query, key, value, beta, logdecay)

def stretch_terms(query, key, value, beta, logdecay):
    width = query.shape[0]
    cumul = jnp.cumsum(logdecay)
    spread = cumul[:, None] - cumul[None, :]
    row_pos = lax.broadcasted_iota(jnp.int32, (width, width), 0)
    column = lax.broadcasted_iota(jnp.int32, (width, width), 1)
    strict = jnp.exp(jnp.where(row_pos > column, spread, NEGATIVE))
    inclusive = jnp.exp(jnp.where(row_pos >= column, spread, NEGATIVE))
    lower = beta[:, None] * strict * dot_high(key, key.T)
    system = jnp.eye(width, dtype=query.dtype) + lower
    solved_value = jax.scipy.linalg.solve_triangular(system, beta[:, None] * value, lower=True, unit_diagonal=True)
    solved_key = jax.scipy.linalg.solve_triangular(system, (beta * jnp.exp(cumul))[:, None] * key, lower=True, unit_diagonal=True)
    scores = inclusive * dot_high(query, key.T)
    query_map = jnp.exp(cumul)[:, None] * query - dot_high(scores, solved_key)
    out_fixed = dot_high(scores, solved_value)
    key_end = jnp.exp(cumul[-1] - cumul)[:, None] * key
    transit = jnp.exp(cumul[-1]) * jnp.eye(key.shape[1], dtype=query.dtype) - dot_high(key_end.T, solved_key)
    feed = dot_high(key_end.T, solved_value)
    return (query_map, out_fixed, transit, feed)

def stretch_head(query, key, value, beta, logdecay):
    count = query.shape[0] // STRETCH

    def split(array):
        return array.reshape((count, STRETCH) + array.shape[1:])
    return jax.vmap(stretch_terms)(split(query), split(key), split(value), split(beta), split(logdecay))

def stretch_heads(query, key, value, beta, logdecay):
    return jax.vmap(stretch_head, in_axes=1, out_axes=0)(query, key, value, beta, logdecay)

def scan_head(terms, state):

    def advance(carry, parts):
        query_map, out_fixed, transit, feed = parts
        return (dot_high(transit, carry) + feed, dot_high(query_map, carry) + out_fixed)
    final, layer_outputs = lax.scan(advance, state, terms)
    return (layer_outputs.reshape(-1, state.shape[1]), final)

def scan_heads(terms, state):
    return jax.vmap(scan_head, in_axes=(0, 0), out_axes=(1, 0))(terms, state)

def gated(layer_outputs, gate, gain):
    return rms_apply(layer_outputs, gain) * jax.nn.silu(gate)

def swiglu(gate_up):
    return jax.nn.silu(gate_up[:, 0]) * gate_up[:, 1]

def group_total(left, right):
    part_width = left.shape[1] // N_HEAD
    total = jnp.zeros((left.shape[0], right.shape[1]), jnp.float32)
    for group in range(N_HEAD):
        part = jnp.dot(left[:, group * part_width:(group + 1) * part_width].astype(jnp.float32), right[group * part_width:(group + 1) * part_width].astype(jnp.float32), preferred_element_type=jnp.float32)
        rounded = lax.optimization_barrier(part.astype(jnp.bfloat16))
        total = total + rounded.astype(jnp.float32)
    return total

def reference(block_input, norm1_gain, w_in, w_ba, conv_weight, decay_log, gnorm_gain, w_out, norm2_gain, w_up, w_down, grad_out):
    length = block_input.shape[0]
    model = block_input.shape[1]
    heads = w_in.shape[1]
    span = w_in.shape[2]
    channels = conv_weight.shape[0]
    units = w_up.shape[2]
    tokens_wide = block_input.astype(jnp.float32)
    normed, pull_first = jax.vjp(rms_apply, tokens_wide, norm1_gain)
    normed_b = normed.astype(jnp.bfloat16)
    w_in_flat = w_in.reshape(model, heads * span)
    w_ba_flat = w_ba.reshape(model, 2 * heads)
    projected = jnp.dot(normed_b.astype(jnp.float32), w_in_flat.astype(jnp.float32), preferred_element_type=jnp.float32).astype(jnp.bfloat16).reshape(length, heads, span)
    mixer_in = jnp.dot(normed_b.astype(jnp.float32), w_ba_flat.astype(jnp.float32), preferred_element_type=jnp.float32).reshape(length, 2, heads)
    edged = jnp.concatenate([jnp.zeros((CONV - 1, heads, channels), jnp.float32), projected[:, :, :channels].astype(jnp.float32)], 0)
    feats, pull_feat = jax.vjp(features, edged, mixer_in, conv_weight, decay_log)
    terms, pull_terms = jax.vjp(stretch_heads, *feats)
    start = jnp.zeros((heads, DK, DV), jnp.float32)
    (layer_outputs, final), pull_scan = jax.vjp(scan_heads, terms, start)
    gate_wide = projected[:, :, channels:].astype(jnp.float32)
    gated_out, pull_gate = jax.vjp(gated, layer_outputs, gate_wide, gnorm_gain)
    gated_b = gated_out.astype(jnp.bfloat16).reshape(length, heads * DV)
    w_out_flat = w_out.transpose(1, 0, 2).reshape(heads * DV, model)
    mixed = group_total(gated_b, w_out_flat)
    hidden = tokens_wide + mixed
    hidden_n, pull_second = jax.vjp(rms_apply, hidden, norm2_gain)
    hidden_b = hidden_n.astype(jnp.bfloat16)
    w_up_flat = w_up.reshape(model, 2 * units)
    gate_up = jnp.dot(hidden_b.astype(jnp.float32), w_up_flat.astype(jnp.float32), preferred_element_type=jnp.float32).reshape(length, 2, units)
    swish, pull_swish = jax.vjp(swiglu, gate_up)
    swish_b = swish.astype(jnp.bfloat16)
    ffn_total = group_total(swish_b, w_down.T)
    result = hidden + ffn_total
    act_grad = jnp.dot(grad_out.astype(jnp.float32), w_down.astype(jnp.float32), preferred_element_type=jnp.float32)
    w_down_grad = jnp.dot(grad_out.T.astype(jnp.float32), swish_b.astype(jnp.float32), preferred_element_type=jnp.float32)
    gate_up_grad, = pull_swish(act_grad)
    gate_up_b = gate_up_grad.astype(jnp.bfloat16).reshape(length, 2 * units)
    w_up_grad = jnp.dot(hidden_b.T.astype(jnp.float32), gate_up_b.astype(jnp.float32), preferred_element_type=jnp.float32).reshape(model, 2, units)
    second_total = jnp.dot(gate_up_b.astype(jnp.float32), w_up_flat.T.astype(jnp.float32), preferred_element_type=jnp.float32)
    hidden_grad, norm2_gain_grad = pull_second(second_total)
    stream = grad_out.astype(jnp.float32) + hidden_grad
    stream_b = stream.astype(jnp.bfloat16)
    w_out_grad = jnp.dot(gated_b.T.astype(jnp.float32), stream_b.astype(jnp.float32), preferred_element_type=jnp.float32).reshape(heads, DV, model).transpose(1, 0, 2)
    gated_grad = jnp.dot(stream_b.astype(jnp.float32), w_out_flat.T.astype(jnp.float32), preferred_element_type=jnp.float32).reshape(length, heads, DV)
    output_gradient, gate_grad, gnorm_gain_grad = pull_gate(gated_grad)
    term_grad, start_grad = pull_scan((output_gradient, jnp.zeros_like(final)))
    feat_grad = pull_terms(term_grad)
    edged_grad, mixer_grad, conv_grad, log_decay_gradient = pull_feat(tuple(feat_grad))
    proj_grad = jnp.concatenate([edged_grad[CONV - 1:], gate_grad], 2).astype(jnp.bfloat16).reshape(length, heads * span)
    mixer_b = mixer_grad.astype(jnp.bfloat16).reshape(length, 2 * heads)
    input_weight_gradient = jnp.dot(normed_b.T.astype(jnp.float32), proj_grad.astype(jnp.float32), preferred_element_type=jnp.float32).reshape(model, heads, span)
    w_ba_grad = jnp.dot(normed_b.T.astype(jnp.float32), mixer_b.astype(jnp.float32), preferred_element_type=jnp.float32).reshape(model, 2, heads)
    first_total = jnp.dot(proj_grad.astype(jnp.float32), w_in_flat.T.astype(jnp.float32), preferred_element_type=jnp.float32) + jnp.dot(mixer_b.astype(jnp.float32), w_ba_flat.T.astype(jnp.float32), preferred_element_type=jnp.float32)
    input_part, norm1_gain_grad = pull_first(first_total)
    input_grad = stream + input_part
    return (result, input_grad, norm1_gain_grad, input_weight_gradient, w_ba_grad, conv_grad, log_decay_gradient, gnorm_gain_grad, w_out_grad, norm2_gain_grad, w_up_grad, w_down_grad)
```

```python
import functools

import jax
import jax.numpy as jnp
from jax import lax
from jax.experimental import pallas as pl
from jax.experimental.pallas import tpu as pltpu
from jax.sharding import PartitionSpec as P

DK = 128
DV = 256
CONV = 4
STRETCH = 64


EPSILON = 1e-06
NEGATIVE = -1e30
FINE = lax.Precision.HIGH


def shifted(block, axis, distance):
    devices = range(lax.axis_size(axis))
    route = [(i - distance, i) for i in devices if i - distance in devices]
    return lax.ppermute(block, axis, route)


MESH = pl.DeviceIdType.MESH
PIECES = 4


def flipped(index, bit):
    mine = (index // bit) % 2
    return index + bit - 2 * bit * mine, mine


def powers(count):
    return [2**i for i in range(count.bit_length() - 1)]


def remote(src, dst, send_sem, recv_sem, axis, device):
    return pltpu.make_async_remote_copy(
        src_ref=src,
        dst_ref=dst,
        send_sem=send_sem,
        recv_sem=recv_sem,
        device_id={axis: device},
        device_id_type=MESH,
    )


def greet(partners):
    barrier = pltpu.get_barrier_semaphore()
    for axis, partner in partners:
        pl.semaphore_signal(barrier, inc=1, device_id={axis: partner}, device_id_type=MESH)
    pl.semaphore_wait(barrier, len(partners))


def together(tasks):
    live = list(tasks)
    while live:
        for task in list(live):
            try:
                next(task)
            except StopIteration:
                live.remove(task)


def bit_partners(axis, count):
    me = lax.axis_index(axis)
    return [(axis, flipped(me, bit)[0]) for bit in powers(count)]


def head_sum_scratch(count, whole):
    piece = whole[2:]
    steps = len(powers(count)) - 1
    dma = pltpu.SemaphoreType.DMA
    return [
        pltpu.VMEM((PIECES,) + piece, jnp.bfloat16),
        pltpu.VMEM((steps, PIECES) + piece, jnp.bfloat16),
        pltpu.VMEM((steps, PIECES) + piece, jnp.bfloat16),
        dma((PIECES,)),
        dma((PIECES,)),
        dma((steps, PIECES)),
        dma((steps, PIECES)),
        dma((PIECES,)),
        dma((PIECES,)),
    ]


def head_sum_task(count, x_ref, out_ref, scratch):
    first, held, sums, near_s, near_r, far_s, far_r, back_s, back_r = scratch
    me = lax.axis_index("head")
    bits = powers(count)
    partner, side = flipped(me, 1)
    peers = [flipped(me, bit)[0] for bit in bits[1:]]

    def send(src, dst, send_sem, recv_sem, device):
        copy = remote(src, dst, send_sem, recv_sem, "head", device)
        copy.start()
        return copy

    def add(left, right):
        return (left.astype(jnp.float32) + right.astype(jnp.float32)).astype(jnp.bfloat16)

    near = [
        send(x_ref.at[1 - side, k], first.at[k], near_s.at[k], near_r.at[k], partner)
        for k in range(PIECES)
    ]
    yield
    steps = len(peers)
    copies = []
    for k in range(PIECES):
        near[k].wait()
        sums[0, k] = add(x_ref[side, k], first[k])
        copies.append(
            send(sums.at[0, k], held.at[0, k], far_s.at[0, k], far_r.at[0, k], peers[0])
        )
    yield
    for step in range(steps):
        later = []
        for k in range(PIECES):
            copies[k].wait()
            total = add(sums[step, k], held[step, k])
            if step < steps - 1:
                sums[step + 1, k] = total
                later.append(
                    send(
                        sums.at[step + 1, k],
                        held.at[step + 1, k],
                        far_s.at[step + 1, k],
                        far_r.at[step + 1, k],
                        peers[step + 1],
                    )
                )
            else:
                out_ref[side, k] = total
                later.append(
                    send(
                        out_ref.at[side, k],
                        out_ref.at[side, k],
                        back_s.at[k],
                        back_r.at[k],
                        partner,
                    )
                )
            yield
        copies = later
    for copy in copies:
        copy.wait()


def head_whole(shape):
    rows, width = shape
    return (2, PIECES, rows // (2 * PIECES), width)


def head_sum_kernel(count, x_ref, out_ref, *scratch):
    greet(bit_partners("head", count))
    together([head_sum_task(count, x_ref, out_ref, scratch)])


VMEM = pl.BlockSpec(memory_space=pltpu.VMEM)


def head_sum(part):
    count = lax.axis_size("head")
    whole = head_whole(part.shape)
    total = pl.pallas_call(
        functools.partial(head_sum_kernel, count),
        out_shape=jax.ShapeDtypeStruct(whole, jnp.bfloat16),
        in_specs=[VMEM],
        out_specs=VMEM,
        scratch_shapes=head_sum_scratch(count, whole),
        compiler_params=pltpu.CompilerParams(
            collective_id=0, has_side_effects=True, vmem_limit_bytes=16 << 20
        ),
        name="head_sum",
    )(part.astype(jnp.bfloat16).reshape(whole))
    return total.reshape(part.shape)


def gather_scratch(count):
    dma = pltpu.SemaphoreType.DMA
    line = max(count // 2, 1)
    return [dma((line,)), dma((line,)), dma((line,)), dma((line,)), dma((2 * line,)), dma((2 * line,))]


def line_partners(count):
    me = lax.axis_index("seq")
    up, down = lax.rem(me + 2, count), lax.rem(me + count - 2, count)
    return [("seq", flipped(me, 1)[0]), ("seq", up), ("seq", down)]


def gather_task(count, out_ref, scratch):
    up_s, up_r, dn_s, dn_r, x_s, x_r = scratch
    me = lax.axis_index("seq")
    line = count // 2
    place, half = me // 2, lax.rem(me, 2)
    other, _ = flipped(me, 1)

    def hop(position, send_sem, recv_sem, device):
        block = out_ref.at[2 * position + half]
        return remote(block, block, send_sem, recv_sem, "seq", device)

    def up(step):
        return hop(place - (step - 1), up_s.at[step], up_r.at[step], me + 2)

    def down(step):
        return hop(place + (step - 1), dn_s.at[step], dn_r.at[step], me - 2)

    def came_up(step):
        return hop(place - step, up_s.at[step], up_r.at[step], me - 2)

    def came_down(step):
        return hop(place + step, dn_s.at[step], dn_r.at[step], me + 2)

    def across(number, position):
        return hop(position, x_s.at[number], x_r.at[number], other)

    def from_across(number, position):
        block = out_ref.at[2 * position + 1 - half]
        return remote(block, block, x_s.at[number], x_r.at[number], "seq", other)

    def sends_up(step):
        return (place + 1 < line) & (place - (step - 1) >= 0)

    def sends_down(step):
        return (place - 1 >= 0) & (place + (step - 1) < line)

    for step in range(1, line):
        if step > 1:
            @pl.when(place - (step - 1) >= 0)
            def _():
                came_up(step - 1).wait_recv()

        @pl.when(sends_up(step))
        def _():
            up(step).start()

        if step > 1:

            @pl.when(place + (step - 1) < line)
            def _():
                came_down(step - 1).wait_recv()

        @pl.when(sends_down(step))
        def _():
            down(step).start()

        if step == 1:
            across(0, place).start()
        else:

            @pl.when(place - (step - 1) >= 0)
            def _():
                across(2 * step - 3, place - (step - 1)).start()

            @pl.when(place + (step - 1) < line)
            def _():
                across(2 * step - 2, place + (step - 1)).start()

        yield
    last = line - 1

    @pl.when(place - last >= 0)
    def _():
        came_up(last).wait_recv()
        across(2 * last - 1, place - last).start()

    @pl.when(place + last < line)
    def _():
        came_down(last).wait_recv()
        across(2 * last, place + last).start()

    yield
    for step in range(1, line):

        @pl.when(sends_up(step))
        def _():
            up(step).wait_send()

        @pl.when(sends_down(step))
        def _():
            down(step).wait_send()

    across(0, place).wait_send()
    from_across(0, place).wait_recv()
    for step in range(1, line):

        @pl.when(place - step >= 0)
        def _():
            across(2 * step - 1, place - step).wait_send()
            from_across(2 * step - 1, place - step).wait_recv()

        @pl.when(place + step < line)
        def _():
            across(2 * step, place + step).wait_send()
            from_across(2 * step, place + step).wait_recv()


def carry_kernel(count, heads, x_ref, state_ref, all_ref, *scratch):
    me = lax.axis_index("seq")
    greet(line_partners(count))
    all_ref[me] = x_ref[...]
    together([gather_task(count, all_ref, scratch)])
    for h in range(heads):
        state = all_ref[0, h, :, DK:].astype(jnp.float32)
        state = jnp.where(me > 0, state, jnp.zeros_like(state))
        for source in range(1, count - 1):
            moved = jnp.dot(
                all_ref[source, h, :, :DK],
                state.astype(jnp.bfloat16),
                preferred_element_type=jnp.float32,
            ) + all_ref[source, h, :, DK:].astype(jnp.float32)
            state = jnp.where(source < me, moved, state)
        state_ref[h] = state


def carried_forward(part):
    count = lax.axis_size("seq")
    heads = part.shape[0]
    return pl.pallas_call(
        functools.partial(carry_kernel, count, heads),
        out_shape=[
            jax.ShapeDtypeStruct((heads, DK, DV), jnp.float32),
            jax.ShapeDtypeStruct((count,) + part.shape, jnp.bfloat16),
        ],
        in_specs=[VMEM],
        out_specs=[VMEM, VMEM],
        scratch_shapes=gather_scratch(count),
        compiler_params=pltpu.CompilerParams(
            collective_id=1, has_side_effects=True, vmem_limit_bytes=24 << 20
        ),
        name="carry_forward",
    )(part.astype(jnp.bfloat16))


def back_kernel(count, ranks, heads, x_ref, maps_ref, part_ref, state_ref, total_ref, all_ref, *scratch):
    me = lax.axis_index("seq")
    n = len(gather_scratch(count))
    greet(line_partners(count) + bit_partners("head", ranks))
    all_ref[me] = x_ref[...]
    together(
        [
            gather_task(count, all_ref, scratch[:n]),
            head_sum_task(ranks, part_ref, total_ref, scratch[n:]),
        ]
    )
    for h in range(heads):
        state = all_ref[count - 1, h].astype(jnp.float32)
        state = jnp.where(me < count - 1, state, jnp.zeros_like(state))
        for source in range(count - 2, 0, -1):
            moved = lax.dot_general(
                maps_ref[source, h, :, :DK],
                state.astype(jnp.bfloat16),
                (((0,), (0,)), ((), ())),
                preferred_element_type=jnp.float32,
            ) + all_ref[source, h].astype(jnp.float32)
            state = jnp.where(source > me, moved, state)
        state_ref[h] = state


def carried_back(feed, maps, part):
    count = lax.axis_size("seq")
    ranks = lax.axis_size("head")
    heads = feed.shape[0]
    whole = head_whole(part.shape)
    state, total = pl.pallas_call(
        functools.partial(back_kernel, count, ranks, heads),
        out_shape=[
            jax.ShapeDtypeStruct((heads, DK, DV), jnp.float32),
            jax.ShapeDtypeStruct(whole, jnp.bfloat16),
        ],
        in_specs=[VMEM] * 3,
        out_specs=[VMEM] * 2,
        scratch_shapes=[pltpu.VMEM((count,) + feed.shape, jnp.bfloat16)]
        + gather_scratch(count)
        + head_sum_scratch(ranks, whole),
        compiler_params=pltpu.CompilerParams(
            collective_id=2, has_side_effects=True, vmem_limit_bytes=32 << 20
        ),
        name="carry_back",
    )(feed.astype(jnp.bfloat16), maps, part.astype(jnp.bfloat16).reshape(whole))
    return state, total.reshape(part.shape)


def share_scratch(count, shapes):
    steps = len(powers(count))
    halves = [(s[1], s[2] // 2) for s in shapes]
    works = 2 * len(shapes)
    dma = pltpu.SemaphoreType.DMA
    return (
        [pltpu.VMEM((2, steps, count // 2) + half, jnp.bfloat16) for half in halves]
        + [pltpu.VMEM((2, max(steps - 1, 1), count // 4) + half, jnp.bfloat16) for half in halves]
        + [dma((works, steps, count // 2)), dma((works, steps, count // 2))]
    )


def share_task(count, x_refs, out_refs, scratch):
    arrays = len(x_refs)
    recv_refs, send_refs = scratch[:arrays], scratch[arrays : 2 * arrays]
    send_sem, recv_sem = scratch[2 * arrays :]
    me = lax.axis_index("seq")
    bits = powers(count)
    partners = {bit: flipped(me, bit)[0] for bit in bits}

    def block(relative):
        index = me
        for bit in bits:
            if relative & bit:
                index = flipped(index, bit)[0]
        return index

    orders = [bits, bits[1:] + bits[:1]]
    works = []
    for a in range(arrays):
        half = x_refs[a].shape[2] // 2
        for way in range(2):
            works.append((a, way, pl.ds(way * half, half)))

    def kept(order, step):
        used = sum(order[:step])
        return [r for r in range(count) if r & used == 0]

    def slot(way, step, relative):
        return kept(orders[way], step + 1).index(relative)

    def partial_sum(work, relative, step):
        a, way, cols = work
        total = x_refs[a][block(relative), :, cols].astype(jnp.float32)
        for earlier in range(step):
            total = total + recv_refs[a][way, earlier, slot(way, earlier, relative)].astype(
                jnp.float32
            )
        return total

    pending = {}
    for step in range(len(bits) + 1):
        for number, work in enumerate(works):
            a, way, cols = work
            order = orders[way]
            for copy in pending.pop(number, []):
                copy.wait()
            if step == len(bits):
                out_refs[a][:, cols] = partial_sum(work, 0, step)
                continue
            bit = order[step]
            started = []
            for relative in kept(order, step):
                if not relative & bit:
                    continue
                place = slot(way, step, relative - bit)
                if step == 0:
                    source = x_refs[a].at[block(relative), :, cols]
                else:
                    send_refs[a][way, step - 1, place] = partial_sum(
                        work, relative, step
                    ).astype(jnp.bfloat16)
                    source = send_refs[a].at[way, step - 1, place]
                copy = remote(
                    source,
                    recv_refs[a].at[way, step, place],
                    send_sem.at[number, step, place],
                    recv_sem.at[number, step, place],
                    "seq",
                    partners[bit],
                )
                copy.start()
                started.append(copy)
            pending[number] = started
            if step:
                yield
        yield


def small_scratch(count, ranks, rows, both):
    dma = pltpu.SemaphoreType.DMA
    near, far = len(powers(ranks)), len(powers(count))
    return [
        pltpu.VMEM((near, both, 128), jnp.float32),
        pltpu.VMEM((far, rows, 128), jnp.float32),
        pltpu.VMEM((near, both, 128), jnp.float32),
        pltpu.VMEM((far, rows, 128), jnp.float32),
        dma((near,)),
        dma((near,)),
        dma((far,)),
        dma((far,)),
    ]


def small_task(count, ranks, both, x_ref, out_ref, scratch):
    got_h, got_s, sent_h, sent_s, hs, hr, ss, sr = scratch
    total = x_ref[:both]
    for i, (axis, partner) in enumerate(bit_partners("head", ranks)):
        sent_h[i] = total
        copy = remote(sent_h.at[i], got_h.at[i], hs.at[i], hr.at[i], axis, partner)
        copy.start()
        yield
        copy.wait()
        total = sent_h[i] + got_h[i]
    for i, (axis, partner) in enumerate(bit_partners("seq", count)):
        if i == 0:
            sent_s[0, :both] = total
            sent_s[0, both:] = x_ref[both:]
        else:
            sent_s[i] = sent_s[i - 1] + got_s[i - 1]
        copy = remote(sent_s.at[i], got_s.at[i], ss.at[i], sr.at[i], axis, partner)
        copy.start()
        yield
        copy.wait()
    last = len(powers(count)) - 1
    out_ref[...] = sent_s[last] + got_s[last]


def final_kernel(count, ranks, both, arrays, *refs):
    part_ref, small_ref, *x_refs = refs[: arrays + 2]
    total_ref, sum_ref, *out_refs = refs[arrays + 2 : 2 * arrays + 4]
    scratch = refs[2 * arrays + 4 :]
    n = len(head_sum_scratch(ranks, (1, 1, 8, 128)))
    m = 8
    greet(bit_partners("seq", count) + bit_partners("head", ranks))
    together(
        [
            share_task(count, x_refs, out_refs, scratch[n + m :]),
            head_sum_task(ranks, part_ref, total_ref, scratch[:n]),
            small_task(count, ranks, both, small_ref, sum_ref, scratch[n : n + m]),
        ]
    )


def final_sums(part, wide, narrow, grads):
    count = lax.axis_size("seq")
    ranks = lax.axis_size("head")
    whole = head_whole(part.shape)

    def padded(flat):
        size = -(-flat.shape[0] // 1024) * 1024
        return jnp.pad(flat, (0, size - flat.shape[0])).reshape(size // 128, 128)

    wide_flat = padded(jnp.concatenate([a.reshape(-1) for a in wide]))
    narrow_flat = padded(jnp.concatenate([a.reshape(-1) for a in narrow]))
    both = wide_flat.shape[0]
    small = jnp.concatenate([wide_flat, narrow_flat])
    blocks = [
        g.astype(jnp.bfloat16).reshape(count, g.shape[0] // count, g.shape[1]) for g in grads
    ]
    total, summed, *shares = pl.pallas_call(
        functools.partial(final_kernel, count, ranks, both, len(grads)),
        out_shape=[
            jax.ShapeDtypeStruct(whole, jnp.bfloat16),
            jax.ShapeDtypeStruct(small.shape, jnp.float32),
        ]
        + [jax.ShapeDtypeStruct(b.shape[1:], jnp.float32) for b in blocks],
        in_specs=[VMEM] * (len(grads) + 2),
        out_specs=[VMEM] * (len(grads) + 2),
        scratch_shapes=head_sum_scratch(ranks, whole)
        + small_scratch(count, ranks, small.shape[0], both)
        + share_scratch(count, [b.shape for b in blocks]),
        compiler_params=pltpu.CompilerParams(
            collective_id=3, has_side_effects=True, vmem_limit_bytes=56 << 20
        ),
        name="final_sums",
    )(part.astype(jnp.bfloat16).reshape(whole), small, *blocks)
    outs = []
    for flat, group in ((summed[:both].reshape(-1), wide), (summed[both:].reshape(-1), narrow)):
        at = 0
        for a in group:
            outs.append(flat[at : at + a.size].reshape(a.shape))
            at += a.size
    return total.reshape(part.shape), outs, shares


def seq_share(grad):
    return lax.psum_scatter(
        grad.astype(jnp.bfloat16), "seq", scatter_dimension=0, tiled=True
    ).astype(jnp.float32)


def rms_apply(values, gain):
    return values * lax.rsqrt(jnp.mean(values * values, axis=-1, keepdims=True) + EPSILON) * gain


def features(edged, mixer_in, conv_weight, decay_log):
    length = edged.shape[1] - (CONV - 1)
    taps = jnp.transpose(conv_weight, (2, 1, 0))[:, :, None, :]
    mixed = edged[:, 0:length] * taps[0]
    for index in range(1, CONV):
        mixed = mixed + edged[:, index : index + length] * taps[index]
    active = jax.nn.silu(mixed)
    query = active[..., :DK]
    key = active[..., DK : 2 * DK]
    value = active[..., 2 * DK :]
    query = (
        query * lax.rsqrt(jnp.sum(query * query, axis=-1, keepdims=True) + EPSILON) * DK ** (-0.5)
    )
    key = key * lax.rsqrt(jnp.sum(key * key, axis=-1, keepdims=True) + EPSILON)
    beta = jax.nn.sigmoid(mixer_in[0])
    logdecay = -jnp.exp(decay_log)[:, None] * jax.nn.softplus(mixer_in[1])
    return (query, key, value, beta, logdecay)


def fine(left, right):
    return jnp.matmul(left, right, precision=FINE)


def flip(array):
    return jnp.swapaxes(array, -1, -2)


@jax.custom_vjp
def unit_inverse(lower):
    width = lower.shape[-1]
    row_pos = lax.broadcasted_iota(jnp.int32, (width, width), 0)
    column = lax.broadcasted_iota(jnp.int32, (width, width), 1)

    def pairs(size):
        return (row_pos // size == column // size + 1) & ((row_pos // size) % 2 == 1)

    inverse = jnp.eye(width, dtype=lower.dtype) - jnp.where(pairs(1), lower, 0.0)
    size = 2
    while size < width:
        inverse = inverse - fine(fine(inverse, jnp.where(pairs(size), lower, 0.0)), inverse)
        size *= 2
    return inverse


def unit_inverse_fwd(lower):
    inverse = unit_inverse(lower)
    return inverse, inverse


def unit_inverse_bwd(inverse, grad):
    turned = flip(inverse)
    return (-fine(fine(turned, grad), turned),)


unit_inverse.defvjp(unit_inverse_fwd, unit_inverse_bwd)


def stretch_terms(query, key, value, beta, logdecay):
    width = query.shape[-2]
    row_pos = lax.broadcasted_iota(jnp.int32, (width, width), 0)
    column = lax.broadcasted_iota(jnp.int32, (width, width), 1)
    upto = (row_pos >= column).astype(jnp.float32)
    cumul = jnp.sum(upto * logdecay[..., None, :], axis=-1)
    last = jnp.sum(logdecay, axis=-1)[..., None, None]
    spread = cumul[..., :, None] - cumul[..., None, :]
    decay = jnp.exp(jnp.where(row_pos >= column, spread, NEGATIVE))
    strict = jnp.where(row_pos > column, decay, 0.0)
    lower = beta[..., None] * strict * fine(key, flip(key))
    inverse = unit_inverse(lower)
    growth = jnp.exp(cumul)[..., None]
    sides = jnp.concatenate(
        [(beta[..., None] * growth) * key, beta[..., None] * value], axis=-1
    )
    solved = jnp.matmul(inverse, sides)
    scores = decay * jnp.matmul(query, flip(key))
    mapped = jnp.matmul(scores, solved)
    query_map = growth * query - mapped[..., :DK]
    out_fixed = mapped[..., DK:]
    key_end = jnp.exp(last - cumul[..., None]) * key
    ended = jnp.matmul(flip(key_end), solved)
    transit = jnp.exp(last) * jnp.eye(DK, dtype=query.dtype) - ended[..., :DK]
    feed = ended[..., DK:]
    return (query_map, out_fixed, transit, feed)


def gated(layer_outputs, gate, gain):
    return rms_apply(layer_outputs, gain) * jax.nn.silu(gate)


def swiglu(gate_up):
    return jax.nn.silu(gate_up[:, 0]) * gate_up[:, 1]


def chain(maps, feeds):
    start = jnp.concatenate(
        [
            jnp.broadcast_to(jnp.eye(DK, dtype=jnp.float32), maps[0].shape),
            jnp.zeros_like(feeds[0]),
        ],
        axis=-1,
    )
    pad = ((0, 0), (0, 0), (DK, 0))
    states = [start]
    for index, (part, feed) in enumerate(zip(maps, feeds)):
        if index == 0:
            states.append(jnp.concatenate([part, feed], axis=-1))
        else:
            states.append(fine(part, states[-1]) + jnp.pad(feed, pad))
    return states


def shards(
    block_input,
    norm1_gain,
    w_in,
    w_ba,
    conv_weight,
    decay_log,
    gnorm_gain,
    w_out,
    norm2_gain,
    w_up,
    w_down,
    grad_out,
):
    length = block_input.shape[0]
    heads = w_in.shape[1]
    channels = conv_weight.shape[0]
    blocks = length // STRETCH
    f32 = jnp.float32
    bf16 = jnp.bfloat16

    def split(array):
        return array.reshape((heads, blocks, STRETCH) + array.shape[2:])

    tokens_wide = block_input.astype(f32)
    normed, pull_first = jax.vjp(rms_apply, tokens_wide, norm1_gain)
    normed_b = normed.astype(bf16)
    projected = jnp.einsum(
        "td,dhc->htc", normed_b, w_in, preferred_element_type=f32
    ).astype(bf16)
    mixer_in = jnp.einsum("td,dch->cht", normed_b, w_ba, preferred_element_type=f32)
    edge = shifted(projected[:, length - (CONV - 1) :, :channels], "seq", 1)
    edged = jnp.concatenate([edge, projected[:, :, :channels]], 1).astype(f32)
    feats, pull_feat = jax.vjp(features, edged, mixer_in, conv_weight, decay_log)
    terms, pull_terms = jax.vjp(stretch_terms, *[split(a) for a in feats])
    query_map, out_fixed, transit, feed = terms
    starts = chain(
        [transit[:, i] for i in range(blocks)], [feed[:, i] for i in range(blocks)]
    )
    carried, maps = carried_forward(starts[-1])
    before = jnp.stack(starts[:-1], axis=1)
    states = jnp.matmul(before[..., :DK], carried[:, None]) + before[..., DK:]
    layer_outputs = (jnp.matmul(query_map, states) + out_fixed).reshape(heads, length, DV)
    gate_wide = projected[:, :, channels:].astype(f32)
    gated_out, pull_gate = jax.vjp(gated, layer_outputs, gate_wide, gnorm_gain)
    gated_b = gated_out.astype(bf16)
    mixer_part = jnp.einsum("htc,chd->td", gated_b, w_out, preferred_element_type=f32)
    mixed = head_sum(mixer_part).astype(f32)
    hidden = tokens_wide + mixed
    hidden_n, pull_second = jax.vjp(rms_apply, hidden, norm2_gain)
    hidden_b = hidden_n.astype(bf16)
    gate_up = jnp.einsum("td,dcf->tcf", hidden_b, w_up, preferred_element_type=f32)
    swish, pull_swish = jax.vjp(swiglu, gate_up)
    swish_b = swish.astype(bf16)
    act_grad = jnp.dot(grad_out, w_down, preferred_element_type=f32)
    (gate_up_grad,) = pull_swish(act_grad)
    gate_up_b = gate_up_grad.astype(bf16)
    second_part = jnp.einsum("tcf,dcf->td", gate_up_b, w_up, preferred_element_type=f32)
    second_total = head_sum(second_part).astype(f32)
    down_grad = lax.dot_general(
        grad_out, swish_b, (((0,), (0,)), ((), ())), preferred_element_type=f32
    )
    up_grad = jnp.einsum("td,tcf->dcf", hidden_b, gate_up_b, preferred_element_type=f32)
    hidden_grad, _ = pull_second(second_total)
    gain_second = pull_second(second_part)[1]
    stream = grad_out.astype(f32) + hidden_grad
    stream_b = stream.astype(bf16)
    gated_grad = jnp.einsum("td,chd->htc", stream_b, w_out, preferred_element_type=f32)
    output_gradient, gate_grad, gain_gated = pull_gate(gated_grad)
    out_weight_grad = jnp.concatenate(
        [
            lax.dot_general(
                gated_b[h], stream_b, (((0,), (0,)), ((), ())), preferred_element_type=f32
            ).astype(bf16)
            for h in range(heads)
        ],
        1,
    )
    out_split = split(output_gradient)
    back_feed = jnp.matmul(flip(query_map), out_split)
    turned = flip(transit)
    backs = chain(
        [turned[:, i] for i in reversed(range(blocks))],
        [back_feed[:, i] for i in reversed(range(blocks))],
    )
    ffn_part = lax.dot_general(
        swish_b, w_down, (((1,), (1,)), ((), ())), preferred_element_type=f32
    )
    later_grad, ffn_total = carried_back(backs[-1][..., DK:], maps, ffn_part)
    result = hidden + ffn_total.astype(f32)
    later_grad, up_grad, down_grad = lax.optimization_barrier(
        (later_grad, up_grad.astype(bf16), down_grad.astype(bf16))
    )
    up_share = seq_share(up_grad)
    down_share = seq_share(down_grad)
    after = jnp.stack(backs[:-1][::-1], axis=1)
    later = jnp.matmul(after[..., :DK], later_grad[:, None]) + after[..., DK:]
    term_grad = (
        jnp.matmul(out_split, flip(states)),
        out_split,
        jnp.matmul(later, flip(states)),
        later,
    )
    feat_grad = [
        a.reshape((heads, length) + a.shape[3:]) for a in pull_terms(term_grad)
    ]
    edged_grad, mixer_grad, conv_grad, log_decay_gradient = pull_feat(tuple(feat_grad))
    back_edge = shifted(edged_grad[:, : CONV - 1], "seq", -1)
    channel_grad = edged_grad[:, CONV - 1 :]
    channel_grad = jnp.concatenate(
        [
            channel_grad[:, : length - (CONV - 1)],
            channel_grad[:, length - (CONV - 1) :] + back_edge,
        ],
        1,
    )
    proj_grad = jnp.concatenate([channel_grad, gate_grad], 2).astype(bf16)
    mixer_b = mixer_grad.astype(bf16)
    first_part = jnp.einsum("htc,dhc->td", proj_grad, w_in, preferred_element_type=f32)
    first_part = first_part + jnp.einsum(
        "cht,dch->td", mixer_b, w_ba, preferred_element_type=f32
    )
    proj_flat = jnp.concatenate([proj_grad[h] for h in range(heads)], 1)
    in_weight_grad = lax.dot_general(
        normed_b, proj_flat, (((0,), (0,)), ((), ())), preferred_element_type=f32
    ).astype(bf16)
    gate_weight_grad = jnp.einsum("td,cht->dch", normed_b, mixer_b, preferred_element_type=f32)
    gain_first = pull_first(first_part)[1]
    first_total, small, (in_share, out_share) = final_sums(
        first_part,
        [gain_first, gain_second, gain_gated],
        [log_decay_gradient, conv_grad, gate_weight_grad],
        [in_weight_grad, out_weight_grad],
    )
    gain_one, gain_two, gain_norm, decay_total, conv_total, gate_total = small
    input_part, _ = pull_first(first_total.astype(f32))
    input_grad = stream + input_part
    in_share = in_share.reshape((in_share.shape[0],) + w_in.shape[1:])
    out_share = out_share.reshape((out_share.shape[0],) + w_out.shape[1:])
    count = lax.axis_size("seq")
    place = lax.axis_index("seq")

    def mine(whole):
        share = whole.shape[0] // count
        return lax.dynamic_slice_in_dim(whole, place * share, share, 0)

    return (
        result,
        input_grad,
        gain_one,
        in_share,
        mine(gate_total),
        mine(conv_total),
        decay_total,
        gain_norm,
        out_share,
        gain_two,
        up_share,
        down_share,
    )


def solution(mesh):
    return jax.shard_map(
        shards,
        mesh=mesh,
        in_specs=(
            P("seq", None),
            P(),
            P(None, "head", None),
            P(None, None, "head"),
            P(None, "head", None),
            P("head"),
            P(),
            P(None, "head", None),
            P(),
            P(None, None, "head"),
            P(None, "head"),
            P("seq", None),
        ),
        out_specs=(
            P("seq", None),
            P("seq", None),
            P(),
            P("seq", "head", None),
            P("seq", None, "head"),
            P("seq", "head", None),
            P("head"),
            P(),
            P("seq", "head", None),
            P(),
            P("seq", None, "head"),
            P("seq", "head"),
        ),
        check_vma=False,
    )
```

```python
import functools

import jax
import jax.numpy as jnp
from jax import lax
from jax.experimental import pallas as pl
from jax.experimental.pallas import tpu as pltpu
from jax.sharding import PartitionSpec as P

DK = 128
DV = 256
CONV = 4
STRETCH = 64


EPSILON = 1e-06
NEGATIVE = -1e30


def shifted(block, axis, distance):
    devices = range(lax.axis_size(axis))
    route = [(i - distance, i) for i in devices if i - distance in devices]
    return lax.ppermute(block, axis, route)


MESH = pl.DeviceIdType.MESH
PIECES = 4


def flipped(index, bit):
    mine = (index // bit) % 2
    return index + bit - 2 * bit * mine, mine


def powers(count):
    return [2**i for i in range(count.bit_length() - 1)]


def remote(src, dst, send_sem, recv_sem, axis, device):
    return pltpu.make_async_remote_copy(
        src_ref=src,
        dst_ref=dst,
        send_sem=send_sem,
        recv_sem=recv_sem,
        device_id={axis: device},
        device_id_type=MESH,
    )


def greet(partners):
    barrier = pltpu.get_barrier_semaphore()
    for axis, partner in partners:
        pl.semaphore_signal(barrier, inc=1, device_id={axis: partner}, device_id_type=MESH)
    pl.semaphore_wait(barrier, len(partners))


def together(tasks):
    live = list(tasks)
    while live:
        for task in list(live):
            try:
                next(task)
            except StopIteration:
                live.remove(task)


def bit_partners(axis, count):
    me = lax.axis_index(axis)
    return [(axis, flipped(me, bit)[0]) for bit in powers(count)]


def head_sum_scratch(count, whole):
    piece = whole[2:]
    steps = len(powers(count)) - 1
    dma = pltpu.SemaphoreType.DMA
    return [
        pltpu.VMEM((PIECES,) + piece, jnp.bfloat16),
        pltpu.VMEM((steps, PIECES) + piece, jnp.bfloat16),
        pltpu.VMEM((steps, PIECES) + piece, jnp.bfloat16),
        dma((PIECES,)),
        dma((PIECES,)),
        dma((steps, PIECES)),
        dma((steps, PIECES)),
        dma((PIECES,)),
        dma((PIECES,)),
    ]


def head_sum_task(count, x_ref, out_ref, scratch):
    first, held, sums, near_s, near_r, far_s, far_r, back_s, back_r = scratch
    me = lax.axis_index("head")
    bits = powers(count)
    partner, side = flipped(me, 1)
    peers = [flipped(me, bit)[0] for bit in bits[1:]]

    def send(src, dst, send_sem, recv_sem, device):
        copy = remote(src, dst, send_sem, recv_sem, "head", device)
        copy.start()
        return copy

    def add(left, right):
        return (left.astype(jnp.float32) + right.astype(jnp.float32)).astype(jnp.bfloat16)

    near = [
        send(x_ref.at[1 - side, k], first.at[k], near_s.at[k], near_r.at[k], partner)
        for k in range(PIECES)
    ]
    yield
    steps = len(peers)
    copies = []
    for k in range(PIECES):
        near[k].wait()
        sums[0, k] = add(x_ref[side, k], first[k])
        copies.append(
            send(sums.at[0, k], held.at[0, k], far_s.at[0, k], far_r.at[0, k], peers[0])
        )
    yield
    for step in range(steps):
        later = []
        for k in range(PIECES):
            copies[k].wait()
            total = add(sums[step, k], held[step, k])
            if step < steps - 1:
                sums[step + 1, k] = total
                later.append(
                    send(
                        sums.at[step + 1, k],
                        held.at[step + 1, k],
                        far_s.at[step + 1, k],
                        far_r.at[step + 1, k],
                        peers[step + 1],
                    )
                )
            else:
                out_ref[side, k] = total
                later.append(
                    send(
                        out_ref.at[side, k],
                        out_ref.at[side, k],
                        back_s.at[k],
                        back_r.at[k],
                        partner,
                    )
                )
            yield
        copies = later
    for copy in copies:
        copy.wait()


def head_whole(shape):
    rows, width = shape
    return (2, PIECES, rows // (2 * PIECES), width)


def head_sum_kernel(count, x_ref, out_ref, *scratch):
    greet(bit_partners("head", count))
    together([head_sum_task(count, x_ref, out_ref, scratch)])


VMEM = pl.BlockSpec(memory_space=pltpu.VMEM)


def head_sum(part):
    count = lax.axis_size("head")
    whole = head_whole(part.shape)
    total = pl.pallas_call(
        functools.partial(head_sum_kernel, count),
        out_shape=jax.ShapeDtypeStruct(whole, jnp.bfloat16),
        in_specs=[VMEM],
        out_specs=VMEM,
        scratch_shapes=head_sum_scratch(count, whole),
        compiler_params=pltpu.CompilerParams(
            collective_id=0, has_side_effects=True, vmem_limit_bytes=16 << 20
        ),
        name="head_sum",
    )(part.astype(jnp.bfloat16).reshape(whole))
    return total.reshape(part.shape)


def gather_scratch(count):
    dma = pltpu.SemaphoreType.DMA
    line = max(count // 2, 1)
    return [dma((line,)), dma((line,)), dma((line,)), dma((line,)), dma((2 * line,)), dma((2 * line,))]


def line_partners(count):
    me = lax.axis_index("seq")
    up, down = lax.rem(me + 2, count), lax.rem(me + count - 2, count)
    return [("seq", flipped(me, 1)[0]), ("seq", up), ("seq", down)]


def gather_task(count, out_ref, scratch):
    up_s, up_r, dn_s, dn_r, x_s, x_r = scratch
    me = lax.axis_index("seq")
    line = count // 2
    place, half = me // 2, lax.rem(me, 2)
    other, _ = flipped(me, 1)

    def hop(position, send_sem, recv_sem, device):
        block = out_ref.at[2 * position + half]
        return remote(block, block, send_sem, recv_sem, "seq", device)

    def up(step):
        return hop(place - (step - 1), up_s.at[step], up_r.at[step], me + 2)

    def down(step):
        return hop(place + (step - 1), dn_s.at[step], dn_r.at[step], me - 2)

    def came_up(step):
        return hop(place - step, up_s.at[step], up_r.at[step], me - 2)

    def came_down(step):
        return hop(place + step, dn_s.at[step], dn_r.at[step], me + 2)

    def across(number, position):
        return hop(position, x_s.at[number], x_r.at[number], other)

    def from_across(number, position):
        block = out_ref.at[2 * position + 1 - half]
        return remote(block, block, x_s.at[number], x_r.at[number], "seq", other)

    def sends_up(step):
        return (place + 1 < line) & (place - (step - 1) >= 0)

    def sends_down(step):
        return (place - 1 >= 0) & (place + (step - 1) < line)

    for step in range(1, line):
        if step > 1:
            @pl.when(place - (step - 1) >= 0)
            def _():
                came_up(step - 1).wait_recv()

        @pl.when(sends_up(step))
        def _():
            up(step).start()

        if step > 1:

            @pl.when(place + (step - 1) < line)
            def _():
                came_down(step - 1).wait_recv()

        @pl.when(sends_down(step))
        def _():
            down(step).start()

        if step == 1:
            across(0, place).start()
        else:

            @pl.when(place - (step - 1) >= 0)
            def _():
                across(2 * step - 3, place - (step - 1)).start()

            @pl.when(place + (step - 1) < line)
            def _():
                across(2 * step - 2, place + (step - 1)).start()

        yield
    last = line - 1

    @pl.when(place - last >= 0)
    def _():
        came_up(last).wait_recv()
        across(2 * last - 1, place - last).start()

    @pl.when(place + last < line)
    def _():
        came_down(last).wait_recv()
        across(2 * last, place + last).start()

    yield
    for step in range(1, line):

        @pl.when(sends_up(step))
        def _():
            up(step).wait_send()

        @pl.when(sends_down(step))
        def _():
            down(step).wait_send()

    across(0, place).wait_send()
    from_across(0, place).wait_recv()
    for step in range(1, line):

        @pl.when(place - step >= 0)
        def _():
            across(2 * step - 1, place - step).wait_send()
            from_across(2 * step - 1, place - step).wait_recv()

        @pl.when(place + step < line)
        def _():
            across(2 * step, place + step).wait_send()
            from_across(2 * step, place + step).wait_recv()


def carry_kernel(count, heads, x_ref, state_ref, all_ref, *scratch):
    me = lax.axis_index("seq")
    greet(line_partners(count))
    all_ref[me] = x_ref[...]
    together([gather_task(count, all_ref, scratch)])
    for h in range(heads):
        state = all_ref[0, h, :, DK:].astype(jnp.float32)
        state = jnp.where(me > 0, state, jnp.zeros_like(state))
        for source in range(1, count - 1):
            moved = jnp.dot(
                all_ref[source, h, :, :DK],
                state.astype(jnp.bfloat16),
                preferred_element_type=jnp.float32,
            ) + all_ref[source, h, :, DK:].astype(jnp.float32)
            state = jnp.where(source < me, moved, state)
        state_ref[h] = state


def carried_forward(part):
    count = lax.axis_size("seq")
    heads = part.shape[0]
    return pl.pallas_call(
        functools.partial(carry_kernel, count, heads),
        out_shape=[
            jax.ShapeDtypeStruct((heads, DK, DV), jnp.float32),
            jax.ShapeDtypeStruct((count,) + part.shape, jnp.bfloat16),
        ],
        in_specs=[VMEM],
        out_specs=[VMEM, VMEM],
        scratch_shapes=gather_scratch(count),
        compiler_params=pltpu.CompilerParams(
            collective_id=1, has_side_effects=True, vmem_limit_bytes=24 << 20
        ),
        name="carry_forward",
    )(part.astype(jnp.bfloat16))


def back_kernel(count, ranks, heads, x_ref, maps_ref, part_ref, state_ref, total_ref, all_ref, *scratch):
    me = lax.axis_index("seq")
    n = len(gather_scratch(count))
    greet(line_partners(count) + bit_partners("head", ranks))
    all_ref[me] = x_ref[...]
    together(
        [
            gather_task(count, all_ref, scratch[:n]),
            head_sum_task(ranks, part_ref, total_ref, scratch[n:]),
        ]
    )
    for h in range(heads):
        state = all_ref[count - 1, h].astype(jnp.float32)
        state = jnp.where(me < count - 1, state, jnp.zeros_like(state))
        for source in range(count - 2, 0, -1):
            moved = lax.dot_general(
                maps_ref[source, h, :, :DK],
                state.astype(jnp.bfloat16),
                (((0,), (0,)), ((), ())),
                preferred_element_type=jnp.float32,
            ) + all_ref[source, h].astype(jnp.float32)
            state = jnp.where(source > me, moved, state)
        state_ref[h] = state


def carried_back(feed, maps, part):
    count = lax.axis_size("seq")
    ranks = lax.axis_size("head")
    heads = feed.shape[0]
    whole = head_whole(part.shape)
    state, total = pl.pallas_call(
        functools.partial(back_kernel, count, ranks, heads),
        out_shape=[
            jax.ShapeDtypeStruct((heads, DK, DV), jnp.float32),
            jax.ShapeDtypeStruct(whole, jnp.bfloat16),
        ],
        in_specs=[VMEM] * 3,
        out_specs=[VMEM] * 2,
        scratch_shapes=[pltpu.VMEM((count,) + feed.shape, jnp.bfloat16)]
        + gather_scratch(count)
        + head_sum_scratch(ranks, whole),
        compiler_params=pltpu.CompilerParams(
            collective_id=2, has_side_effects=True, vmem_limit_bytes=32 << 20
        ),
        name="carry_back",
    )(feed.astype(jnp.bfloat16), maps, part.astype(jnp.bfloat16).reshape(whole))
    return state, total.reshape(part.shape)


def share_scratch(count, shapes):
    steps = len(powers(count))
    halves = [(s[1], s[2] // 2) for s in shapes]
    works = 2 * len(shapes)
    dma = pltpu.SemaphoreType.DMA
    return (
        [pltpu.VMEM((2, steps, count // 2) + half, jnp.bfloat16) for half in halves]
        + [pltpu.VMEM((2, max(steps - 1, 1), count // 4) + half, jnp.bfloat16) for half in halves]
        + [dma((works, steps, count // 2)), dma((works, steps, count // 2))]
    )


def share_task(count, x_refs, out_refs, scratch):
    arrays = len(x_refs)
    recv_refs, send_refs = scratch[:arrays], scratch[arrays : 2 * arrays]
    send_sem, recv_sem = scratch[2 * arrays :]
    me = lax.axis_index("seq")
    bits = powers(count)
    partners = {bit: flipped(me, bit)[0] for bit in bits}

    def block(relative):
        index = me
        for bit in bits:
            if relative & bit:
                index = flipped(index, bit)[0]
        return index

    orders = [bits, bits[1:] + bits[:1]]
    works = []
    for a in range(arrays):
        half = x_refs[a].shape[2] // 2
        for way in range(2):
            works.append((a, way, pl.ds(way * half, half)))

    def kept(order, step):
        used = sum(order[:step])
        return [r for r in range(count) if r & used == 0]

    def slot(way, step, relative):
        return kept(orders[way], step + 1).index(relative)

    def partial_sum(work, relative, step):
        a, way, cols = work
        total = x_refs[a][block(relative), :, cols].astype(jnp.float32)
        for earlier in range(step):
            total = total + recv_refs[a][way, earlier, slot(way, earlier, relative)].astype(
                jnp.float32
            )
        return total

    pending = {}
    for step in range(len(bits) + 1):
        for number, work in enumerate(works):
            a, way, cols = work
            order = orders[way]
            for copy in pending.pop(number, []):
                copy.wait()
            if step == len(bits):
                out_refs[a][:, cols] = partial_sum(work, 0, step)
                continue
            bit = order[step]
            started = []
            for relative in kept(order, step):
                if not relative & bit:
                    continue
                place = slot(way, step, relative - bit)
                if step == 0:
                    source = x_refs[a].at[block(relative), :, cols]
                else:
                    send_refs[a][way, step - 1, place] = partial_sum(
                        work, relative, step
                    ).astype(jnp.bfloat16)
                    source = send_refs[a].at[way, step - 1, place]
                copy = remote(
                    source,
                    recv_refs[a].at[way, step, place],
                    send_sem.at[number, step, place],
                    recv_sem.at[number, step, place],
                    "seq",
                    partners[bit],
                )
                copy.start()
                started.append(copy)
            pending[number] = started
            if step:
                yield
        yield


def small_scratch(count, ranks, rows, both):
    dma = pltpu.SemaphoreType.DMA
    near, far = len(powers(ranks)), len(powers(count))
    return [
        pltpu.VMEM((near, both, 128), jnp.float32),
        pltpu.VMEM((far, rows, 128), jnp.float32),
        pltpu.VMEM((near, both, 128), jnp.float32),
        pltpu.VMEM((far, rows, 128), jnp.float32),
        dma((near,)),
        dma((near,)),
        dma((far,)),
        dma((far,)),
    ]


def small_task(count, ranks, both, x_ref, out_ref, scratch):
    got_h, got_s, sent_h, sent_s, hs, hr, ss, sr = scratch
    total = x_ref[:both]
    for i, (axis, partner) in enumerate(bit_partners("head", ranks)):
        sent_h[i] = total
        copy = remote(sent_h.at[i], got_h.at[i], hs.at[i], hr.at[i], axis, partner)
        copy.start()
        yield
        copy.wait()
        total = sent_h[i] + got_h[i]
    for i, (axis, partner) in enumerate(bit_partners("seq", count)):
        if i == 0:
            sent_s[0, :both] = total
            sent_s[0, both:] = x_ref[both:]
        else:
            sent_s[i] = sent_s[i - 1] + got_s[i - 1]
        copy = remote(sent_s.at[i], got_s.at[i], ss.at[i], sr.at[i], axis, partner)
        copy.start()
        yield
        copy.wait()
    last = len(powers(count)) - 1
    out_ref[...] = sent_s[last] + got_s[last]


def final_kernel(count, ranks, both, arrays, *refs):
    part_ref, small_ref, *x_refs = refs[: arrays + 2]
    total_ref, sum_ref, *out_refs = refs[arrays + 2 : 2 * arrays + 4]
    scratch = refs[2 * arrays + 4 :]
    n = len(head_sum_scratch(ranks, (1, 1, 8, 128)))
    m = 8
    greet(bit_partners("seq", count) + bit_partners("head", ranks))
    together(
        [
            share_task(count, x_refs, out_refs, scratch[n + m :]),
            head_sum_task(ranks, part_ref, total_ref, scratch[:n]),
            small_task(count, ranks, both, small_ref, sum_ref, scratch[n : n + m]),
        ]
    )


def final_sums(part, wide, narrow, grads):
    count = lax.axis_size("seq")
    ranks = lax.axis_size("head")
    whole = head_whole(part.shape)

    def padded(flat):
        size = -(-flat.shape[0] // 1024) * 1024
        return jnp.pad(flat, (0, size - flat.shape[0])).reshape(size // 128, 128)

    wide_flat = padded(jnp.concatenate([a.reshape(-1) for a in wide]))
    narrow_flat = padded(jnp.concatenate([a.reshape(-1) for a in narrow]))
    both = wide_flat.shape[0]
    small = jnp.concatenate([wide_flat, narrow_flat])
    blocks = [
        g.astype(jnp.bfloat16).reshape(count, g.shape[0] // count, g.shape[1]) for g in grads
    ]
    total, summed, *shares = pl.pallas_call(
        functools.partial(final_kernel, count, ranks, both, len(grads)),
        out_shape=[
            jax.ShapeDtypeStruct(whole, jnp.bfloat16),
            jax.ShapeDtypeStruct(small.shape, jnp.float32),
        ]
        + [jax.ShapeDtypeStruct(b.shape[1:], jnp.float32) for b in blocks],
        in_specs=[VMEM] * (len(grads) + 2),
        out_specs=[VMEM] * (len(grads) + 2),
        scratch_shapes=head_sum_scratch(ranks, whole)
        + small_scratch(count, ranks, small.shape[0], both)
        + share_scratch(count, [b.shape for b in blocks]),
        compiler_params=pltpu.CompilerParams(
            collective_id=3, has_side_effects=True, vmem_limit_bytes=56 << 20
        ),
        name="final_sums",
    )(part.astype(jnp.bfloat16).reshape(whole), small, *blocks)
    outs = []
    for flat, group in ((summed[:both].reshape(-1), wide), (summed[both:].reshape(-1), narrow)):
        at = 0
        for a in group:
            outs.append(flat[at : at + a.size].reshape(a.shape))
            at += a.size
    return total.reshape(part.shape), outs, shares


def seq_share(grad):
    return lax.psum_scatter(
        grad.astype(jnp.bfloat16), "seq", scatter_dimension=0, tiled=True
    ).astype(jnp.float32)


BLOCK = 128


def mm(left, right, dims=((1,), (0,))):
    return lax.dot_general(
        left.astype(jnp.bfloat16),
        right.astype(jnp.bfloat16),
        (dims, ((), ())),
        preferred_element_type=jnp.float32,
    )


AB = ((1,), (0,))
ABT = ((1,), (1,))
ATB = ((0,), (0,))


def parts(x):
    high = x.astype(jnp.bfloat16)
    return high, (x - high.astype(jnp.float32)).astype(jnp.bfloat16)


def fine_parts(left, right, dims=AB):
    lh, ll = left
    rh, rl = right
    return mm(lh, rh, dims) + (mm(lh, rl, dims) + mm(ll, rh, dims))


def fine(left, right, dims=AB):
    return fine_parts(parts(left), parts(right), dims)


def places(width):
    rows = lax.broadcasted_iota(jnp.int32, (width, width), 0)
    columns = lax.broadcasted_iota(jnp.int32, (width, width), 1)
    return rows, columns


def sigmoid(x):
    return 1.0 / (1.0 + jnp.exp(-x))


def softplus(x):
    return jnp.maximum(x, 0.0) + jnp.log1p(jnp.exp(-jnp.abs(x)))


def conv_rows(proj_ref, halo_ref, i):
    channels = halo_ref.shape[1]
    main = proj_ref[i * BLOCK : (i + 1) * BLOCK, :channels].astype(jnp.float32)
    if i == 0:
        ahead = halo_ref[...].astype(jnp.float32)
    else:
        ahead = proj_ref[i * BLOCK - 16 : i * BLOCK, :channels].astype(jnp.float32)
    rows = jnp.concatenate([ahead, main], 0)
    start = rows.shape[0] - BLOCK - (CONV - 1)
    return [rows[start + t : start + t + BLOCK] for t in range(CONV)]


def mixing(rows, taps_ref):
    mixed = rows[0] * taps_ref[0:1]
    for t in range(1, CONV):
        mixed = mixed + rows[t] * taps_ref[t : t + 1]
    return mixed


def unit_features(rows, taps_ref):
    mixed = mixing(rows, taps_ref)
    gate = sigmoid(mixed)
    active = mixed * gate
    query, key, value = active[:, :DK], active[:, DK : 2 * DK], active[:, 2 * DK :]
    query_norm = lax.rsqrt(jnp.sum(query * query, axis=-1, keepdims=True) + EPSILON)
    key_norm = lax.rsqrt(jnp.sum(key * key, axis=-1, keepdims=True) + EPSILON)
    return mixed, gate, active, query_norm, key_norm


def unit_decays(mix_ref, mix_t_ref, rate, i):
    span = slice(i * BLOCK, (i + 1) * BLOCK)
    beta = sigmoid(mix_ref[span, 0:1])
    ld_column = -rate * softplus(mix_ref[span, 1:2])
    ld_row = -rate * softplus(mix_t_ref[1:2, span])
    rows, columns = places(BLOCK)
    cumul = jnp.sum(jnp.where(rows >= columns, ld_row, 0.0), axis=1, keepdims=True)
    cumul_row = jnp.sum(jnp.where(rows <= columns, ld_column, 0.0), axis=0, keepdims=True)
    last = jnp.sum(ld_row, axis=1, keepdims=True)
    decay = jnp.exp(jnp.where(rows >= columns, cumul - cumul_row, NEGATIVE))
    return beta, ld_column, cumul, last, decay


def inverse_all(lowers):
    width = lowers[0].shape[0]
    rows, columns = places(width)

    def pairs(size):
        return (rows // size == columns // size + 1) & ((rows // size) % 2 == 1)

    eye = (rows == columns).astype(jnp.float32)
    inverses = [eye - jnp.where(pairs(1), lower, 0.0) for lower in lowers]
    size = 2
    while size < width:
        mask = pairs(size)
        cut = [parts(jnp.where(mask, lower, 0.0)) for lower in lowers]
        held = [parts(inverse) for inverse in inverses]
        middle = [fine_parts(a, b) for a, b in zip(held, cut)]
        inverses = [
            inverse - fine_parts(parts(m), a) for inverse, m, a in zip(inverses, middle, held)
        ]
        size *= 2
    return inverses


def front_kernel(
    proj_ref, halo_ref, mix_ref, mix_t_ref, taps_ref, rate_ref,
    inv_ref, solved_ref, value_ref, scores_ref, gq_ref, end_ref, last_ref, agg_ref,
):
    units = proj_ref.shape[0] // BLOCK
    rows, columns = places(BLOCK)
    strictly = rows > columns
    rate = jnp.exp(rate_ref[0:1, 0:1])
    kept = []
    for i in range(units):
        _, _, active, query_norm, key_norm = unit_features(
            conv_rows(proj_ref, halo_ref, i), taps_ref
        )
        query = active[:, :DK] * query_norm * DK ** (-0.5)
        key = active[:, DK : 2 * DK] * key_norm
        beta, _, cumul, last, decay = unit_decays(mix_ref, mix_t_ref, rate, i)
        split = parts(key)
        gram = fine_parts(split, split, ABT)
        lower = jnp.where(strictly, beta * decay * gram, 0.0)
        growth = jnp.exp(cumul)
        scores = decay * mm(query, key, ABT)
        span = slice(i * BLOCK, (i + 1) * BLOCK)
        scores_ref[span] = scores.astype(jnp.bfloat16)
        gq_ref[span] = (growth * query).astype(jnp.bfloat16)
        key_end = (jnp.exp(last - cumul) * key).astype(jnp.bfloat16)
        end_ref[span] = key_end
        sides = jnp.concatenate([(beta * growth) * key, beta * active[:, 2 * DK :]], axis=-1)
        finish = jnp.exp(last)
        last_ref[i : i + 1] = jnp.broadcast_to(finish, (1, 128))
        kept.append((lower, sides.astype(jnp.bfloat16), key_end, finish))
    inverses = inverse_all([unit[0] for unit in kept])
    total = None
    for i in range(units):
        span = slice(i * BLOCK, (i + 1) * BLOCK)
        _, sides, key_end, finish = kept[i]
        inverse = inverses[i].astype(jnp.bfloat16)
        inv_ref[span] = inverse
        solved = mm(inverse, sides)
        solved_ref[span] = solved.astype(jnp.bfloat16)
        value_ref[span] = solved[:, DK:]
        if total is None:
            fresh = jnp.concatenate([-solved[:, :DK], solved[:, DK:]], axis=-1)
            eye = (rows == columns).astype(jnp.float32)
            base = jnp.concatenate([finish * eye, jnp.zeros((DK, DV), jnp.float32)], axis=-1)
        else:
            moved = mm(solved[:, :DK], total)
            fresh = jnp.concatenate([-moved[:, :DK], solved[:, DK:] - moved[:, DK:]], axis=-1)
            base = finish * total
        total = base + mm(key_end, fresh, ATB)
    agg_ref[0] = total.astype(jnp.bfloat16)


def per_head(width, rows):
    return pl.BlockSpec((rows, width), lambda h: (0, h))


def stacked(*shape):
    return pl.BlockSpec((1,) + shape, lambda h: (h,) + (0,) * len(shape))


def squeezed(*shape):
    return pl.BlockSpec((None,) + shape, lambda h: (h,) + (0,) * len(shape))


def local_call(kernel, heads, name):
    def call(ins, outs, *arrays):
        return pl.pallas_call(
            kernel,
            grid=(heads,),
            in_specs=ins,
            out_specs=[spec for spec, _ in outs],
            out_shape=[shape for _, shape in outs],
            compiler_params=pltpu.CompilerParams(vmem_limit_bytes=48 << 20),
            name=name,
        )(*arrays)

    return call


def delta_front(projected, halo, mix, mix_t, taps, decay_log):
    length = projected.shape[0]
    heads = taps.shape[0]
    channels = taps.shape[2]
    f32, bf16 = jnp.float32, jnp.bfloat16
    units = length // BLOCK
    shape = jax.ShapeDtypeStruct

    def side(width, kind):
        return per_head(width, length), shape((length, heads * width), kind)

    rate = jnp.broadcast_to(decay_log[:, None, None], (heads, 8, 128))
    return local_call(front_kernel, heads, "delta_front")(
        [
            per_head(channels + DV, length),
            squeezed(16, channels),
            squeezed(length, 2),
            squeezed(2, length),
            squeezed(CONV, channels),
            squeezed(8, 128),
        ],
        [
            side(BLOCK, bf16),
            side(DK + DV, bf16),
            side(DV, f32),
            side(BLOCK, bf16),
            side(DK, bf16),
            side(DK, bf16),
            (squeezed(units, 128), shape((heads, units, 128), f32)),
            (stacked(DK, DK + DV), shape((heads, DK, DK + DV), bf16)),
        ],
        projected, halo, mix, mix_t, taps, rate,
    )


def outer_kernel(
    solved_ref, value_ref, scores_ref, gq_ref, end_ref, last_ref, carried_ref, proj_ref, gain_ref,
    out_ref, gated_ref, state_ref, fresh_ref,
):
    units = solved_ref.shape[0] // BLOCK
    state = carried_ref[...]
    for i in range(units):
        span = slice(i * BLOCK, (i + 1) * BLOCK)
        narrow = state.astype(jnp.bfloat16)
        state_ref[i] = narrow
        fresh = value_ref[span] - mm(solved_ref[span, :DK], narrow)
        fresh = fresh.astype(jnp.bfloat16)
        fresh_ref[span] = fresh
        out = mm(gq_ref[span], narrow) + mm(scores_ref[span], fresh)
        if i < units - 1:
            state = last_ref[i : i + 1, 0:1] * state + mm(end_ref[span], fresh, ATB)
        out_ref[span] = out
        gate = proj_ref[span, 2 * DK + DV :].astype(jnp.float32)
        normed = out * lax.rsqrt(jnp.mean(out * out, axis=-1, keepdims=True) + EPSILON)
        gated_ref[span] = (normed * gain_ref[...] * (gate * sigmoid(gate))).astype(jnp.bfloat16)


def delta_outer(front, carried, projected, gnorm_gain):
    inv, solved, value, scores, gq, end, last, agg = front
    length = solved.shape[0]
    heads = carried.shape[0]
    units = length // BLOCK
    f32, bf16 = jnp.float32, jnp.bfloat16
    shape = jax.ShapeDtypeStruct
    return local_call(outer_kernel, heads, "delta_outer")(
        [
            per_head(DK + DV, length),
            per_head(DV, length),
            per_head(BLOCK, length),
            per_head(DK, length),
            per_head(DK, length),
            squeezed(units, 128),
            squeezed(DK, DV),
            per_head(projected.shape[1] // heads, length),
            pl.BlockSpec((1, DV), lambda h: (0, 0)),
        ],
        [
            (per_head(DV, length), shape((length, heads * DV), f32)),
            (per_head(DV, length), shape((length, heads * DV), bf16)),
            (squeezed(units, DK, DV), shape((heads, units, DK, DV), bf16)),
            (per_head(DV, length), shape((length, heads * DV), bf16)),
        ],
        solved, value, scores, gq, end, last, carried, projected, gnorm_gain[None],
    )


def gate_kernel(
    grad_ref, out_ref, proj_ref, gain_ref, solved_ref, scores_ref, gq_ref, end_ref, last_ref,
    back_ref, gate_grad_ref, gain_grad_ref, feed_ref,
):
    units = solved_ref.shape[0] // BLOCK
    gain = gain_ref[...]
    total = jnp.zeros((1, DV), jnp.float32)
    later = None
    for i in reversed(range(units)):
        span = slice(i * BLOCK, (i + 1) * BLOCK)
        gate = proj_ref[span, 2 * DK + DV :].astype(jnp.float32)
        out = out_ref[span]
        grad = grad_ref[span]
        scale = lax.rsqrt(jnp.mean(out * out, axis=-1, keepdims=True) + EPSILON)
        normed = out * scale
        sig = sigmoid(gate)
        silu = gate * sig
        gate_grad = grad * (normed * gain) * (sig * (1.0 + gate * (1.0 - sig)))
        gate_grad_ref[span] = gate_grad.astype(jnp.bfloat16)
        wide = grad * silu
        total = total + jnp.sum(wide * normed, axis=0, keepdims=True)
        wide = wide * gain
        back = scale * (wide - normed * jnp.mean(wide * normed, axis=-1, keepdims=True))
        back = back.astype(jnp.bfloat16)
        back_ref[span] = back
        fresh = mm(scores_ref[span], back, ATB)
        step = mm(gq_ref[span], back, ATB)
        if later is not None:
            fresh = fresh + mm(end_ref[span], later)
            step = step + last_ref[i : i + 1, 0:1] * later
        later = step - mm(solved_ref[span, :DK], fresh, ATB)
    gain_grad_ref[...] = jnp.broadcast_to(total, (8, DV))
    feed_ref[0] = later.astype(jnp.bfloat16)


def delta_gate(grad, out, projected, gnorm_gain, front):
    inv, solved, value, scores, gq, end, last, agg = front
    length = solved.shape[0]
    heads = agg.shape[0]
    units = length // BLOCK
    f32, bf16 = jnp.float32, jnp.bfloat16
    shape = jax.ShapeDtypeStruct
    return local_call(gate_kernel, heads, "delta_gate")(
        [
            per_head(DV, length),
            per_head(DV, length),
            per_head(projected.shape[1] // heads, length),
            pl.BlockSpec((1, DV), lambda h: (0, 0)),
            per_head(DK + DV, length),
            per_head(BLOCK, length),
            per_head(DK, length),
            per_head(DK, length),
            squeezed(units, 128),
        ],
        [
            (per_head(DV, length), shape((length, heads * DV), bf16)),
            (per_head(DV, length), shape((length, heads * DV), bf16)),
            (squeezed(8, DV), shape((heads, 8, DV), f32)),
            (stacked(DK, DV), shape((heads, DK, DV), bf16)),
        ],
        grad, out, projected, gnorm_gain[None], solved, scores, gq, end, last,
    )


def back_terms_kernel(
    proj_ref, halo_ref, mix_ref, mix_t_ref, taps_ref, rate_ref,
    inv_ref, solved_ref, scores_ref, gq_ref, end_ref, last_ref, state_ref, fresh_ref,
    back_ref, later_ref, gate_grad_ref,
    proj_grad_ref, tail_ref, edge_ref, mix_grad_ref, small_ref,
):
    units = proj_ref.shape[0] // BLOCK
    channels = halo_ref.shape[1]
    rows, columns = places(BLOCK)
    strictly = rows > columns
    suffix = (rows <= columns).astype(jnp.bfloat16)
    rate = jnp.exp(rate_ref[0:1, 0:1])
    later = later_ref[...]
    follow = jnp.zeros((8, channels), jnp.float32)
    conv_total = [jnp.zeros((1, channels), jnp.float32) for _ in range(CONV)]
    decay_total = jnp.zeros((1, 1), jnp.float32)
    for i in reversed(range(units)):
        span = slice(i * BLOCK, (i + 1) * BLOCK)
        edged = conv_rows(proj_ref, halo_ref, i)
        mixed, gate, active, query_norm, key_norm = unit_features(edged, taps_ref)
        query_act, key_act, value = active[:, :DK], active[:, DK : 2 * DK], active[:, 2 * DK :]
        query = query_act * query_norm * DK ** (-0.5)
        key = key_act * key_norm
        beta, ld, cumul, last, decay = unit_decays(mix_ref, mix_t_ref, rate, i)
        growth = jnp.exp(cumul)
        key_b = key.astype(jnp.bfloat16)
        gram = mm(key_b, key_b, ABT)
        finish = last_ref[i : i + 1, 0:1]
        key_end = end_ref[span]
        gq = gq_ref[span]
        scores = scores_ref[span]
        solved = solved_ref[span]
        state = state_ref[i]
        fresh = fresh_ref[span]
        back = back_ref[span]
        later_b = later.astype(jnp.bfloat16)

        fresh_grad = mm(scores, back, ATB) + mm(key_end, later_b)
        fresh_grad_b = fresh_grad.astype(jnp.bfloat16)
        scores_grad = mm(back, fresh, ABT)
        gq_grad = mm(back, state, ABT)
        end_grad = mm(fresh, later_b, ABT)
        wide_grad = -mm(fresh_grad_b, state, ABT)
        finish_grad = jnp.sum(
            jnp.sum(state.astype(jnp.float32) * later, axis=0, keepdims=True),
            axis=1,
            keepdims=True,
        )
        later = mm(gq, back, ATB) + finish * later - mm(solved[:, :DK], fresh_grad_b, ATB)

        sides_grad = mm(
            inv_ref[span],
            jnp.concatenate([wide_grad.astype(jnp.bfloat16), fresh_grad_b], axis=-1),
            ATB,
        )
        lower_grad = jnp.where(strictly, -mm(sides_grad, solved, ABT) * decay, 0.0)
        key_side = sides_grad[:, :DK]
        value_side = sides_grad[:, DK:]
        key_dot = jnp.sum(key_side * key, axis=-1, keepdims=True)
        gram_part = lower_grad * gram
        beta_grad = (
            growth * key_dot
            + jnp.sum(value_side * value, axis=-1, keepdims=True)
            + jnp.sum(gram_part, axis=-1, keepdims=True)
        )
        gram_grad = (beta * lower_grad).astype(jnp.bfloat16)
        pair_grad = (scores_grad * decay).astype(jnp.bfloat16)
        end_part = end_grad * key_end.astype(jnp.float32)
        cross = beta * gram_part + scores_grad * scores.astype(jnp.float32)
        end_dot = jnp.sum(end_part, axis=-1, keepdims=True)
        single = (
            (beta * growth) * key_dot
            + jnp.sum(gq_grad * gq.astype(jnp.float32), axis=-1, keepdims=True)
            - end_dot
        )
        last_grad = jnp.sum(end_dot, axis=0, keepdims=True) + finish * finish_grad
        cross_parts = parts(cross)
        above = mm(suffix, cross_parts[0]) + mm(suffix, cross_parts[1])
        single_parts = parts(jnp.broadcast_to(single, (BLOCK, 128)))
        single_sum = mm(suffix, single_parts[0]) + mm(suffix, single_parts[1])
        ld_grad = (
            jnp.sum(jnp.where(columns < rows, above, 0.0), axis=-1, keepdims=True)
            + single_sum[:, 0:1]
            + last_grad
        )
        query_grad = growth * gq_grad + mm(pair_grad, key_b)
        key_grad = (
            (beta * growth) * key_side
            + jnp.exp(last - cumul) * end_grad
            + mm(gram_grad, key_b)
            + mm(gram_grad, key_b, ATB)
            + mm(pair_grad, query, ATB)
        )
        value_grad = beta * value_side

        decay_total = decay_total + jnp.sum(ld_grad * ld, axis=0, keepdims=True)
        mix_grad_ref[span, 0:1] = beta_grad * beta * (1.0 - beta)
        mix_grad_ref[span, 1:2] = ld_grad * (-rate) * sigmoid(mix_ref[span, 1:2])

        query_scaled = query_grad * DK ** (-0.5)
        query_dot = jnp.sum(query_scaled * query_act, axis=-1, keepdims=True)
        query_back = query_norm * (query_scaled - query_act * (query_norm * query_norm * query_dot))
        key_sum = jnp.sum(key_grad * key_act, axis=-1, keepdims=True)
        key_back = key_norm * (key_grad - key_act * (key_norm * key_norm * key_sum))
        active_grad = jnp.concatenate([query_back, key_back, value_grad], axis=-1)
        mixed_grad = active_grad * gate * (1.0 + mixed * (1.0 - gate))
        for t in range(CONV):
            conv_total[t] = conv_total[t] + jnp.sum(mixed_grad * edged[t], axis=0, keepdims=True)
        longer = jnp.concatenate([mixed_grad, follow], 0)
        grad = longer[CONV - 1 : CONV - 1 + BLOCK] * taps_ref[0:1]
        for t in range(1, CONV):
            begin = CONV - 1 - t
            grad = grad + longer[begin : begin + BLOCK] * taps_ref[t : t + 1]
        proj_grad_ref[span, :channels] = grad.astype(jnp.bfloat16)
        if i == units - 1:
            tail_ref[...] = grad[BLOCK - 16 :]
        follow = mixed_grad[:8]
    first = jnp.concatenate([jnp.zeros((16, channels), jnp.float32), follow], 0)
    spill = first[CONV - 1 : CONV - 1 + 16] * taps_ref[0:1]
    for t in range(1, CONV):
        begin = CONV - 1 - t
        spill = spill + first[begin : begin + 16] * taps_ref[t : t + 1]
    edge_ref[...] = spill
    proj_grad_ref[:, channels:] = gate_grad_ref[...]
    small_ref[0:CONV] = jnp.concatenate(conv_total, 0)
    small_ref[CONV : CONV + 1] = jnp.broadcast_to(decay_total, (1, channels))


def delta_back(projected, halo, mix, mix_t, taps, decay_log, front, states, fresh, back, later, gate_grad):
    inv, solved, value, scores, gq, end, last, agg = front
    length = projected.shape[0]
    heads = taps.shape[0]
    channels = taps.shape[2]
    units = length // BLOCK
    f32, bf16 = jnp.float32, jnp.bfloat16
    shape = jax.ShapeDtypeStruct
    rate = jnp.broadcast_to(decay_log[:, None, None], (heads, 8, 128))
    span = channels + DV
    return local_call(back_terms_kernel, heads, "delta_back")(
        [
            per_head(span, length),
            squeezed(16, channels),
            squeezed(length, 2),
            squeezed(2, length),
            squeezed(CONV, channels),
            squeezed(8, 128),
            per_head(BLOCK, length),
            per_head(DK + DV, length),
            per_head(BLOCK, length),
            per_head(DK, length),
            per_head(DK, length),
            squeezed(units, 128),
            squeezed(units, DK, DV),
            per_head(DV, length),
            per_head(DV, length),
            squeezed(DK, DV),
            per_head(DV, length),
        ],
        [
            (per_head(span, length), shape((length, heads * span), bf16)),
            (squeezed(16, channels), shape((heads, 16, channels), f32)),
            (squeezed(16, channels), shape((heads, 16, channels), f32)),
            (squeezed(length, 2), shape((heads, length, 2), f32)),
            (squeezed(8, channels), shape((heads, 8, channels), f32)),
        ],
        projected, halo, mix, mix_t, taps, rate, inv, solved, scores, gq, end, last, states, fresh,
        back, later, gate_grad,
    )


def rms_apply(values, gain):
    return values * lax.rsqrt(jnp.mean(values * values, axis=-1, keepdims=True) + EPSILON) * gain


def swiglu(gate_up):
    return jax.nn.silu(gate_up[:, 0]) * gate_up[:, 1]


def product(left, right, dims=((1,), (0,))):
    return lax.dot_general(left, right, (dims, ((), ())), preferred_element_type=jnp.float32)


def shards(
    block_input,
    norm1_gain,
    w_in,
    w_ba,
    conv_weight,
    decay_log,
    gnorm_gain,
    w_out,
    norm2_gain,
    w_up,
    w_down,
    grad_out,
):
    model = block_input.shape[1]
    heads = w_in.shape[1]
    span = w_in.shape[2]
    channels = conv_weight.shape[0]
    f32 = jnp.float32
    bf16 = jnp.bfloat16

    tail_rows = shifted(block_input[-16:], "seq", 1)
    tokens_wide = block_input.astype(f32)
    normed, pull_first = jax.vjp(rms_apply, tokens_wide, norm1_gain)
    normed_b = normed.astype(bf16)
    w_in_flat = w_in.reshape(model, heads * span)
    w_ba_flat = w_ba.reshape(model, 2 * heads)
    projected = product(normed_b, w_in_flat).astype(bf16)
    halo_normed = rms_apply(tail_rows.astype(f32), norm1_gain).astype(bf16)
    halo = product(halo_normed, w_in_flat).astype(bf16)
    halo = jnp.stack([halo[:, h * span : h * span + channels] for h in range(heads)])
    mixer_in = product(normed_b, w_ba_flat)
    mix = jnp.stack([mixer_in[:, h::heads] for h in range(heads)])
    mix_t = jnp.swapaxes(mix, 1, 2)
    taps = jnp.transpose(conv_weight, (1, 2, 0))
    front = delta_front(projected, halo, mix, mix_t, taps, decay_log)
    carried, maps = carried_forward(front[-1])
    layer_outputs, gated_b, states, fresh = delta_outer(front, carried, projected, gnorm_gain)
    w_out_flat = jnp.concatenate([w_out[:, h] for h in range(heads)], 0)
    mixed = head_sum(product(gated_b, w_out_flat)).astype(f32)
    hidden = tokens_wide + mixed
    hidden_n, pull_second = jax.vjp(rms_apply, hidden, norm2_gain)
    hidden_b = hidden_n.astype(bf16)
    gate_up = jnp.einsum("td,dcf->tcf", hidden_b, w_up, preferred_element_type=f32)
    swish, pull_swish = jax.vjp(swiglu, gate_up)
    swish_b = swish.astype(bf16)
    act_grad = product(grad_out, w_down)
    (gate_up_grad,) = pull_swish(act_grad)
    gate_up_b = gate_up_grad.astype(bf16)
    second_part = jnp.einsum("tcf,dcf->td", gate_up_b, w_up, preferred_element_type=f32)
    up_grad = jnp.einsum("td,tcf->dcf", hidden_b, gate_up_b, preferred_element_type=f32)
    down_grad = product(grad_out, swish_b, ((0,), (0,)))
    up_share = seq_share(up_grad)
    down_share = seq_share(down_grad)
    second_total = head_sum(second_part).astype(f32)
    hidden_grad, _ = pull_second(second_total)
    gain_second = pull_second(second_part)[1]
    stream = grad_out.astype(f32) + hidden_grad
    stream_b = stream.astype(bf16)
    gated_grad = product(stream_b, w_out_flat, ((1,), (1,)))
    back, gate_grad, gain_gated, feed = delta_gate(
        gated_grad, layer_outputs, projected, gnorm_gain, front
    )
    out_weight_grad = jnp.concatenate(
        [
            product(gated_b[:, h * DV : (h + 1) * DV], stream_b, ((0,), (0,))).astype(bf16)
            for h in range(heads)
        ],
        1,
    )
    ffn_part = product(swish_b, w_down, ((1,), (1,)))
    later, ffn_total = carried_back(feed, maps, ffn_part)
    result = hidden + ffn_total.astype(f32)
    proj_grad, tail, edge, mix_grad, small_grad = delta_back(
        projected, halo, mix, mix_t, taps, decay_log, front, states, fresh, back, later, gate_grad
    )
    back_edge = shifted(edge, "seq", -1)
    fixed = (tail + back_edge).astype(bf16)
    for h in range(heads):
        proj_grad = lax.dynamic_update_slice(
            proj_grad, fixed[h], (proj_grad.shape[0] - 16, h * span)
        )
    mixer_b = jnp.concatenate(
        [mix_grad[h, :, c : c + 1] for c in range(2) for h in range(heads)], 1
    ).astype(bf16)
    first_part = product(proj_grad, w_in_flat, ((1,), (1,)))
    first_part = first_part + product(mixer_b, w_ba_flat, ((1,), (1,)))
    in_weight_grad = product(normed_b, proj_grad, ((0,), (0,))).astype(bf16)
    gate_weight_grad = product(mixer_b, normed_b, ((0,), (0,)))
    gain_first = pull_first(first_part)[1]
    first_total, small, (in_share, out_share) = final_sums(
        first_part,
        [gain_first, gain_second, jnp.sum(gain_gated[:, 0], 0)],
        [small_grad[:, CONV, 0], small_grad[:, :CONV], gate_weight_grad],
        [in_weight_grad, out_weight_grad],
    )
    gain_one, gain_two, gain_norm, decay_total, conv_total, gate_total = small
    input_part, _ = pull_first(first_total.astype(f32))
    input_grad = stream + input_part
    in_share = in_share.reshape((in_share.shape[0],) + w_in.shape[1:])
    out_share = out_share.reshape((out_share.shape[0],) + w_out.shape[1:])
    count = lax.axis_size("seq")
    place = lax.axis_index("seq")

    def mine(whole, axis):
        share = whole.shape[axis] // count
        return lax.dynamic_slice_in_dim(whole, place * share, share, axis)

    return (
        result,
        input_grad,
        gain_one,
        in_share,
        mine(gate_total, 1).T.reshape(model // count, 2, heads),
        jnp.transpose(mine(conv_total, 2), (2, 0, 1)),
        decay_total,
        gain_norm,
        out_share,
        gain_two,
        up_share,
        down_share,
    )


def solution(mesh):
    return jax.shard_map(
        shards,
        mesh=mesh,
        in_specs=(
            P("seq", None),
            P(),
            P(None, "head", None),
            P(None, None, "head"),
            P(None, "head", None),
            P("head"),
            P(),
            P(None, "head", None),
            P(),
            P(None, None, "head"),
            P(None, "head"),
            P("seq", None),
        ),
        out_specs=(
            P("seq", None),
            P("seq", None),
            P(),
            P("seq", "head", None),
            P("seq", None, "head"),
            P("seq", "head", None),
            P("head"),
            P(),
            P("seq", "head", None),
            P(),
            P("seq", None, "head"),
            P("seq", "head"),
        ),
        check_vma=False,
    )
```

```python
import functools

import jax
import jax.numpy as jnp
from jax import lax
from jax.experimental import pallas as pl
from jax.experimental.pallas import tpu as pltpu
from jax.sharding import PartitionSpec as P

DK = 128
DV = 256
CONV = 4
STRETCH = 64


EPSILON = 1e-06
NEGATIVE = -1e30


def shifted(block, axis, distance):
    devices = range(lax.axis_size(axis))
    route = [(i - distance, i) for i in devices if i - distance in devices]
    return lax.ppermute(block, axis, route)


MESH = pl.DeviceIdType.MESH
PIECES = 4


def flipped(index, bit):
    mine = (index // bit) % 2
    return index + bit - 2 * bit * mine, mine


def powers(count):
    return [2**i for i in range(count.bit_length() - 1)]


def remote(src, dst, send_sem, recv_sem, axis, device):
    return pltpu.make_async_remote_copy(
        src_ref=src,
        dst_ref=dst,
        send_sem=send_sem,
        recv_sem=recv_sem,
        device_id={axis: device},
        device_id_type=MESH,
    )


def greet(partners):
    barrier = pltpu.get_barrier_semaphore()
    for axis, partner in partners:
        pl.semaphore_signal(barrier, inc=1, device_id={axis: partner}, device_id_type=MESH)
    pl.semaphore_wait(barrier, len(partners))


def together(tasks):
    live = list(tasks)
    while live:
        for task in list(live):
            try:
                next(task)
            except StopIteration:
                live.remove(task)


def bit_partners(axis, count):
    me = lax.axis_index(axis)
    return [(axis, flipped(me, bit)[0]) for bit in powers(count)]


def head_sum_scratch(count, whole):
    piece = whole[2:]
    steps = len(powers(count)) - 1
    dma = pltpu.SemaphoreType.DMA
    return [
        pltpu.VMEM((PIECES,) + piece, jnp.bfloat16),
        pltpu.VMEM((steps, PIECES) + piece, jnp.bfloat16),
        pltpu.VMEM((steps, PIECES) + piece, jnp.bfloat16),
        dma((PIECES,)),
        dma((PIECES,)),
        dma((steps, PIECES)),
        dma((steps, PIECES)),
        dma((PIECES,)),
        dma((PIECES,)),
    ]


def head_sum_task(count, x_ref, out_ref, scratch):
    first, held, sums, near_s, near_r, far_s, far_r, back_s, back_r = scratch
    me = lax.axis_index("head")
    bits = powers(count)
    partner, side = flipped(me, 1)
    peers = [flipped(me, bit)[0] for bit in bits[1:]]

    def send(src, dst, send_sem, recv_sem, device):
        copy = remote(src, dst, send_sem, recv_sem, "head", device)
        copy.start()
        return copy

    def add(left, right):
        return (left.astype(jnp.float32) + right.astype(jnp.float32)).astype(jnp.bfloat16)

    near = [
        send(x_ref.at[1 - side, k], first.at[k], near_s.at[k], near_r.at[k], partner)
        for k in range(PIECES)
    ]
    yield
    steps = len(peers)
    copies = []
    for k in range(PIECES):
        near[k].wait()
        sums[0, k] = add(x_ref[side, k], first[k])
        copies.append(
            send(sums.at[0, k], held.at[0, k], far_s.at[0, k], far_r.at[0, k], peers[0])
        )
    yield
    for step in range(steps):
        later = []
        for k in range(PIECES):
            copies[k].wait()
            total = add(sums[step, k], held[step, k])
            if step < steps - 1:
                sums[step + 1, k] = total
                later.append(
                    send(
                        sums.at[step + 1, k],
                        held.at[step + 1, k],
                        far_s.at[step + 1, k],
                        far_r.at[step + 1, k],
                        peers[step + 1],
                    )
                )
            else:
                out_ref[side, k] = total
                later.append(
                    send(
                        out_ref.at[side, k],
                        out_ref.at[side, k],
                        back_s.at[k],
                        back_r.at[k],
                        partner,
                    )
                )
            yield
        copies = later
    for copy in copies:
        copy.wait()


def head_whole(shape):
    rows, width = shape
    return (2, PIECES, rows // (2 * PIECES), width)


def head_sum_kernel(count, x_ref, out_ref, *scratch):
    greet(bit_partners("head", count))
    together([head_sum_task(count, x_ref, out_ref, scratch)])


VMEM = pl.BlockSpec(memory_space=pltpu.VMEM)


def head_sum(part):
    count = lax.axis_size("head")
    whole = head_whole(part.shape)
    total = pl.pallas_call(
        functools.partial(head_sum_kernel, count),
        out_shape=jax.ShapeDtypeStruct(whole, jnp.bfloat16),
        in_specs=[VMEM],
        out_specs=VMEM,
        scratch_shapes=head_sum_scratch(count, whole),
        compiler_params=pltpu.CompilerParams(
            collective_id=0, has_side_effects=True, vmem_limit_bytes=16 << 20
        ),
        cost_estimate=cost(0),
        name="head_sum",
    )(part.astype(jnp.bfloat16).reshape(whole))
    return total.reshape(part.shape)


def gather_scratch(count):
    dma = pltpu.SemaphoreType.DMA
    line = max(count // 2, 1)
    return [dma((line,)), dma((line,)), dma((line,)), dma((line,)), dma((2 * line,)), dma((2 * line,))]


def line_partners(count):
    me = lax.axis_index("seq")
    up, down = lax.rem(me + 2, count), lax.rem(me + count - 2, count)
    return [("seq", flipped(me, 1)[0]), ("seq", up), ("seq", down)]


def gather_task(count, out_ref, scratch):
    up_s, up_r, dn_s, dn_r, x_s, x_r = scratch
    me = lax.axis_index("seq")
    line = count // 2
    place, half = me // 2, lax.rem(me, 2)
    other, _ = flipped(me, 1)

    def hop(position, send_sem, recv_sem, device):
        block = out_ref.at[2 * position + half]
        return remote(block, block, send_sem, recv_sem, "seq", device)

    def up(step):
        return hop(place - (step - 1), up_s.at[step], up_r.at[step], me + 2)

    def down(step):
        return hop(place + (step - 1), dn_s.at[step], dn_r.at[step], me - 2)

    def came_up(step):
        return hop(place - step, up_s.at[step], up_r.at[step], me - 2)

    def came_down(step):
        return hop(place + step, dn_s.at[step], dn_r.at[step], me + 2)

    def across(number, position):
        return hop(position, x_s.at[number], x_r.at[number], other)

    def from_across(number, position):
        block = out_ref.at[2 * position + 1 - half]
        return remote(block, block, x_s.at[number], x_r.at[number], "seq", other)

    def sends_up(step):
        return (place + 1 < line) & (place - (step - 1) >= 0)

    def sends_down(step):
        return (place - 1 >= 0) & (place + (step - 1) < line)

    for step in range(1, line):
        if step > 1:
            @pl.when(place - (step - 1) >= 0)
            def _():
                came_up(step - 1).wait_recv()

        @pl.when(sends_up(step))
        def _():
            up(step).start()

        if step > 1:

            @pl.when(place + (step - 1) < line)
            def _():
                came_down(step - 1).wait_recv()

        @pl.when(sends_down(step))
        def _():
            down(step).start()

        if step == 1:
            across(0, place).start()
        else:

            @pl.when(place - (step - 1) >= 0)
            def _():
                across(2 * step - 3, place - (step - 1)).start()

            @pl.when(place + (step - 1) < line)
            def _():
                across(2 * step - 2, place + (step - 1)).start()

        yield
    last = line - 1

    @pl.when(place - last >= 0)
    def _():
        came_up(last).wait_recv()
        across(2 * last - 1, place - last).start()

    @pl.when(place + last < line)
    def _():
        came_down(last).wait_recv()
        across(2 * last, place + last).start()

    yield
    for step in range(1, line):

        @pl.when(sends_up(step))
        def _():
            up(step).wait_send()

        @pl.when(sends_down(step))
        def _():
            down(step).wait_send()

    across(0, place).wait_send()
    from_across(0, place).wait_recv()
    for step in range(1, line):

        @pl.when(place - step >= 0)
        def _():
            across(2 * step - 1, place - step).wait_send()
            from_across(2 * step - 1, place - step).wait_recv()

        @pl.when(place + step < line)
        def _():
            across(2 * step, place + step).wait_send()
            from_across(2 * step, place + step).wait_recv()


def carry_kernel(count, heads, x_ref, state_ref, all_ref, *scratch):
    me = lax.axis_index("seq")
    greet(line_partners(count))
    all_ref[me] = x_ref[...]
    together([gather_task(count, all_ref, scratch)])
    for h in range(heads):
        state = all_ref[0, h, :, DK:].astype(jnp.float32)
        state = jnp.where(me > 0, state, jnp.zeros_like(state))
        for source in range(1, count - 1):
            moved = jnp.dot(
                all_ref[source, h, :, :DK],
                state.astype(jnp.bfloat16),
                preferred_element_type=jnp.float32,
            ) + all_ref[source, h, :, DK:].astype(jnp.float32)
            state = jnp.where(source < me, moved, state)
        state_ref[h] = state


def carried_forward(part):
    count = lax.axis_size("seq")
    heads = part.shape[0]
    return pl.pallas_call(
        functools.partial(carry_kernel, count, heads),
        out_shape=[
            jax.ShapeDtypeStruct((heads, DK, DV), jnp.float32),
            jax.ShapeDtypeStruct((count,) + part.shape, jnp.bfloat16),
        ],
        in_specs=[VMEM],
        out_specs=[VMEM, VMEM],
        scratch_shapes=gather_scratch(count),
        compiler_params=pltpu.CompilerParams(
            collective_id=1, has_side_effects=True, vmem_limit_bytes=24 << 20
        ),
        cost_estimate=cost(0),
        name="carry_forward",
    )(part.astype(jnp.bfloat16))


def back_kernel(count, ranks, heads, x_ref, maps_ref, part_ref, state_ref, total_ref, all_ref, *scratch):
    me = lax.axis_index("seq")
    n = len(gather_scratch(count))
    greet(line_partners(count) + bit_partners("head", ranks))
    all_ref[me] = x_ref[...]
    together(
        [
            gather_task(count, all_ref, scratch[:n]),
            head_sum_task(ranks, part_ref, total_ref, scratch[n:]),
        ]
    )
    for h in range(heads):
        state = all_ref[count - 1, h].astype(jnp.float32)
        state = jnp.where(me < count - 1, state, jnp.zeros_like(state))
        for source in range(count - 2, 0, -1):
            moved = lax.dot_general(
                maps_ref[source, h, :, :DK],
                state.astype(jnp.bfloat16),
                (((0,), (0,)), ((), ())),
                preferred_element_type=jnp.float32,
            ) + all_ref[source, h].astype(jnp.float32)
            state = jnp.where(source > me, moved, state)
        state_ref[h] = state


def carried_back(feed, maps, part):
    count = lax.axis_size("seq")
    ranks = lax.axis_size("head")
    heads = feed.shape[0]
    whole = head_whole(part.shape)
    state, total = pl.pallas_call(
        functools.partial(back_kernel, count, ranks, heads),
        out_shape=[
            jax.ShapeDtypeStruct((heads, DK, DV), jnp.float32),
            jax.ShapeDtypeStruct(whole, jnp.bfloat16),
        ],
        in_specs=[VMEM] * 3,
        out_specs=[VMEM] * 2,
        scratch_shapes=[pltpu.VMEM((count,) + feed.shape, jnp.bfloat16)]
        + gather_scratch(count)
        + head_sum_scratch(ranks, whole),
        compiler_params=pltpu.CompilerParams(
            collective_id=2, has_side_effects=True, vmem_limit_bytes=32 << 20
        ),
        cost_estimate=cost(0),
        name="carry_back",
    )(feed.astype(jnp.bfloat16), maps, part.astype(jnp.bfloat16).reshape(whole))
    return state, total.reshape(part.shape)


def share_works(count, shapes):
    bits = powers(count)
    works = []
    for a, (_, rows, width) in enumerate(shapes):
        pieces = 2
        size = width // pieces
        for piece in range(pieces):
            order = bits if piece < pieces - 1 else bits[1:] + bits[:1]
            works.append((a, pl.ds(piece * size, size), order, (rows, size)))
    return sorted(works, key=lambda work: work[1].start)


def share_scratch(count, shapes):
    steps = len(powers(count))
    works = share_works(count, shapes)
    dma = pltpu.SemaphoreType.DMA
    return (
        [pltpu.VMEM((steps, count // 2) + work[3], jnp.bfloat16) for work in works]
        + [pltpu.VMEM((max(steps - 1, 1), count // 4) + work[3], jnp.bfloat16) for work in works]
        + [dma((len(works), steps, count // 2)), dma((len(works), steps, count // 2))]
    )


def share_task(count, x_refs, out_refs, scratch):
    works = share_works(count, [x.shape for x in x_refs])
    recv_refs, send_refs = scratch[: len(works)], scratch[len(works) : 2 * len(works)]
    send_sem, recv_sem = scratch[2 * len(works) :]
    me = lax.axis_index("seq")
    bits = powers(count)
    partners = {bit: flipped(me, bit)[0] for bit in bits}

    def block(relative):
        index = me
        for bit in bits:
            if relative & bit:
                index = flipped(index, bit)[0]
        return index

    def kept(order, step):
        used = sum(order[:step])
        return [r for r in range(count) if r & used == 0]

    def slot(order, step, relative):
        return kept(order, step + 1).index(relative)

    def partial_sum(number, relative, step):
        a, cols, order, _ = works[number]
        total = x_refs[a][block(relative), :, cols].astype(jnp.float32)
        for earlier in range(step):
            total = total + recv_refs[number][earlier, slot(order, earlier, relative)].astype(
                jnp.float32
            )
        return total

    pending = {}
    for step in range(len(bits) + 1):
        for number, (a, cols, order, _) in enumerate(works):
            for copy in pending.pop(number, []):
                copy.wait()
            if step == len(bits):
                out_refs[a][:, cols] = partial_sum(number, 0, step)
                continue
            bit = order[step]
            started = []
            for relative in kept(order, step):
                if not relative & bit:
                    continue
                place = slot(order, step, relative - bit)
                if step == 0:
                    source = x_refs[a].at[block(relative), :, cols]
                else:
                    send_refs[number][step - 1, place] = partial_sum(
                        number, relative, step
                    ).astype(jnp.bfloat16)
                    source = send_refs[number].at[step - 1, place]
                copy = remote(
                    source,
                    recv_refs[number].at[step, place],
                    send_sem.at[number, step, place],
                    recv_sem.at[number, step, place],
                    "seq",
                    partners[bit],
                )
                copy.start()
                started.append(copy)
            pending[number] = started
            if step:
                yield
        yield


def small_scratch(count, ranks, rows, both):
    dma = pltpu.SemaphoreType.DMA
    near, far = len(powers(ranks)), len(powers(count))
    return [
        pltpu.VMEM((near, both, 128), jnp.float32),
        pltpu.VMEM((far, rows, 128), jnp.float32),
        pltpu.VMEM((near, both, 128), jnp.float32),
        pltpu.VMEM((far, rows, 128), jnp.float32),
        dma((near,)),
        dma((near,)),
        dma((far,)),
        dma((far,)),
    ]


def small_task(count, ranks, both, x_ref, out_ref, scratch):
    got_h, got_s, sent_h, sent_s, hs, hr, ss, sr = scratch
    total = x_ref[:both]
    for i, (axis, partner) in enumerate(bit_partners("head", ranks)):
        sent_h[i] = total
        copy = remote(sent_h.at[i], got_h.at[i], hs.at[i], hr.at[i], axis, partner)
        copy.start()
        yield
        copy.wait()
        total = sent_h[i] + got_h[i]
    for i, (axis, partner) in enumerate(bit_partners("seq", count)):
        if i == 0:
            sent_s[0, :both] = total
            sent_s[0, both:] = x_ref[both:]
        else:
            sent_s[i] = sent_s[i - 1] + got_s[i - 1]
        copy = remote(sent_s.at[i], got_s.at[i], ss.at[i], sr.at[i], axis, partner)
        copy.start()
        yield
        copy.wait()
    last = len(powers(count)) - 1
    out_ref[...] = sent_s[last] + got_s[last]


def input_task(before, total_ref, tokens_ref, gain_ref, stream_ref, grad_ref):
    yield from before
    for side in range(total_ref.shape[0]):
        for k in range(total_ref.shape[1]):
            tokens = tokens_ref[side, k].astype(jnp.float32)
            scale = lax.rsqrt(jnp.mean(tokens * tokens, axis=-1, keepdims=True) + EPSILON)
            normed = tokens * scale
            wide = total_ref[side, k].astype(jnp.float32) * gain_ref[...]
            along = jnp.mean(wide * normed, axis=-1, keepdims=True)
            grad_ref[side, k] = stream_ref[side, k] + scale * (wide - normed * along)
        yield


def final_kernel(count, ranks, both, arrays, *refs):
    part_ref, small_ref, tokens_ref, gain_ref, stream_ref, *x_refs = refs[: arrays + 5]
    grad_ref, sum_ref, *out_refs = refs[arrays + 5 : 2 * arrays + 7]
    total_ref, *scratch = refs[2 * arrays + 7 :]
    n = len(head_sum_scratch(ranks, (1, 1, 8, 128)))
    m = 8
    greet(bit_partners("seq", count) + bit_partners("head", ranks))
    together(
        [
            share_task(count, x_refs, out_refs, scratch[n + m :]),
            input_task(
                head_sum_task(ranks, part_ref, total_ref, scratch[:n]),
                total_ref, tokens_ref, gain_ref, stream_ref, grad_ref,
            ),
            small_task(count, ranks, both, small_ref, sum_ref, scratch[n : n + m]),
        ]
    )


def final_sums(part, tokens, gain, stream, wide, narrow, grads):
    count = lax.axis_size("seq")
    ranks = lax.axis_size("head")
    whole = head_whole(part.shape)

    def padded(flat):
        size = -(-flat.shape[0] // 1024) * 1024
        return jnp.pad(flat, (0, size - flat.shape[0])).reshape(size // 128, 128)

    wide_flat = padded(jnp.concatenate([a.reshape(-1) for a in wide]))
    narrow_flat = padded(jnp.concatenate([a.reshape(-1) for a in narrow]))
    both = wide_flat.shape[0]
    small = jnp.concatenate([wide_flat, narrow_flat])
    blocks = [
        g.astype(jnp.bfloat16).reshape(count, g.shape[0] // count, g.shape[1]) for g in grads
    ]
    total, summed, *shares = pl.pallas_call(
        functools.partial(final_kernel, count, ranks, both, len(grads)),
        out_shape=[
            jax.ShapeDtypeStruct(whole, jnp.float32),
            jax.ShapeDtypeStruct(small.shape, jnp.float32),
        ]
        + [jax.ShapeDtypeStruct(b.shape[1:], jnp.float32) for b in blocks],
        in_specs=[VMEM] * (len(grads) + 5),
        out_specs=[VMEM] * (len(grads) + 2),
        scratch_shapes=[pltpu.VMEM(whole, jnp.bfloat16)]
        + head_sum_scratch(ranks, whole)
        + small_scratch(count, ranks, small.shape[0], both)
        + share_scratch(count, [b.shape for b in blocks]),
        compiler_params=pltpu.CompilerParams(
            collective_id=3, has_side_effects=True, vmem_limit_bytes=56 << 20
        ),
        cost_estimate=cost(0),
        name="final_sums",
    )(
        part.astype(jnp.bfloat16).reshape(whole),
        small,
        tokens.reshape(whole),
        gain[None],
        stream.reshape(whole),
        *blocks,
    )
    outs = []
    for flat, group in ((summed[:both].reshape(-1), wide), (summed[both:].reshape(-1), narrow)):
        at = 0
        for a in group:
            outs.append(flat[at : at + a.size].reshape(a.shape))
            at += a.size
    return total.reshape(part.shape), outs, shares


class Share:
    def __init__(self, grad, order):
        count = lax.axis_size("seq")
        self.bits = powers(count)[::-1]
        self.order = list(order)
        self.count = count
        rows = grad.shape[0] // count
        self.blocks = grad.astype(jnp.bfloat16).reshape((2,) * len(self.bits) + (rows, -1))

    def cut(self):
        bit = self.order[0]
        axis = self.bits.index(bit)
        mine = lax.rem(lax.axis_index("seq") // bit, 2)
        self.keep = lax.dynamic_index_in_dim(self.blocks, mine, axis, False)
        self.send = lax.dynamic_index_in_dim(self.blocks, 1 - mine, axis, False)

    def start(self):
        bit = self.order.pop(0)
        self.bits.remove(bit)
        route = [(i, i ^ bit) for i in range(self.count)]
        self.got = lax.ppermute(self.send, "seq", route)

    def add(self):
        total = self.keep.astype(jnp.float32) + self.got.astype(jnp.float32)
        self.blocks = total if not self.order else total.astype(jnp.bfloat16)


def begin(shares, beside):
    for share in shares:
        share.cut()
    beside, sends = lax.optimization_barrier((beside, [share.send for share in shares]))
    for share, send in zip(shares, sends):
        share.send = send
        share.start()
    return beside


def proceed(shares, beside):
    beside, got = lax.optimization_barrier((beside, [share.got for share in shares]))
    for share, g in zip(shares, got):
        share.got = g
        share.add()
    left = [share for share in shares if share.order]
    return begin(left, beside) if left else beside


BLOCK = 128


def mm(left, right, dims=((1,), (0,))):
    return lax.dot_general(
        left.astype(jnp.bfloat16),
        right.astype(jnp.bfloat16),
        (dims, ((), ())),
        preferred_element_type=jnp.float32,
    )


AB = ((1,), (0,))
ABT = ((1,), (1,))
ATB = ((0,), (0,))


def parts(x):
    high = x.astype(jnp.bfloat16)
    return high, (x - high.astype(jnp.float32)).astype(jnp.bfloat16)


def fine_parts(left, right, dims=AB):
    lh, ll = left
    rh, rl = right
    return mm(lh, rh, dims) + (mm(lh, rl, dims) + mm(ll, rh, dims))


def fine(left, right, dims=AB):
    return fine_parts(parts(left), parts(right), dims)


def places(width):
    rows = lax.broadcasted_iota(jnp.int32, (width, width), 0)
    columns = lax.broadcasted_iota(jnp.int32, (width, width), 1)
    return rows, columns


def sigmoid(x):
    return 1.0 / (1.0 + jnp.exp(-x))


def softplus(x):
    return jnp.maximum(x, 0.0) + jnp.log1p(jnp.exp(-jnp.abs(x)))


def conv_rows(proj_ref, halo_ref, i):
    channels = halo_ref.shape[1]
    main = proj_ref[i * BLOCK : (i + 1) * BLOCK, :channels].astype(jnp.float32)
    if i == 0:
        ahead = halo_ref[...].astype(jnp.float32)
    else:
        ahead = proj_ref[i * BLOCK - 16 : i * BLOCK, :channels].astype(jnp.float32)
    rows = jnp.concatenate([ahead, main], 0)
    start = rows.shape[0] - BLOCK - (CONV - 1)
    return [rows[start + t : start + t + BLOCK] for t in range(CONV)]


def mixing(rows, taps_ref):
    mixed = rows[0] * taps_ref[0:1]
    for t in range(1, CONV):
        mixed = mixed + rows[t] * taps_ref[t : t + 1]
    return mixed


def unit_features(rows, taps_ref):
    mixed = mixing(rows, taps_ref)
    gate = sigmoid(mixed)
    active = mixed * gate
    query, key, value = active[:, :DK], active[:, DK : 2 * DK], active[:, 2 * DK :]
    query_norm = lax.rsqrt(jnp.sum(query * query, axis=-1, keepdims=True) + EPSILON)
    key_norm = lax.rsqrt(jnp.sum(key * key, axis=-1, keepdims=True) + EPSILON)
    return mixed, gate, active, query_norm, key_norm


def unit_decays(mix_ref, mix_t_ref, rate, i):
    span = slice(i * BLOCK, (i + 1) * BLOCK)
    beta = sigmoid(mix_ref[span, 0:1])
    ld_column = -rate * softplus(mix_ref[span, 1:2])
    ld_row = -rate * softplus(mix_t_ref[1:2, span])
    rows, columns = places(BLOCK)
    cumul = jnp.sum(jnp.where(rows >= columns, ld_row, 0.0), axis=1, keepdims=True)
    cumul_row = jnp.sum(jnp.where(rows <= columns, ld_column, 0.0), axis=0, keepdims=True)
    last = jnp.sum(ld_row, axis=1, keepdims=True)
    decay = jnp.exp(jnp.where(rows >= columns, cumul - cumul_row, NEGATIVE))
    return beta, ld_column, cumul, last, decay


def inverse_all(lowers):
    width = lowers[0].shape[0]
    rows, columns = places(width)

    def pairs(size):
        return (rows // size == columns // size + 1) & ((rows // size) % 2 == 1)

    eye = (rows == columns).astype(jnp.float32)
    inverses = [eye - jnp.where(pairs(1), lower, 0.0) for lower in lowers]
    size = 2
    while size < width:
        mask = pairs(size)
        cut = [parts(jnp.where(mask, lower, 0.0)) for lower in lowers]
        held = [parts(inverse) for inverse in inverses]
        middle = [fine_parts(a, b) for a, b in zip(held, cut)]
        inverses = [
            inverse - fine_parts(parts(m), a) for inverse, m, a in zip(inverses, middle, held)
        ]
        size *= 2
    return inverses


def front_kernel(
    proj_ref, halo_ref, mix_ref, mix_t_ref, taps_ref, rate_ref,
    inv_ref, solved_ref, scores_ref, gq_ref, end_ref, last_ref, agg_ref,
):
    units = proj_ref.shape[0] // BLOCK
    rows, columns = places(BLOCK)
    strictly = rows > columns
    rate = jnp.exp(rate_ref[0:1, 0:1])
    kept = []
    for i in range(units):
        _, _, active, query_norm, key_norm = unit_features(
            conv_rows(proj_ref, halo_ref, i), taps_ref
        )
        query = active[:, :DK] * query_norm * DK ** (-0.5)
        key = active[:, DK : 2 * DK] * key_norm
        beta, _, cumul, last, decay = unit_decays(mix_ref, mix_t_ref, rate, i)
        split = parts(key)
        gram = fine_parts(split, split, ABT)
        lower = jnp.where(strictly, beta * decay * gram, 0.0)
        growth = jnp.exp(cumul)
        scores = decay * mm(query, key, ABT)
        span = slice(i * BLOCK, (i + 1) * BLOCK)
        scores_ref[span] = scores
        gq_ref[span] = growth * query
        key_end = jnp.exp(last - cumul) * key
        end_ref[span] = key_end
        sides = jnp.concatenate([(beta * growth) * key, beta * active[:, 2 * DK :]], axis=-1)
        finish = jnp.exp(last)
        last_ref[i : i + 1] = jnp.broadcast_to(finish, (1, 128))
        kept.append((lower, sides.astype(jnp.bfloat16), key_end, finish))
    inverses = inverse_all([unit[0] for unit in kept])
    total = None
    for i in range(units):
        span = slice(i * BLOCK, (i + 1) * BLOCK)
        _, sides, key_end, finish = kept[i]
        inverse = inverses[i].astype(jnp.bfloat16)
        inv_ref[span] = inverse
        solved = mm(inverse, sides)
        solved_ref[span] = solved
        if total is None:
            fresh = jnp.concatenate([-solved[:, :DK], solved[:, DK:]], axis=-1)
            eye = (rows == columns).astype(jnp.float32)
            base = jnp.concatenate([finish * eye, jnp.zeros((DK, DV), jnp.float32)], axis=-1)
        else:
            moved = fine(solved[:, :DK], total)
            fresh = jnp.concatenate([-moved[:, :DK], solved[:, DK:] - moved[:, DK:]], axis=-1)
            base = finish * total
        total = base + fine(key_end, fresh, ATB)
    agg_ref[0] = total.astype(jnp.bfloat16)


def per_head(width, rows):
    return pl.BlockSpec((rows, width), lambda h: (0, h))


def stacked(*shape):
    return pl.BlockSpec((1,) + shape, lambda h: (h,) + (0,) * len(shape))


def squeezed(*shape):
    return pl.BlockSpec((None,) + shape, lambda h: (h,) + (0,) * len(shape))


def cost(micros):
    return pl.CostEstimate(flops=int(micros * 1e9), bytes_accessed=1 << 20, transcendentals=0)


def local_call(kernel, heads, name, micros):
    def call(ins, outs, *arrays):
        return pl.pallas_call(
            kernel,
            grid=(heads,),
            in_specs=ins,
            out_specs=[spec for spec, _ in outs],
            out_shape=[shape for _, shape in outs],
            compiler_params=pltpu.CompilerParams(vmem_limit_bytes=48 << 20),
            cost_estimate=cost(micros),
            name=name,
        )(*arrays)

    return call


def delta_front(projected, halo, mix, mix_t, taps, decay_log):
    length = projected.shape[0]
    heads = taps.shape[0]
    channels = taps.shape[2]
    f32, bf16 = jnp.float32, jnp.bfloat16
    units = length // BLOCK
    shape = jax.ShapeDtypeStruct

    def side(width, kind):
        return per_head(width, length), shape((length, heads * width), kind)

    rate = jnp.broadcast_to(decay_log[:, None, None], (heads, 8, 128))
    return local_call(front_kernel, heads, "delta_front", 0)(
        [
            per_head(channels + DV, length),
            squeezed(16, channels),
            squeezed(length, 2),
            squeezed(2, length),
            squeezed(CONV, channels),
            squeezed(8, 128),
        ],
        [
            side(BLOCK, bf16),
            side(DK + DV, f32),
            side(BLOCK, f32),
            side(DK, f32),
            side(DK, f32),
            (squeezed(units, 128), shape((heads, units, 128), f32)),
            (stacked(DK, DK + DV), shape((heads, DK, DK + DV), bf16)),
        ],
        projected, halo, mix, mix_t, taps, rate,
    )


def outer_kernel(
    solved_ref, scores_ref, gq_ref, end_ref, last_ref, carried_ref, proj_ref, gain_ref,
    out_ref, gated_ref, state_ref, fresh_ref,
):
    units = solved_ref.shape[0] // BLOCK
    state = carried_ref[...]
    for i in range(units):
        span = slice(i * BLOCK, (i + 1) * BLOCK)
        narrow = state.astype(jnp.bfloat16)
        state_ref[i] = state
        fresh = solved_ref[span, DK:] - mm(solved_ref[span, :DK], narrow)
        fresh = fresh.astype(jnp.bfloat16)
        fresh_ref[span] = fresh
        out = mm(gq_ref[span], narrow) + mm(scores_ref[span], fresh)
        if i < units - 1:
            state = last_ref[i : i + 1, 0:1] * state + mm(end_ref[span], fresh, ATB)
        out_ref[span] = out
        gate = proj_ref[span, 2 * DK + DV :].astype(jnp.float32)
        normed = out * lax.rsqrt(jnp.mean(out * out, axis=-1, keepdims=True) + EPSILON)
        gated_ref[span] = (normed * gain_ref[...] * (gate * sigmoid(gate))).astype(jnp.bfloat16)


def delta_outer(front, carried, projected, gnorm_gain):
    inv, solved, scores, gq, end, last, agg = front
    length = solved.shape[0]
    heads = carried.shape[0]
    units = length // BLOCK
    f32, bf16 = jnp.float32, jnp.bfloat16
    shape = jax.ShapeDtypeStruct
    return local_call(outer_kernel, heads, "delta_outer", 0)(
        [
            per_head(DK + DV, length),
            per_head(BLOCK, length),
            per_head(DK, length),
            per_head(DK, length),
            squeezed(units, 128),
            squeezed(DK, DV),
            per_head(projected.shape[1] // heads, length),
            pl.BlockSpec((1, DV), lambda h: (0, 0)),
        ],
        [
            (per_head(DV, length), shape((length, heads * DV), f32)),
            (per_head(DV, length), shape((length, heads * DV), bf16)),
            (squeezed(units, DK, DV), shape((heads, units, DK, DV), f32)),
            (per_head(DV, length), shape((length, heads * DV), bf16)),
        ],
        solved, scores, gq, end, last, carried, projected, gnorm_gain[None],
    )


def gate_kernel(
    grad_ref, out_ref, proj_ref, gain_ref, solved_ref, scores_ref, gq_ref, end_ref, last_ref,
    back_ref, gate_grad_ref, gain_grad_ref, feed_ref,
):
    units = solved_ref.shape[0] // BLOCK
    gain = gain_ref[...]
    total = jnp.zeros((1, DV), jnp.float32)
    later = None
    for i in reversed(range(units)):
        span = slice(i * BLOCK, (i + 1) * BLOCK)
        gate = proj_ref[span, 2 * DK + DV :].astype(jnp.float32)
        out = out_ref[span]
        grad = grad_ref[span]
        scale = lax.rsqrt(jnp.mean(out * out, axis=-1, keepdims=True) + EPSILON)
        normed = out * scale
        sig = sigmoid(gate)
        silu = gate * sig
        gate_grad = grad * (normed * gain) * (sig * (1.0 + gate * (1.0 - sig)))
        gate_grad_ref[span] = gate_grad.astype(jnp.bfloat16)
        wide = grad * silu
        total = total + jnp.sum(wide * normed, axis=0, keepdims=True)
        wide = wide * gain
        back = scale * (wide - normed * jnp.mean(wide * normed, axis=-1, keepdims=True))
        back = back.astype(jnp.bfloat16)
        back_ref[span] = back
        fresh = mm(scores_ref[span], back, ATB)
        step = mm(gq_ref[span], back, ATB)
        if later is not None:
            fresh = fresh + fine(end_ref[span], later)
            step = step + last_ref[i : i + 1, 0:1] * later
        later = step - fine(solved_ref[span, :DK], fresh, ATB)
    gain_grad_ref[...] = jnp.broadcast_to(total, (8, DV))
    feed_ref[0] = later.astype(jnp.bfloat16)


def delta_gate(grad, out, projected, gnorm_gain, front):
    inv, solved, scores, gq, end, last, agg = front
    length = solved.shape[0]
    heads = agg.shape[0]
    units = length // BLOCK
    f32, bf16 = jnp.float32, jnp.bfloat16
    shape = jax.ShapeDtypeStruct
    return local_call(gate_kernel, heads, "delta_gate", 0)(
        [
            per_head(DV, length),
            per_head(DV, length),
            per_head(projected.shape[1] // heads, length),
            pl.BlockSpec((1, DV), lambda h: (0, 0)),
            per_head(DK + DV, length),
            per_head(BLOCK, length),
            per_head(DK, length),
            per_head(DK, length),
            squeezed(units, 128),
        ],
        [
            (per_head(DV, length), shape((length, heads * DV), bf16)),
            (per_head(DV, length), shape((length, heads * DV), bf16)),
            (squeezed(8, DV), shape((heads, 8, DV), f32)),
            (stacked(DK, DV), shape((heads, DK, DV), bf16)),
        ],
        grad, out, projected, gnorm_gain[None], solved, scores, gq, end, last,
    )


def back_terms_kernel(
    proj_ref, halo_ref, mix_ref, mix_t_ref, taps_ref, rate_ref,
    inv_ref, solved_ref, scores_ref, gq_ref, end_ref, last_ref, state_ref, fresh_ref,
    back_ref, later_ref, gate_grad_ref,
    proj_grad_ref, tail_ref, edge_ref, mix_grad_ref, small_ref,
):
    units = proj_ref.shape[0] // BLOCK
    channels = halo_ref.shape[1]
    rows, columns = places(BLOCK)
    strictly = rows > columns
    suffix = (rows <= columns).astype(jnp.bfloat16)
    rate = jnp.exp(rate_ref[0:1, 0:1])
    later = later_ref[...]
    follow = jnp.zeros((8, channels), jnp.float32)
    conv_total = [jnp.zeros((1, channels), jnp.float32) for _ in range(CONV)]
    decay_total = jnp.zeros((1, 1), jnp.float32)
    for i in reversed(range(units)):
        span = slice(i * BLOCK, (i + 1) * BLOCK)
        edged = conv_rows(proj_ref, halo_ref, i)
        mixed, gate, active, query_norm, key_norm = unit_features(edged, taps_ref)
        query_act, key_act, value = active[:, :DK], active[:, DK : 2 * DK], active[:, 2 * DK :]
        query = query_act * query_norm * DK ** (-0.5)
        key = key_act * key_norm
        beta, ld, cumul, last, decay = unit_decays(mix_ref, mix_t_ref, rate, i)
        growth = jnp.exp(cumul)
        key_b = key.astype(jnp.bfloat16)
        key_parts = parts(key)
        gram = fine_parts(key_parts, key_parts, ABT)
        finish = last_ref[i : i + 1, 0:1]
        key_end = end_ref[span]
        gq = gq_ref[span]
        scores = scores_ref[span]
        solved = solved_ref[span]
        solved_b = solved.astype(jnp.bfloat16)
        state = state_ref[i]
        state_b = state.astype(jnp.bfloat16)
        fresh = fresh_ref[span]
        back = back_ref[span]
        later_b = later.astype(jnp.bfloat16)

        fresh_grad = mm(scores, back, ATB) + fine(key_end, later)
        fresh_grad_b = fresh_grad.astype(jnp.bfloat16)
        scores_grad = mm(back, fresh, ABT)
        gq_grad = mm(back, state_b, ABT)
        end_grad = mm(fresh, later_b, ABT)
        wide_grad = -mm(fresh_grad_b, state_b, ABT)
        finish_grad = jnp.sum(
            jnp.sum(state * later, axis=0, keepdims=True),
            axis=1,
            keepdims=True,
        )
        later = mm(gq, back, ATB) + finish * later - fine(solved[:, :DK], fresh_grad, ATB)

        sides_grad = mm(
            inv_ref[span],
            jnp.concatenate([wide_grad.astype(jnp.bfloat16), fresh_grad_b], axis=-1),
            ATB,
        )
        lower_grad = jnp.where(strictly, -mm(sides_grad, solved_b, ABT) * decay, 0.0)
        key_side = sides_grad[:, :DK]
        value_side = sides_grad[:, DK:]
        key_dot = jnp.sum(key_side * key, axis=-1, keepdims=True)
        gram_part = lower_grad * gram
        beta_grad = (
            growth * key_dot
            + jnp.sum(value_side * value, axis=-1, keepdims=True)
            + jnp.sum(gram_part, axis=-1, keepdims=True)
        )
        gram_grad = (beta * lower_grad).astype(jnp.bfloat16)
        pair_grad = (scores_grad * decay).astype(jnp.bfloat16)
        end_part = end_grad * key_end
        cross = beta * gram_part + scores_grad * scores
        end_dot = jnp.sum(end_part, axis=-1, keepdims=True)
        single = (
            (beta * growth) * key_dot
            + jnp.sum(gq_grad * gq, axis=-1, keepdims=True)
            - end_dot
        )
        last_grad = jnp.sum(end_dot, axis=0, keepdims=True) + finish * finish_grad
        cross_parts = parts(cross)
        above = mm(suffix, cross_parts[0]) + mm(suffix, cross_parts[1])
        single_parts = parts(jnp.broadcast_to(single, (BLOCK, 128)))
        single_sum = mm(suffix, single_parts[0]) + mm(suffix, single_parts[1])
        ld_grad = (
            jnp.sum(jnp.where(columns < rows, above, 0.0), axis=-1, keepdims=True)
            + single_sum[:, 0:1]
            + last_grad
        )
        query_grad = growth * gq_grad + mm(pair_grad, key_b)
        key_grad = (
            (beta * growth) * key_side
            + jnp.exp(last - cumul) * end_grad
            + mm(gram_grad, key_b)
            + mm(gram_grad, key_b, ATB)
            + mm(pair_grad, query, ATB)
        )
        value_grad = beta * value_side

        decay_total = decay_total + jnp.sum(ld_grad * ld, axis=0, keepdims=True)
        mix_grad_ref[span, 0:1] = beta_grad * beta * (1.0 - beta)
        mix_grad_ref[span, 1:2] = ld_grad * (-rate) * sigmoid(mix_ref[span, 1:2])

        query_scaled = query_grad * DK ** (-0.5)
        query_dot = jnp.sum(query_scaled * query_act, axis=-1, keepdims=True)
        query_back = query_norm * (query_scaled - query_act * (query_norm * query_norm * query_dot))
        key_sum = jnp.sum(key_grad * key_act, axis=-1, keepdims=True)
        key_back = key_norm * (key_grad - key_act * (key_norm * key_norm * key_sum))
        active_grad = jnp.concatenate([query_back, key_back, value_grad], axis=-1)
        mixed_grad = active_grad * gate * (1.0 + mixed * (1.0 - gate))
        for t in range(CONV):
            conv_total[t] = conv_total[t] + jnp.sum(mixed_grad * edged[t], axis=0, keepdims=True)
        longer = jnp.concatenate([mixed_grad, follow], 0)
        grad = longer[CONV - 1 : CONV - 1 + BLOCK] * taps_ref[0:1]
        for t in range(1, CONV):
            begin = CONV - 1 - t
            grad = grad + longer[begin : begin + BLOCK] * taps_ref[t : t + 1]
        proj_grad_ref[span, :channels] = grad.astype(jnp.bfloat16)
        if i == units - 1:
            tail_ref[...] = grad[BLOCK - 16 :]
        follow = mixed_grad[:8]
    first = jnp.concatenate([jnp.zeros((16, channels), jnp.float32), follow], 0)
    spill = first[CONV - 1 : CONV - 1 + 16] * taps_ref[0:1]
    for t in range(1, CONV):
        begin = CONV - 1 - t
        spill = spill + first[begin : begin + 16] * taps_ref[t : t + 1]
    edge_ref[...] = spill
    proj_grad_ref[:, channels:] = gate_grad_ref[...]
    small_ref[0:CONV] = jnp.concatenate(conv_total, 0)
    small_ref[CONV : CONV + 1] = jnp.broadcast_to(decay_total, (1, channels))


def delta_back(projected, halo, mix, mix_t, taps, decay_log, front, states, fresh, back, later, gate_grad):
    inv, solved, scores, gq, end, last, agg = front
    length = projected.shape[0]
    heads = taps.shape[0]
    channels = taps.shape[2]
    units = length // BLOCK
    f32, bf16 = jnp.float32, jnp.bfloat16
    shape = jax.ShapeDtypeStruct
    rate = jnp.broadcast_to(decay_log[:, None, None], (heads, 8, 128))
    span = channels + DV
    return local_call(back_terms_kernel, heads, "delta_back", 10)(
        [
            per_head(span, length),
            squeezed(16, channels),
            squeezed(length, 2),
            squeezed(2, length),
            squeezed(CONV, channels),
            squeezed(8, 128),
            per_head(BLOCK, length),
            per_head(DK + DV, length),
            per_head(BLOCK, length),
            per_head(DK, length),
            per_head(DK, length),
            squeezed(units, 128),
            squeezed(units, DK, DV),
            per_head(DV, length),
            per_head(DV, length),
            squeezed(DK, DV),
            per_head(DV, length),
        ],
        [
            (per_head(span, length), shape((length, heads * span), bf16)),
            (squeezed(16, channels), shape((heads, 16, channels), f32)),
            (squeezed(16, channels), shape((heads, 16, channels), f32)),
            (squeezed(length, 2), shape((heads, length, 2), f32)),
            (squeezed(8, channels), shape((heads, 8, channels), f32)),
        ],
        projected, halo, mix, mix_t, taps, rate, inv, solved, scores, gq, end, last, states, fresh,
        back, later, gate_grad,
    )


def ffn_kernel(
    tokens_ref, mixed_ref, gain_ref, up_w_ref, down_w_ref, grad_ref,
    hidden_ref, hidden_b_ref, swish_ref, gate_grad_ref, up_grad_ref, second_ref, gain_grad_ref,
):
    hidden = tokens_ref[...].astype(jnp.float32) + mixed_ref[...].astype(jnp.float32)
    hidden_ref[...] = hidden
    normed = hidden * lax.rsqrt(jnp.mean(hidden * hidden, axis=-1, keepdims=True) + EPSILON)
    hidden_b = (normed * gain_ref[...]).astype(jnp.bfloat16)
    hidden_b_ref[...] = hidden_b
    gate = mm(hidden_b, up_w_ref[0], ABT)
    up = mm(hidden_b, up_w_ref[1], ABT)
    act = mm(grad_ref[...], down_w_ref[...], ABT)
    sig = sigmoid(gate)
    silu = gate * sig
    swish_ref[...] = (silu * up).astype(jnp.bfloat16)
    gate_grad = (act * up * (sig * (1.0 + gate * (1.0 - sig)))).astype(jnp.bfloat16)
    up_grad = (act * silu).astype(jnp.bfloat16)
    gate_grad_ref[...] = gate_grad
    up_grad_ref[...] = up_grad
    second = mm(gate_grad, up_w_ref[0]) + mm(up_grad, up_w_ref[1])
    second_ref[...] = second.astype(jnp.bfloat16)
    total = jnp.sum(second * normed, axis=0, keepdims=True)
    gain_grad_ref[...] = jnp.broadcast_to(total, gain_grad_ref.shape)


def feed_forward(tokens, mixed, gain, up_w, down_w, grad_out):
    length, model = tokens.shape
    units = down_w.shape[0]
    steps = length // (2 * BLOCK)
    f32, bf16 = jnp.float32, jnp.bfloat16
    shape = jax.ShapeDtypeStruct

    def rows(width):
        return pl.BlockSpec((2 * BLOCK, width), lambda i: (i, 0))

    def whole(array):
        return pl.BlockSpec(array.shape, lambda i: (0,) * array.ndim)

    return pl.pallas_call(
        ffn_kernel,
        grid=(steps,),
        in_specs=[
            rows(model), rows(model), whole(gain[None]), whole(up_w), whole(down_w), rows(model),
        ],
        out_specs=[
            rows(model), rows(model), rows(units), rows(units), rows(units), rows(model),
            pl.BlockSpec((None, 8, model), lambda i: (i, 0, 0)),
        ],
        out_shape=[
            shape((length, model), f32),
            shape((length, model), bf16),
            shape((length, units), bf16),
            shape((length, units), bf16),
            shape((length, units), bf16),
            shape((length, model), bf16),
            shape((steps, 8, model), f32),
        ],
        compiler_params=pltpu.CompilerParams(vmem_limit_bytes=48 << 20),
        cost_estimate=cost(0),
        name="feed_forward",
    )(tokens, mixed, gain[None], up_w, down_w, grad_out)


def ffn_grads_kernel(hidden_ref, grad_ref, gate_ref, up_ref, swish_ref, out_ref):
    pieces, _, _, rows = out_ref.shape
    for j, (left, right) in enumerate(
        ((hidden_ref, gate_ref), (hidden_ref, up_ref), (grad_ref, swish_ref))
    ):
        value = mm(right[...], left[...], ATB).astype(jnp.bfloat16)
        for k in range(pieces):
            out_ref[k, j] = value[:, k * rows : (k + 1) * rows]


def ffn_grads(hidden_b, grad_out, gate_grad, up_grad, swish_b):
    length, model = hidden_b.shape
    units = swish_b.shape[1]
    count = lax.axis_size("seq")
    rows = model // count
    pieces = max(2 * BLOCK // rows, 1)
    part = rows * pieces
    columns = pl.BlockSpec((length, part), lambda i: (0, i))
    full = pl.BlockSpec((length, units), lambda i: (0, 0))
    return pl.pallas_call(
        ffn_grads_kernel,
        grid=(model // part,),
        in_specs=[columns, columns, full, full, full],
        out_specs=pl.BlockSpec((pieces, 3, units, rows), lambda i: (i, 0, 0, 0)),
        out_shape=jax.ShapeDtypeStruct((count, 3, units, rows), jnp.bfloat16),
        compiler_params=pltpu.CompilerParams(vmem_limit_bytes=48 << 20),
        cost_estimate=cost(0),
        name="ffn_grads",
    )(hidden_b, grad_out, gate_grad, up_grad, swish_b)


def early_kernel(normed_ref, gate_grad_ref, gated_ref, stream_ref, gate_ref, out_ref):
    count, rows, width = out_ref.shape
    gate_ref[...] = mm(normed_ref[...], gate_grad_ref[...], ATB).astype(jnp.bfloat16)
    heads = gated_ref.shape[1] // DV
    share = DV // count
    halves = stream_ref.shape[1] // width
    for h in range(heads):
        value = mm(gated_ref[:, h * DV : (h + 1) * DV], stream_ref[...], ATB).astype(jnp.bfloat16)
        for i in range(count):
            for j in range(halves):
                at = (h * halves + j) * share
                out_ref[i, at : at + share] = value[
                    i * share : (i + 1) * share, j * width : (j + 1) * width
                ]


def early_grads(normed_b, gate_grad, gated_b, stream_b):
    count = lax.axis_size("seq")
    model, width = stream_b.shape[1], gate_grad.shape[1]
    return pl.pallas_call(
        early_kernel,
        in_specs=[VMEM] * 4,
        out_specs=[VMEM] * 2,
        out_shape=[
            jax.ShapeDtypeStruct((model, width), jnp.bfloat16),
            jax.ShapeDtypeStruct((count, model // count, width), jnp.bfloat16),
        ],
        compiler_params=pltpu.CompilerParams(vmem_limit_bytes=40 << 20),
        cost_estimate=cost(0),
        name="early_grads",
    )(normed_b, gate_grad, gated_b, stream_b)


def rms_apply(values, gain):
    return values * lax.rsqrt(jnp.mean(values * values, axis=-1, keepdims=True) + EPSILON) * gain


def product(left, right, dims=((1,), (0,))):
    return lax.dot_general(left, right, (dims, ((), ())), preferred_element_type=jnp.float32)


def shards(
    block_input,
    norm1_gain,
    w_in,
    w_ba,
    conv_weight,
    decay_log,
    gnorm_gain,
    w_out,
    norm2_gain,
    w_up,
    w_down,
    grad_out,
):
    model = block_input.shape[1]
    heads = w_in.shape[1]
    span = w_in.shape[2]
    channels = conv_weight.shape[0]
    f32 = jnp.float32
    bf16 = jnp.bfloat16

    tail_rows = shifted(block_input[-16:], "seq", 1)
    tokens_wide = block_input.astype(f32)
    normed, pull_first = jax.vjp(rms_apply, tokens_wide, norm1_gain)
    normed_b = normed.astype(bf16)
    w_in_flat = w_in.reshape(model, heads * span)
    w_ba_flat = w_ba.reshape(model, 2 * heads)
    projected = product(normed_b, w_in_flat).astype(bf16)
    halo_normed = rms_apply(tail_rows.astype(f32), norm1_gain).astype(bf16)
    halo = product(halo_normed, w_in_flat).astype(bf16)
    halo = jnp.stack([halo[:, h * span : h * span + channels] for h in range(heads)])
    mixer_in = product(normed_b, w_ba_flat)
    mix = jnp.stack([mixer_in[:, h::heads] for h in range(heads)])
    mix_t = jnp.swapaxes(mix, 1, 2)
    taps = jnp.transpose(conv_weight, (1, 2, 0))
    front = delta_front(projected, halo, mix, mix_t, taps, decay_log)
    carried, maps = carried_forward(front[-1])
    layer_outputs, gated_b, states, fresh = delta_outer(front, carried, projected, gnorm_gain)
    w_out_flat = jnp.concatenate([w_out[:, h] for h in range(heads)], 0)
    mixed = head_sum(product(gated_b, w_out_flat))
    hidden, hidden_b, swish_b, gate_b, up_b, second_part, gain_second = feed_forward(
        block_input, mixed, norm2_gain, jnp.transpose(w_up, (1, 2, 0)), w_down.T, grad_out
    )
    ffn_parts = ffn_grads(hidden_b, grad_out, gate_b, up_b, swish_b)
    second_b, ffn_parts = lax.optimization_barrier((second_part, ffn_parts))
    ffn_share = lax.psum_scatter(ffn_parts, "seq", scatter_dimension=0, tiled=True)
    _, pull_second = jax.vjp(rms_apply, hidden, norm2_gain)
    second_total = head_sum(second_b).astype(f32)
    hidden_grad, _ = pull_second(second_total)
    gain_second = jnp.sum(gain_second[:, 0], 0)
    stream = grad_out.astype(f32) + hidden_grad
    stream_b = stream.astype(bf16)
    gated_grad = product(stream_b, w_out_flat, ((1,), (1,)))
    back, gate_grad, gain_gated, feed = delta_gate(
        gated_grad, layer_outputs, projected, gnorm_gain, front
    )
    gate_columns, out_rows = early_grads(normed_b, gate_grad, gated_b, stream_b)
    bits = powers(lax.axis_size("seq"))
    shares = [
        Share(gate_columns, bits),
        Share(out_rows.reshape(gate_columns.shape), bits[1:] + bits[:1]),
    ]
    feed = begin(shares, feed)
    ffn_part = product(swish_b, w_down, ((1,), (1,)))
    later, ffn_total = carried_back(feed, maps, ffn_part)
    result = hidden + ffn_total.astype(f32)
    later = proceed(shares, later)
    back_outs = delta_back(
        projected, halo, mix, mix_t, taps, decay_log, front, states, fresh, back, later, gate_grad
    )
    proj_grad, tail, edge, mix_grad, small_grad = proceed(shares, back_outs)
    back_edge = shifted(edge, "seq", -1)
    fixed = (tail + back_edge).astype(bf16)
    for h in range(heads):
        proj_grad = lax.dynamic_update_slice(
            proj_grad, fixed[h], (proj_grad.shape[0] - 16, h * span)
        )
    mixer_b = jnp.concatenate(
        [mix_grad[h, :, c : c + 1] for c in range(2) for h in range(heads)], 1
    ).astype(bf16)
    first_part = product(proj_grad, w_in_flat, ((1,), (1,)))
    first_part = first_part + product(mixer_b, w_ba_flat, ((1,), (1,)))
    qkv_grad = jnp.concatenate(
        [proj_grad[:, h * span : h * span + channels] for h in range(heads)], 1
    )
    in_weight_grad = product(normed_b, qkv_grad, ((0,), (0,))).astype(bf16)
    gate_weight_grad = product(mixer_b, normed_b, ((0,), (0,)))
    gain_first = pull_first(first_part)[1]
    first_part, ffn_share = lax.optimization_barrier((first_part.astype(bf16), ffn_share))
    while any(share.order for share in shares):
        first_part = proceed(shares, first_part)
    first_part = proceed(shares, first_part)
    gate_share, out_share = shares[0].blocks, shares[1].blocks
    input_grad, small, (in_share,) = final_sums(
        first_part,
        block_input,
        norm1_gain,
        stream,
        [gain_first, gain_second, jnp.sum(gain_gated[:, 0], 0)],
        [small_grad[:, CONV, 0], small_grad[:, :CONV], gate_weight_grad],
        [in_weight_grad],
    )
    ffn_share = ffn_share[0].astype(f32)
    up_share, down_share = jnp.transpose(ffn_share[:2], (2, 0, 1)), ffn_share[2].T
    gain_one, gain_two, gain_norm, decay_total, conv_total, gate_total = small
    in_share = jnp.stack(
        [
            jnp.concatenate(
                [
                    in_share[:, h * channels : (h + 1) * channels],
                    gate_share[:, h * DV : (h + 1) * DV],
                ],
                1,
            )
            for h in range(heads)
        ],
        1,
    )
    out_share = out_share.reshape(heads, -1, DV // lax.axis_size("seq"), heads * DV)
    out_share = jnp.transpose(out_share, (2, 0, 1, 3)).reshape((-1,) + w_out.shape[1:])
    count = lax.axis_size("seq")
    place = lax.axis_index("seq")

    def mine(whole, axis):
        share = whole.shape[axis] // count
        return lax.dynamic_slice_in_dim(whole, place * share, share, axis)

    return (
        result,
        input_grad,
        gain_one,
        in_share,
        mine(gate_total, 1).T.reshape(model // count, 2, heads),
        jnp.transpose(mine(conv_total, 2), (2, 0, 1)),
        decay_total,
        gain_norm,
        out_share,
        gain_two,
        up_share,
        down_share,
    )


def solution(mesh):
    return jax.shard_map(
        shards,
        mesh=mesh,
        in_specs=(
            P("seq", None),
            P(),
            P(None, "head", None),
            P(None, None, "head"),
            P(None, "head", None),
            P("head"),
            P(),
            P(None, "head", None),
            P(),
            P(None, None, "head"),
            P(None, "head"),
            P("seq", None),
        ),
        out_specs=(
            P("seq", None),
            P("seq", None),
            P(),
            P("seq", "head", None),
            P("seq", None, "head"),
            P("seq", "head", None),
            P("head"),
            P(),
            P("seq", "head", None),
            P(),
            P("seq", None, "head"),
            P("seq", "head"),
        ),
        check_vma=False,
    )
```

```python
import functools

import jax
import jax.numpy as jnp
from jax import lax
from jax.experimental import pallas as pl
from jax.experimental.pallas import tpu as pltpu
from jax.sharding import PartitionSpec as P

DK = 128
DV = 256
CONV = 4
STRETCH = 64


EPSILON = 1e-06
NEGATIVE = -1e30


def shifted(block, axis, distance):
    devices = range(lax.axis_size(axis))
    route = [(i - distance, i) for i in devices if i - distance in devices]
    return lax.ppermute(block, axis, route)


MESH = pl.DeviceIdType.MESH
PIECES = 8


def flipped(index, bit):
    mine = (index // bit) % 2
    return index + bit - 2 * bit * mine, mine


def powers(count):
    return [2**i for i in range(count.bit_length() - 1)]


def remote(src, dst, send_sem, recv_sem, axis, device):
    return pltpu.make_async_remote_copy(
        src_ref=src,
        dst_ref=dst,
        send_sem=send_sem,
        recv_sem=recv_sem,
        device_id={axis: device},
        device_id_type=MESH,
    )


def greet(partners):
    barrier = pltpu.get_barrier_semaphore()
    for axis, partner in partners:
        pl.semaphore_signal(barrier, inc=1, device_id={axis: partner}, device_id_type=MESH)
    pl.semaphore_wait(barrier, len(partners))


def together(tasks, paces=None):
    live = [(task, pace) for task, pace in zip(tasks, paces or [1] * len(tasks))]
    while live:
        for entry in list(live):
            task, pace = entry
            try:
                for _ in range(pace):
                    next(task)
            except StopIteration:
                live.remove(entry)


def bit_partners(axis, count):
    me = lax.axis_index(axis)
    return [(axis, flipped(me, bit)[0]) for bit in powers(count)]


def head_sum_scratch(count, whole):
    piece = whole[2:]
    steps = len(powers(count)) - 1
    dma = pltpu.SemaphoreType.DMA
    return [
        pltpu.VMEM((PIECES,) + piece, jnp.bfloat16),
        pltpu.VMEM((steps, PIECES) + piece, jnp.bfloat16),
        pltpu.VMEM((steps, PIECES) + piece, jnp.bfloat16),
        dma((PIECES,)),
        dma((PIECES,)),
        dma((steps, PIECES)),
        dma((steps, PIECES)),
        dma((PIECES,)),
        dma((PIECES,)),
    ]


def head_sum_task(count, x_ref, out_ref, scratch):
    first, held, sums, near_s, near_r, far_s, far_r, back_s, back_r = scratch
    me = lax.axis_index("head")
    bits = powers(count)
    partner, side = flipped(me, 1)
    peers = [flipped(me, bit)[0] for bit in bits[1:]]

    def send(src, dst, send_sem, recv_sem, device):
        copy = remote(src, dst, send_sem, recv_sem, "head", device)
        copy.start()
        return copy

    def add(left, right):
        return (left.astype(jnp.float32) + right.astype(jnp.float32)).astype(jnp.bfloat16)

    near = [
        send(x_ref.at[1 - side, k], first.at[k], near_s.at[k], near_r.at[k], partner)
        for k in range(PIECES)
    ]
    yield
    steps = len(peers)
    copies = []
    for k in range(PIECES):
        near[k].wait()
        sums[0, k] = add(x_ref[side, k], first[k])
        copies.append(
            send(sums.at[0, k], held.at[0, k], far_s.at[0, k], far_r.at[0, k], peers[0])
        )
    yield
    for step in range(steps):
        later = []
        for k in range(PIECES):
            copies[k].wait()
            total = add(sums[step, k], held[step, k])
            if step < steps - 1:
                sums[step + 1, k] = total
                later.append(
                    send(
                        sums.at[step + 1, k],
                        held.at[step + 1, k],
                        far_s.at[step + 1, k],
                        far_r.at[step + 1, k],
                        peers[step + 1],
                    )
                )
            else:
                out_ref[side, k] = total
                later.append(
                    send(
                        out_ref.at[side, k],
                        out_ref.at[side, k],
                        back_s.at[k],
                        back_r.at[k],
                        partner,
                    )
                )
            yield
        copies = later
    for copy in copies:
        copy.wait()


def head_whole(shape):
    rows, width = shape
    return (2, PIECES, rows // (2 * PIECES), width)


def head_sum_kernel(count, x_ref, out_ref, *scratch):
    greet(bit_partners("head", count))
    together([head_sum_task(count, x_ref, out_ref, scratch)])


VMEM = pl.BlockSpec(memory_space=pltpu.VMEM)


def head_sum(part):
    count = lax.axis_size("head")
    whole = head_whole(part.shape)
    total = pl.pallas_call(
        functools.partial(head_sum_kernel, count),
        out_shape=jax.ShapeDtypeStruct(whole, jnp.bfloat16),
        in_specs=[VMEM],
        out_specs=VMEM,
        scratch_shapes=head_sum_scratch(count, whole),
        compiler_params=pltpu.CompilerParams(
            collective_id=0, has_side_effects=True, vmem_limit_bytes=16 << 20
        ),
        cost_estimate=cost(0),
        name="head_sum",
    )(part.astype(jnp.bfloat16).reshape(whole))
    return total.reshape(part.shape)


def gather_scratch(count):
    dma = pltpu.SemaphoreType.DMA
    line = max(count // 2, 1)
    return [dma((line,)), dma((line,)), dma((line,)), dma((line,)), dma((2 * line,)), dma((2 * line,))]


def line_partners(count):
    me = lax.axis_index("seq")
    up, down = lax.rem(me + 2, count), lax.rem(me + count - 2, count)
    return [("seq", flipped(me, 1)[0]), ("seq", up), ("seq", down)]


def gather_task(count, out_ref, scratch):
    up_s, up_r, dn_s, dn_r, x_s, x_r = scratch
    me = lax.axis_index("seq")
    line = count // 2
    place, half = me // 2, lax.rem(me, 2)
    other, _ = flipped(me, 1)

    def hop(position, send_sem, recv_sem, device):
        block = out_ref.at[2 * position + half]
        return remote(block, block, send_sem, recv_sem, "seq", device)

    def up(step):
        return hop(place - (step - 1), up_s.at[step], up_r.at[step], me + 2)

    def down(step):
        return hop(place + (step - 1), dn_s.at[step], dn_r.at[step], me - 2)

    def came_up(step):
        return hop(place - step, up_s.at[step], up_r.at[step], me - 2)

    def came_down(step):
        return hop(place + step, dn_s.at[step], dn_r.at[step], me + 2)

    def across(number, position):
        return hop(position, x_s.at[number], x_r.at[number], other)

    def from_across(number, position):
        block = out_ref.at[2 * position + 1 - half]
        return remote(block, block, x_s.at[number], x_r.at[number], "seq", other)

    def sends_up(step):
        return (place + 1 < line) & (place - (step - 1) >= 0)

    def sends_down(step):
        return (place - 1 >= 0) & (place + (step - 1) < line)

    for step in range(1, line):
        if step > 1:
            @pl.when(place - (step - 1) >= 0)
            def _():
                came_up(step - 1).wait_recv()

        @pl.when(sends_up(step))
        def _():
            up(step).start()

        if step > 1:

            @pl.when(place + (step - 1) < line)
            def _():
                came_down(step - 1).wait_recv()

        @pl.when(sends_down(step))
        def _():
            down(step).start()

        if step == 1:
            across(0, place).start()
        else:

            @pl.when(place - (step - 1) >= 0)
            def _():
                across(2 * step - 3, place - (step - 1)).start()

            @pl.when(place + (step - 1) < line)
            def _():
                across(2 * step - 2, place + (step - 1)).start()

        yield
    last = line - 1

    @pl.when(place - last >= 0)
    def _():
        came_up(last).wait_recv()
        across(2 * last - 1, place - last).start()

    @pl.when(place + last < line)
    def _():
        came_down(last).wait_recv()
        across(2 * last, place + last).start()

    yield
    for step in range(1, line):

        @pl.when(sends_up(step))
        def _():
            up(step).wait_send()

        @pl.when(sends_down(step))
        def _():
            down(step).wait_send()

    across(0, place).wait_send()
    from_across(0, place).wait_recv()
    for step in range(1, line):

        @pl.when(place - step >= 0)
        def _():
            across(2 * step - 1, place - step).wait_send()
            from_across(2 * step - 1, place - step).wait_recv()

        @pl.when(place + step < line)
        def _():
            across(2 * step, place + step).wait_send()
            from_across(2 * step, place + step).wait_recv()


def carry_kernel(count, heads, x_ref, state_ref, all_ref, *scratch):
    me = lax.axis_index("seq")
    greet(line_partners(count))
    all_ref[me] = x_ref[...]
    together([gather_task(count, all_ref, scratch)])
    for h in range(heads):
        state = all_ref[0, h, :, DK:].astype(jnp.float32)
        state = jnp.where(me > 0, state, jnp.zeros_like(state))
        for source in range(1, count - 1):
            moved = jnp.dot(
                all_ref[source, h, :, :DK],
                state.astype(jnp.bfloat16),
                preferred_element_type=jnp.float32,
            ) + all_ref[source, h, :, DK:].astype(jnp.float32)
            state = jnp.where(source < me, moved, state)
        state_ref[h] = state


def carried_forward(part):
    count = lax.axis_size("seq")
    heads = part.shape[0]
    return pl.pallas_call(
        functools.partial(carry_kernel, count, heads),
        out_shape=[
            jax.ShapeDtypeStruct((heads, DK, DV), jnp.float32),
            jax.ShapeDtypeStruct((count,) + part.shape, jnp.bfloat16),
        ],
        in_specs=[VMEM],
        out_specs=[VMEM, VMEM],
        scratch_shapes=gather_scratch(count),
        compiler_params=pltpu.CompilerParams(
            collective_id=1, has_side_effects=True, vmem_limit_bytes=24 << 20
        ),
        cost_estimate=cost(0),
        name="carry_forward",
    )(part.astype(jnp.bfloat16))


def back_kernel(count, ranks, heads, x_ref, maps_ref, part_ref, state_ref, total_ref, all_ref, *scratch):
    me = lax.axis_index("seq")
    n = len(gather_scratch(count))
    greet(line_partners(count) + bit_partners("head", ranks))
    all_ref[me] = x_ref[...]
    gather = gather_task(count, all_ref, scratch[:n])
    total = head_sum_task(ranks, part_ref, total_ref, scratch[n:])
    next(gather)
    next(total)
    next(total)
    together([gather, total])
    for h in range(heads):
        state = all_ref[count - 1, h].astype(jnp.float32)
        state = jnp.where(me < count - 1, state, jnp.zeros_like(state))
        for source in range(count - 2, 0, -1):
            moved = lax.dot_general(
                maps_ref[source, h, :, :DK],
                state.astype(jnp.bfloat16),
                (((0,), (0,)), ((), ())),
                preferred_element_type=jnp.float32,
            ) + all_ref[source, h].astype(jnp.float32)
            state = jnp.where(source > me, moved, state)
        state_ref[h] = state


def carried_back(feed, maps, part):
    count = lax.axis_size("seq")
    ranks = lax.axis_size("head")
    heads = feed.shape[0]
    whole = head_whole(part.shape)
    state, total = pl.pallas_call(
        functools.partial(back_kernel, count, ranks, heads),
        out_shape=[
            jax.ShapeDtypeStruct((heads, DK, DV), jnp.float32),
            jax.ShapeDtypeStruct(whole, jnp.bfloat16),
        ],
        in_specs=[VMEM] * 3,
        out_specs=[VMEM] * 2,
        scratch_shapes=[pltpu.VMEM((count,) + feed.shape, jnp.bfloat16)]
        + gather_scratch(count)
        + head_sum_scratch(ranks, whole),
        compiler_params=pltpu.CompilerParams(
            collective_id=2, has_side_effects=True, vmem_limit_bytes=32 << 20
        ),
        cost_estimate=cost(0),
        name="carry_back",
    )(feed.astype(jnp.bfloat16), maps, part.astype(jnp.bfloat16).reshape(whole))
    return state, total.reshape(part.shape)


def share_works(count, shapes):
    bits = powers(count)
    works = []
    for a, (_, rows, width) in enumerate(shapes):
        half = rows // 2
        works.append((a, pl.ds(0, half), bits, (half, width)))
        works.append((a, pl.ds(half, half), bits[1:] + bits[:1], (half, width)))
    return works


def share_scratch(count, shapes):
    steps = len(powers(count))
    works = share_works(count, shapes)
    dma = pltpu.SemaphoreType.DMA
    return (
        [pltpu.VMEM((steps, count // 2) + work[3], jnp.bfloat16) for work in works]
        + [pltpu.VMEM((max(steps - 1, 1), count // 4) + work[3], jnp.bfloat16) for work in works]
        + [dma((len(works), steps, count // 2)), dma((len(works), steps, count // 2))]
    )


def share_task(count, x_refs, out_refs, scratch):
    works = share_works(count, [x.shape for x in x_refs])
    recv_refs, send_refs = scratch[: len(works)], scratch[len(works) : 2 * len(works)]
    send_sem, recv_sem = scratch[2 * len(works) :]
    me = lax.axis_index("seq")
    bits = powers(count)
    partners = {bit: flipped(me, bit)[0] for bit in bits}

    def block(relative):
        index = me
        for bit in bits:
            if relative & bit:
                index = flipped(index, bit)[0]
        return index

    def kept(order, step):
        used = sum(order[:step])
        return [r for r in range(count) if r & used == 0]

    def slot(order, step, relative):
        return kept(order, step + 1).index(relative)

    def partial_sum(number, relative, step):
        a, rows, order, _ = works[number]
        total = x_refs[a][block(relative), rows, :].astype(jnp.float32)
        for earlier in range(step):
            total = total + recv_refs[number][earlier, slot(order, earlier, relative)].astype(
                jnp.float32
            )
        return total

    pending = {}
    for step in range(len(bits) + 1):
        for number, (a, rows, order, _) in enumerate(works):
            for copy in pending.pop(number, []):
                copy.wait()
            if step == len(bits):
                out_refs[a][rows, :] = partial_sum(number, 0, step)
                continue
            bit = order[step]
            started = []
            for relative in kept(order, step):
                if not relative & bit:
                    continue
                place = slot(order, step, relative - bit)
                if step == 0:
                    source = x_refs[a].at[block(relative), rows, :]
                else:
                    send_refs[number][step - 1, place] = partial_sum(
                        number, relative, step
                    ).astype(jnp.bfloat16)
                    source = send_refs[number].at[step - 1, place]
                copy = remote(
                    source,
                    recv_refs[number].at[step, place],
                    send_sem.at[number, step, place],
                    recv_sem.at[number, step, place],
                    "seq",
                    partners[bit],
                )
                copy.start()
                started.append(copy)
            pending[number] = started
        yield


def small_scratch(count, ranks, rows, both):
    dma = pltpu.SemaphoreType.DMA
    near, far = len(powers(ranks)), len(powers(count))
    return [
        pltpu.VMEM((near, both, 128), jnp.float32),
        pltpu.VMEM((far, rows, 128), jnp.float32),
        pltpu.VMEM((near, both, 128), jnp.float32),
        pltpu.VMEM((far, rows, 128), jnp.float32),
        dma((near,)),
        dma((near,)),
        dma((far,)),
        dma((far,)),
    ]


def small_task(count, ranks, both, x_ref, out_ref, scratch):
    got_h, got_s, sent_h, sent_s, hs, hr, ss, sr = scratch
    total = x_ref[:both]
    for i, (axis, partner) in enumerate(bit_partners("head", ranks)):
        sent_h[i] = total
        copy = remote(sent_h.at[i], got_h.at[i], hs.at[i], hr.at[i], axis, partner)
        copy.start()
        yield
        copy.wait()
        total = sent_h[i] + got_h[i]
    for i, (axis, partner) in enumerate(bit_partners("seq", count)):
        if i == 0:
            sent_s[0, :both] = total
            sent_s[0, both:] = x_ref[both:]
        else:
            sent_s[i] = sent_s[i - 1] + got_s[i - 1]
        copy = remote(sent_s.at[i], got_s.at[i], ss.at[i], sr.at[i], axis, partner)
        copy.start()
        yield
        copy.wait()
    last = len(powers(count)) - 1
    out_ref[...] = sent_s[last] + got_s[last]


def input_task(before, total_ref, tokens_ref, gain_ref, stream_ref, grad_ref):
    yield from before
    for side in range(total_ref.shape[0]):
        for k in range(total_ref.shape[1]):
            tokens = tokens_ref[side, k].astype(jnp.float32)
            scale = lax.rsqrt(jnp.mean(tokens * tokens, axis=-1, keepdims=True) + EPSILON)
            normed = tokens * scale
            wide = total_ref[side, k].astype(jnp.float32) * gain_ref[...]
            along = jnp.mean(wide * normed, axis=-1, keepdims=True)
            grad_ref[side, k] = stream_ref[side, k] + scale * (wide - normed * along)
        yield


def final_kernel(count, ranks, both, arrays, *refs):
    part_ref, small_ref, tokens_ref, gain_ref, stream_ref, *x_refs = refs[: arrays + 5]
    grad_ref, sum_ref, *out_refs = refs[arrays + 5 : 2 * arrays + 7]
    total_ref, *scratch = refs[2 * arrays + 7 :]
    n = len(head_sum_scratch(ranks, (1, 1, 8, 128)))
    m = 8
    greet(bit_partners("seq", count) + bit_partners("head", ranks))
    shares = share_task(count, x_refs, out_refs, scratch[n + m :])
    tokens = input_task(
        head_sum_task(ranks, part_ref, total_ref, scratch[:n]),
        total_ref, tokens_ref, gain_ref, stream_ref, grad_ref,
    )
    small = small_task(count, ranks, both, small_ref, sum_ref, scratch[n : n + m])
    next(tokens)
    next(shares)
    next(small)
    next(tokens)
    next(small)
    together([shares, tokens, small], [1, PIECES + 1, 2])


def final_sums(part, tokens, gain, stream, wide, narrow, grads):
    count = lax.axis_size("seq")
    ranks = lax.axis_size("head")
    whole = head_whole(part.shape)

    def padded(flat):
        size = -(-flat.shape[0] // 1024) * 1024
        return jnp.pad(flat, (0, size - flat.shape[0])).reshape(size // 128, 128)

    wide_flat = padded(jnp.concatenate([a.reshape(-1) for a in wide]))
    narrow_flat = padded(jnp.concatenate([a.reshape(-1) for a in narrow]))
    both = wide_flat.shape[0]
    small = jnp.concatenate([wide_flat, narrow_flat])
    blocks = [
        g.astype(jnp.bfloat16).reshape(count, g.shape[0] // count, g.shape[1]) for g in grads
    ]
    total, summed, *shares = pl.pallas_call(
        functools.partial(final_kernel, count, ranks, both, len(grads)),
        out_shape=[
            jax.ShapeDtypeStruct(whole, jnp.float32),
            jax.ShapeDtypeStruct(small.shape, jnp.float32),
        ]
        + [jax.ShapeDtypeStruct(b.shape[1:], jnp.float32) for b in blocks],
        in_specs=[VMEM] * (len(grads) + 5),
        out_specs=[VMEM] * (len(grads) + 2),
        scratch_shapes=[pltpu.VMEM(whole, jnp.bfloat16)]
        + head_sum_scratch(ranks, whole)
        + small_scratch(count, ranks, small.shape[0], both)
        + share_scratch(count, [b.shape for b in blocks]),
        compiler_params=pltpu.CompilerParams(
            collective_id=3, has_side_effects=True, vmem_limit_bytes=56 << 20
        ),
        cost_estimate=cost(0),
        name="final_sums",
    )(
        part.astype(jnp.bfloat16).reshape(whole),
        small,
        tokens.reshape(whole),
        gain[None],
        stream.reshape(whole),
        *blocks,
    )
    outs = []
    for flat, group in ((summed[:both].reshape(-1), wide), (summed[both:].reshape(-1), narrow)):
        at = 0
        for a in group:
            outs.append(flat[at : at + a.size].reshape(a.shape))
            at += a.size
    return total.reshape(part.shape), outs, shares


class Share:
    def __init__(self, grad, order):
        count = lax.axis_size("seq")
        self.bits = powers(count)[::-1]
        self.order = list(order)
        self.count = count
        rows = grad.shape[0] // count
        self.blocks = grad.astype(jnp.bfloat16).reshape((2,) * len(self.bits) + (rows, -1))

    def cut(self):
        bit = self.order[0]
        axis = self.bits.index(bit)
        mine = lax.rem(lax.axis_index("seq") // bit, 2)
        self.keep = lax.dynamic_index_in_dim(self.blocks, mine, axis, False)
        self.send = lax.dynamic_index_in_dim(self.blocks, 1 - mine, axis, False)

    def start(self):
        bit = self.order.pop(0)
        self.bits.remove(bit)
        route = [(i, i ^ bit) for i in range(self.count)]
        self.got = lax.ppermute(self.send, "seq", route)

    def add(self):
        total = self.keep.astype(jnp.float32) + self.got.astype(jnp.float32)
        self.blocks = total if not self.order else total.astype(jnp.bfloat16)


def begin(shares, beside):
    for share in shares:
        share.cut()
    beside, sends = lax.optimization_barrier((beside, [share.send for share in shares]))
    for share, send in zip(shares, sends):
        share.send = send
        share.start()
    return beside


def proceed(shares, beside):
    beside, got = lax.optimization_barrier((beside, [share.got for share in shares]))
    for share, g in zip(shares, got):
        share.got = g
        share.add()
    left = [share for share in shares if share.order]
    return begin(left, beside) if left else beside


BLOCK = 128


def mm(left, right, dims=((1,), (0,))):
    return lax.dot_general(
        left.astype(jnp.bfloat16),
        right.astype(jnp.bfloat16),
        (dims, ((), ())),
        preferred_element_type=jnp.float32,
    )


AB = ((1,), (0,))
ABT = ((1,), (1,))
ATB = ((0,), (0,))


def parts(x):
    high = x.astype(jnp.bfloat16)
    return high, (x - high.astype(jnp.float32)).astype(jnp.bfloat16)


def fine_parts(left, right, dims=AB):
    lh, ll = left
    rh, rl = right
    return mm(lh, rh, dims) + (mm(lh, rl, dims) + mm(ll, rh, dims))


def fine(left, right, dims=AB):
    return fine_parts(parts(left), parts(right), dims)


def places(width):
    rows = lax.broadcasted_iota(jnp.int32, (width, width), 0)
    columns = lax.broadcasted_iota(jnp.int32, (width, width), 1)
    return rows, columns


def sigmoid(x):
    return 1.0 / (1.0 + jnp.exp(-x))


def softplus(x):
    return jnp.maximum(x, 0.0) + jnp.log1p(jnp.exp(-jnp.abs(x)))


def conv_rows(proj_ref, halo_ref, i):
    channels = halo_ref.shape[1]
    main = proj_ref[i * BLOCK : (i + 1) * BLOCK, :channels].astype(jnp.float32)
    if i == 0:
        ahead = halo_ref[...].astype(jnp.float32)
    else:
        ahead = proj_ref[i * BLOCK - 16 : i * BLOCK, :channels].astype(jnp.float32)
    rows = jnp.concatenate([ahead, main], 0)
    start = rows.shape[0] - BLOCK - (CONV - 1)
    return [rows[start + t : start + t + BLOCK] for t in range(CONV)]


def mixing(rows, taps_ref):
    mixed = rows[0] * taps_ref[0:1]
    for t in range(1, CONV):
        mixed = mixed + rows[t] * taps_ref[t : t + 1]
    return mixed


def unit_features(rows, taps_ref):
    mixed = mixing(rows, taps_ref)
    gate = sigmoid(mixed)
    active = mixed * gate
    query, key, value = active[:, :DK], active[:, DK : 2 * DK], active[:, 2 * DK :]
    query_norm = lax.rsqrt(jnp.sum(query * query, axis=-1, keepdims=True) + EPSILON)
    key_norm = lax.rsqrt(jnp.sum(key * key, axis=-1, keepdims=True) + EPSILON)
    return mixed, gate, active, query_norm, key_norm


def unit_decays(mix_ref, mix_t_ref, rate, i):
    span = slice(i * BLOCK, (i + 1) * BLOCK)
    beta = sigmoid(mix_ref[span, 0:1])
    ld_column = -rate * softplus(mix_ref[span, 1:2])
    ld_row = -rate * softplus(mix_t_ref[1:2, span])
    rows, columns = places(BLOCK)
    cumul = jnp.sum(jnp.where(rows >= columns, ld_row, 0.0), axis=1, keepdims=True)
    cumul_row = jnp.sum(jnp.where(rows <= columns, ld_column, 0.0), axis=0, keepdims=True)
    last = jnp.sum(ld_row, axis=1, keepdims=True)
    decay = jnp.exp(jnp.where(rows >= columns, cumul - cumul_row, NEGATIVE))
    return beta, ld_column, cumul, last, decay


def inverse_all(lowers):
    width = lowers[0].shape[0]
    rows, columns = places(width)

    def pairs(size):
        return (rows // size == columns // size + 1) & ((rows // size) % 2 == 1)

    eye = (rows == columns).astype(jnp.float32)
    inverses = [eye - jnp.where(pairs(1), lower, 0.0) for lower in lowers]
    size = 2
    while size < width:
        mask = pairs(size)
        cut = [parts(jnp.where(mask, lower, 0.0)) for lower in lowers]
        held = [parts(inverse) for inverse in inverses]
        middle = [fine_parts(a, b) for a, b in zip(held, cut)]
        inverses = [
            inverse - fine_parts(parts(m), a) for inverse, m, a in zip(inverses, middle, held)
        ]
        size *= 2
    return inverses


def front_kernel(
    tokens_ref, tail_ref, gain_ref, w_ref, w_ba_ref, w_ba_t_ref, taps_ref, rate_ref,
    normed_ref, proj_ref, halo_ref, mix_ref, mix_t_ref, inv_ref, solved_ref, scores_ref, gq_ref, end_ref, last_ref, agg_ref,
):
    def normed_of(ref):
        wide = ref[...].astype(jnp.float32)
        scale = lax.rsqrt(jnp.mean(wide * wide, axis=-1, keepdims=True) + EPSILON)
        return (wide * scale * gain_ref[...]).astype(jnp.bfloat16)

    @pl.when(pl.program_id(0) == 0)
    def _():
        normed_ref[...] = normed_of(tokens_ref)

    normed = normed_ref[...]
    proj_ref[...] = mm(normed, w_ref[...]).astype(jnp.bfloat16)
    halo = mm(normed_of(tail_ref), w_ref[:, : halo_ref.shape[1]])
    halo_ref[...] = halo.astype(jnp.bfloat16)
    mix_ref[...] = mm(normed, w_ba_ref[...])
    mix_t_ref[...] = mm(w_ba_t_ref[...], normed, ABT)
    units = proj_ref.shape[0] // BLOCK
    rows, columns = places(BLOCK)
    strictly = rows > columns
    rate = jnp.exp(rate_ref[0:1, 0:1])
    kept = []
    for i in range(units):
        _, _, active, query_norm, key_norm = unit_features(
            conv_rows(proj_ref, halo_ref, i), taps_ref
        )
        query = active[:, :DK] * query_norm * DK ** (-0.5)
        key = active[:, DK : 2 * DK] * key_norm
        beta, _, cumul, last, decay = unit_decays(mix_ref, mix_t_ref, rate, i)
        split = parts(key)
        gram = fine_parts(split, split, ABT)
        lower = jnp.where(strictly, beta * decay * gram, 0.0)
        growth = jnp.exp(cumul)
        scores = decay * mm(query, key, ABT)
        span = slice(i * BLOCK, (i + 1) * BLOCK)
        scores_ref[span] = scores
        gq_ref[span] = growth * query
        key_end = jnp.exp(last - cumul) * key
        end_ref[span] = key_end
        sides = jnp.concatenate([(beta * growth) * key, beta * active[:, 2 * DK :]], axis=-1)
        finish = jnp.exp(last)
        last_ref[i : i + 1] = jnp.broadcast_to(finish, (1, 128))
        kept.append((lower, sides.astype(jnp.bfloat16), key_end, finish))
    inverses = inverse_all([unit[0] for unit in kept])
    total = None
    for i in range(units):
        span = slice(i * BLOCK, (i + 1) * BLOCK)
        _, sides, key_end, finish = kept[i]
        inverse = inverses[i].astype(jnp.bfloat16)
        inv_ref[span] = inverse
        solved = mm(inverse, sides)
        solved_ref[span] = solved
        if total is None:
            fresh = jnp.concatenate([-solved[:, :DK], solved[:, DK:]], axis=-1)
            eye = (rows == columns).astype(jnp.float32)
            base = jnp.concatenate([finish * eye, jnp.zeros((DK, DV), jnp.float32)], axis=-1)
        else:
            moved = fine(solved[:, :DK], total)
            fresh = jnp.concatenate([-moved[:, :DK], solved[:, DK:] - moved[:, DK:]], axis=-1)
            base = finish * total
        total = base + fine(key_end, fresh, ATB)
    agg_ref[0] = total.astype(jnp.bfloat16)


def per_head(width, rows):
    return pl.BlockSpec((rows, width), lambda h: (0, h))


def stacked(*shape):
    return pl.BlockSpec((1,) + shape, lambda h: (h,) + (0,) * len(shape))


def squeezed(*shape):
    return pl.BlockSpec((None,) + shape, lambda h: (h,) + (0,) * len(shape))


def cost(micros):
    return pl.CostEstimate(flops=int(micros * 1e9), bytes_accessed=1 << 20, transcendentals=0)


def local_call(kernel, heads, name, micros):
    def call(ins, outs, *arrays):
        return pl.pallas_call(
            kernel,
            grid=(heads,),
            in_specs=ins,
            out_specs=[spec for spec, _ in outs],
            out_shape=[shape for _, shape in outs],
            compiler_params=pltpu.CompilerParams(vmem_limit_bytes=48 << 20),
            cost_estimate=cost(micros),
            name=name,
        )(*arrays)

    return call


def delta_front(tokens, tail, gain, w_in_flat, w_ba, taps, decay_log):
    length, model = tokens.shape
    heads = taps.shape[0]
    channels = taps.shape[2]
    f32, bf16 = jnp.float32, jnp.bfloat16
    units = length // BLOCK
    shape = jax.ShapeDtypeStruct

    def side(width, kind):
        return per_head(width, length), shape((length, heads * width), kind)

    rate = jnp.broadcast_to(decay_log[:, None, None], (heads, 8, 128))
    span = channels + DV
    alone = pl.BlockSpec((length, model), lambda h: (0, 0))
    return local_call(front_kernel, heads, "delta_front", 0)(
        [
            alone,
            pl.BlockSpec(tail.shape, lambda h: (0, 0)),
            pl.BlockSpec((1, model), lambda h: (0, 0)),
            per_head(span, model),
            squeezed(model, 2),
            squeezed(2, model),
            squeezed(CONV, channels),
            squeezed(8, 128),
        ],
        [
            (alone, shape((length, model), bf16)),
            side(span, bf16),
            (squeezed(16, channels), shape((heads, 16, channels), bf16)),
            (squeezed(length, 2), shape((heads, length, 2), f32)),
            (squeezed(2, length), shape((heads, 2, length), f32)),
            side(BLOCK, bf16),
            side(DK + DV, f32),
            side(BLOCK, f32),
            side(DK, f32),
            side(DK, f32),
            (squeezed(units, 128), shape((heads, units, 128), f32)),
            (stacked(DK, DK + DV), shape((heads, DK, DK + DV), bf16)),
        ],
        tokens, tail, gain[None], w_in_flat, jnp.transpose(w_ba, (2, 0, 1)),
        jnp.transpose(w_ba, (2, 1, 0)), taps, rate,
    )


def outer_kernel(
    solved_ref, scores_ref, gq_ref, end_ref, last_ref, carried_ref, proj_ref, gain_ref,
    out_ref, gated_ref, state_ref, fresh_ref,
):
    units = solved_ref.shape[0] // BLOCK
    state = carried_ref[...]
    for i in range(units):
        span = slice(i * BLOCK, (i + 1) * BLOCK)
        narrow = state.astype(jnp.bfloat16)
        state_ref[i] = state
        fresh = solved_ref[span, DK:] - mm(solved_ref[span, :DK], narrow)
        fresh = fresh.astype(jnp.bfloat16)
        fresh_ref[span] = fresh
        out = mm(gq_ref[span], narrow) + mm(scores_ref[span], fresh)
        if i < units - 1:
            state = last_ref[i : i + 1, 0:1] * state + mm(end_ref[span], fresh, ATB)
        out_ref[span] = out
        gate = proj_ref[span, 2 * DK + DV :].astype(jnp.float32)
        normed = out * lax.rsqrt(jnp.mean(out * out, axis=-1, keepdims=True) + EPSILON)
        gated_ref[span] = (normed * gain_ref[...] * (gate * sigmoid(gate))).astype(jnp.bfloat16)


def delta_outer(front, carried, projected, gnorm_gain):
    inv, solved, scores, gq, end, last, agg = front
    length = solved.shape[0]
    heads = carried.shape[0]
    units = length // BLOCK
    f32, bf16 = jnp.float32, jnp.bfloat16
    shape = jax.ShapeDtypeStruct
    return local_call(outer_kernel, heads, "delta_outer", 0)(
        [
            per_head(DK + DV, length),
            per_head(BLOCK, length),
            per_head(DK, length),
            per_head(DK, length),
            squeezed(units, 128),
            squeezed(DK, DV),
            per_head(projected.shape[1] // heads, length),
            pl.BlockSpec((1, DV), lambda h: (0, 0)),
        ],
        [
            (per_head(DV, length), shape((length, heads * DV), f32)),
            (per_head(DV, length), shape((length, heads * DV), bf16)),
            (squeezed(units, DK, DV), shape((heads, units, DK, DV), f32)),
            (per_head(DV, length), shape((length, heads * DV), bf16)),
        ],
        solved, scores, gq, end, last, carried, projected, gnorm_gain[None],
    )


def gate_kernel(
    grad_ref, out_ref, proj_ref, gain_ref, solved_ref, scores_ref, gq_ref, end_ref, last_ref,
    back_ref, gate_grad_ref, gain_grad_ref, feed_ref,
):
    units = solved_ref.shape[0] // BLOCK
    gain = gain_ref[...]
    total = jnp.zeros((1, DV), jnp.float32)
    later = None
    for i in reversed(range(units)):
        span = slice(i * BLOCK, (i + 1) * BLOCK)
        gate = proj_ref[span, 2 * DK + DV :].astype(jnp.float32)
        out = out_ref[span]
        grad = grad_ref[span]
        scale = lax.rsqrt(jnp.mean(out * out, axis=-1, keepdims=True) + EPSILON)
        normed = out * scale
        sig = sigmoid(gate)
        silu = gate * sig
        gate_grad = grad * (normed * gain) * (sig * (1.0 + gate * (1.0 - sig)))
        gate_grad_ref[span] = gate_grad.astype(jnp.bfloat16)
        wide = grad * silu
        total = total + jnp.sum(wide * normed, axis=0, keepdims=True)
        wide = wide * gain
        back = scale * (wide - normed * jnp.mean(wide * normed, axis=-1, keepdims=True))
        back = back.astype(jnp.bfloat16)
        back_ref[span] = back
        fresh = mm(scores_ref[span], back, ATB)
        step = mm(gq_ref[span], back, ATB)
        if later is not None:
            fresh = fresh + fine(end_ref[span], later)
            step = step + last_ref[i : i + 1, 0:1] * later
        later = step - fine(solved_ref[span, :DK], fresh, ATB)
    gain_grad_ref[...] = jnp.broadcast_to(total, (8, DV))
    feed_ref[0] = later.astype(jnp.bfloat16)


def delta_gate(grad, out, projected, gnorm_gain, front):
    inv, solved, scores, gq, end, last, agg = front
    length = solved.shape[0]
    heads = agg.shape[0]
    units = length // BLOCK
    f32, bf16 = jnp.float32, jnp.bfloat16
    shape = jax.ShapeDtypeStruct
    return local_call(gate_kernel, heads, "delta_gate", 0)(
        [
            per_head(DV, length),
            per_head(DV, length),
            per_head(projected.shape[1] // heads, length),
            pl.BlockSpec((1, DV), lambda h: (0, 0)),
            per_head(DK + DV, length),
            per_head(BLOCK, length),
            per_head(DK, length),
            per_head(DK, length),
            squeezed(units, 128),
        ],
        [
            (per_head(DV, length), shape((length, heads * DV), bf16)),
            (per_head(DV, length), shape((length, heads * DV), bf16)),
            (squeezed(8, DV), shape((heads, 8, DV), f32)),
            (stacked(DK, DV), shape((heads, DK, DV), bf16)),
        ],
        grad, out, projected, gnorm_gain[None], solved, scores, gq, end, last,
    )


def back_terms_kernel(
    proj_ref, halo_ref, mix_ref, mix_t_ref, taps_ref, rate_ref,
    inv_ref, solved_ref, scores_ref, gq_ref, end_ref, last_ref, state_ref, fresh_ref,
    back_ref, later_ref, gate_grad_ref,
    proj_grad_ref, tail_ref, edge_ref, mix_grad_ref, small_ref,
):
    units = proj_ref.shape[0] // BLOCK
    channels = halo_ref.shape[1]
    rows, columns = places(BLOCK)
    strictly = rows > columns
    suffix = (rows <= columns).astype(jnp.bfloat16)
    rate = jnp.exp(rate_ref[0:1, 0:1])
    later = later_ref[...]
    follow = jnp.zeros((8, channels), jnp.float32)
    conv_total = [jnp.zeros((1, channels), jnp.float32) for _ in range(CONV)]
    decay_total = jnp.zeros((1, 1), jnp.float32)
    for i in reversed(range(units)):
        span = slice(i * BLOCK, (i + 1) * BLOCK)
        edged = conv_rows(proj_ref, halo_ref, i)
        mixed, gate, active, query_norm, key_norm = unit_features(edged, taps_ref)
        query_act, key_act, value = active[:, :DK], active[:, DK : 2 * DK], active[:, 2 * DK :]
        query = query_act * query_norm * DK ** (-0.5)
        key = key_act * key_norm
        beta, ld, cumul, last, decay = unit_decays(mix_ref, mix_t_ref, rate, i)
        growth = jnp.exp(cumul)
        key_b = key.astype(jnp.bfloat16)
        key_parts = parts(key)
        gram = fine_parts(key_parts, key_parts, ABT)
        finish = last_ref[i : i + 1, 0:1]
        key_end = end_ref[span]
        gq = gq_ref[span]
        scores = scores_ref[span]
        solved = solved_ref[span]
        solved_b = solved.astype(jnp.bfloat16)
        state = state_ref[i]
        state_b = state.astype(jnp.bfloat16)
        fresh = fresh_ref[span]
        back = back_ref[span]
        later_b = later.astype(jnp.bfloat16)

        fresh_grad = mm(scores, back, ATB) + fine(key_end, later)
        fresh_grad_b = fresh_grad.astype(jnp.bfloat16)
        scores_grad = mm(back, fresh, ABT)
        gq_grad = mm(back, state_b, ABT)
        end_grad = mm(fresh, later_b, ABT)
        wide_grad = -mm(fresh_grad_b, state_b, ABT)
        finish_grad = jnp.sum(
            jnp.sum(state * later, axis=0, keepdims=True),
            axis=1,
            keepdims=True,
        )
        later = mm(gq, back, ATB) + finish * later - fine(solved[:, :DK], fresh_grad, ATB)

        sides_grad = mm(
            inv_ref[span],
            jnp.concatenate([wide_grad.astype(jnp.bfloat16), fresh_grad_b], axis=-1),
            ATB,
        )
        lower_grad = jnp.where(strictly, -mm(sides_grad, solved_b, ABT) * decay, 0.0)
        key_side = sides_grad[:, :DK]
        value_side = sides_grad[:, DK:]
        key_dot = jnp.sum(key_side * key, axis=-1, keepdims=True)
        gram_part = lower_grad * gram
        beta_grad = (
            growth * key_dot
            + jnp.sum(value_side * value, axis=-1, keepdims=True)
            + jnp.sum(gram_part, axis=-1, keepdims=True)
        )
        gram_grad = (beta * lower_grad).astype(jnp.bfloat16)
        pair_grad = (scores_grad * decay).astype(jnp.bfloat16)
        end_part = end_grad * key_end
        cross = beta * gram_part + scores_grad * scores
        end_dot = jnp.sum(end_part, axis=-1, keepdims=True)
        single = (
            (beta * growth) * key_dot
            + jnp.sum(gq_grad * gq, axis=-1, keepdims=True)
            - end_dot
        )
        last_grad = jnp.sum(end_dot, axis=0, keepdims=True) + finish * finish_grad
        cross_parts = parts(cross)
        above = mm(suffix, cross_parts[0]) + mm(suffix, cross_parts[1])
        single_parts = parts(jnp.broadcast_to(single, (BLOCK, 128)))
        single_sum = mm(suffix, single_parts[0]) + mm(suffix, single_parts[1])
        ld_grad = (
            jnp.sum(jnp.where(columns < rows, above, 0.0), axis=-1, keepdims=True)
            + single_sum[:, 0:1]
            + last_grad
        )
        query_grad = growth * gq_grad + mm(pair_grad, key_b)
        key_grad = (
            (beta * growth) * key_side
            + jnp.exp(last - cumul) * end_grad
            + mm(gram_grad, key_b)
            + mm(gram_grad, key_b, ATB)
            + mm(pair_grad, query, ATB)
        )
        value_grad = beta * value_side

        decay_total = decay_total + jnp.sum(ld_grad * ld, axis=0, keepdims=True)
        mix_grad_ref[span, 0:1] = beta_grad * beta * (1.0 - beta)
        mix_grad_ref[span, 1:2] = ld_grad * (-rate) * sigmoid(mix_ref[span, 1:2])

        query_scaled = query_grad * DK ** (-0.5)
        query_dot = jnp.sum(query_scaled * query_act, axis=-1, keepdims=True)
        query_back = query_norm * (query_scaled - query_act * (query_norm * query_norm * query_dot))
        key_sum = jnp.sum(key_grad * key_act, axis=-1, keepdims=True)
        key_back = key_norm * (key_grad - key_act * (key_norm * key_norm * key_sum))
        active_grad = jnp.concatenate([query_back, key_back, value_grad], axis=-1)
        mixed_grad = active_grad * gate * (1.0 + mixed * (1.0 - gate))
        for t in range(CONV):
            conv_total[t] = conv_total[t] + jnp.sum(mixed_grad * edged[t], axis=0, keepdims=True)
        longer = jnp.concatenate([mixed_grad, follow], 0)
        grad = longer[CONV - 1 : CONV - 1 + BLOCK] * taps_ref[0:1]
        for t in range(1, CONV):
            begin = CONV - 1 - t
            grad = grad + longer[begin : begin + BLOCK] * taps_ref[t : t + 1]
        proj_grad_ref[span, :channels] = grad.astype(jnp.bfloat16)
        if i == units - 1:
            tail_ref[...] = grad[BLOCK - 16 :]
        follow = mixed_grad[:8]
    first = jnp.concatenate([jnp.zeros((16, channels), jnp.float32), follow], 0)
    spill = first[CONV - 1 : CONV - 1 + 16] * taps_ref[0:1]
    for t in range(1, CONV):
        begin = CONV - 1 - t
        spill = spill + first[begin : begin + 16] * taps_ref[t : t + 1]
    edge_ref[...] = spill
    proj_grad_ref[:, channels:] = gate_grad_ref[...]
    small_ref[0:CONV] = jnp.concatenate(conv_total, 0)
    small_ref[CONV : CONV + 1] = jnp.broadcast_to(decay_total, (1, channels))


def delta_back(projected, halo, mix, mix_t, taps, decay_log, front, states, fresh, back, later, gate_grad):
    inv, solved, scores, gq, end, last, agg = front
    length = projected.shape[0]
    heads = taps.shape[0]
    channels = taps.shape[2]
    units = length // BLOCK
    f32, bf16 = jnp.float32, jnp.bfloat16
    shape = jax.ShapeDtypeStruct
    rate = jnp.broadcast_to(decay_log[:, None, None], (heads, 8, 128))
    span = channels + DV
    return local_call(back_terms_kernel, heads, "delta_back", 10)(
        [
            per_head(span, length),
            squeezed(16, channels),
            squeezed(length, 2),
            squeezed(2, length),
            squeezed(CONV, channels),
            squeezed(8, 128),
            per_head(BLOCK, length),
            per_head(DK + DV, length),
            per_head(BLOCK, length),
            per_head(DK, length),
            per_head(DK, length),
            squeezed(units, 128),
            squeezed(units, DK, DV),
            per_head(DV, length),
            per_head(DV, length),
            squeezed(DK, DV),
            per_head(DV, length),
        ],
        [
            (per_head(span, length), shape((length, heads * span), bf16)),
            (squeezed(16, channels), shape((heads, 16, channels), f32)),
            (squeezed(16, channels), shape((heads, 16, channels), f32)),
            (squeezed(length, 2), shape((heads, length, 2), f32)),
            (squeezed(8, channels), shape((heads, 8, channels), f32)),
        ],
        projected, halo, mix, mix_t, taps, rate, inv, solved, scores, gq, end, last, states, fresh,
        back, later, gate_grad,
    )


def ffn_kernel(
    tokens_ref, mixed_ref, gain_ref, up_w_ref, down_w_ref, grad_ref,
    hidden_ref, hidden_b_ref, swish_ref, gate_grad_ref, up_grad_ref, second_ref, gain_grad_ref,
):
    hidden = tokens_ref[...].astype(jnp.float32) + mixed_ref[...].astype(jnp.float32)
    hidden_ref[...] = hidden
    normed = hidden * lax.rsqrt(jnp.mean(hidden * hidden, axis=-1, keepdims=True) + EPSILON)
    hidden_b = (normed * gain_ref[...]).astype(jnp.bfloat16)
    hidden_b_ref[...] = hidden_b
    gate = mm(hidden_b, up_w_ref[0], ABT)
    up = mm(hidden_b, up_w_ref[1], ABT)
    act = mm(grad_ref[...], down_w_ref[...], ABT)
    sig = sigmoid(gate)
    silu = gate * sig
    swish_ref[...] = (silu * up).astype(jnp.bfloat16)
    gate_grad = (act * up * (sig * (1.0 + gate * (1.0 - sig)))).astype(jnp.bfloat16)
    up_grad = (act * silu).astype(jnp.bfloat16)
    gate_grad_ref[...] = gate_grad
    up_grad_ref[...] = up_grad
    second = mm(gate_grad, up_w_ref[0]) + mm(up_grad, up_w_ref[1])
    second_ref[...] = second.astype(jnp.bfloat16)
    total = jnp.sum(second * normed, axis=0, keepdims=True)
    gain_grad_ref[...] = jnp.broadcast_to(total, gain_grad_ref.shape)


def feed_forward(tokens, mixed, gain, up_w, down_w, grad_out):
    length, model = tokens.shape
    units = down_w.shape[0]
    steps = length // (2 * BLOCK)
    f32, bf16 = jnp.float32, jnp.bfloat16
    shape = jax.ShapeDtypeStruct

    def rows(width):
        return pl.BlockSpec((2 * BLOCK, width), lambda i: (i, 0))

    def whole(array):
        return pl.BlockSpec(array.shape, lambda i: (0,) * array.ndim)

    return pl.pallas_call(
        ffn_kernel,
        grid=(steps,),
        in_specs=[
            rows(model), rows(model), whole(gain[None]), whole(up_w), whole(down_w), rows(model),
        ],
        out_specs=[
            rows(model), rows(model), rows(units), rows(units), rows(units), rows(model),
            pl.BlockSpec((None, 8, model), lambda i: (i, 0, 0)),
        ],
        out_shape=[
            shape((length, model), f32),
            shape((length, model), bf16),
            shape((length, units), bf16),
            shape((length, units), bf16),
            shape((length, units), bf16),
            shape((length, model), bf16),
            shape((steps, 8, model), f32),
        ],
        compiler_params=pltpu.CompilerParams(vmem_limit_bytes=48 << 20),
        cost_estimate=cost(0),
        name="feed_forward",
    )(tokens, mixed, gain[None], up_w, down_w, grad_out)


def ffn_grads_kernel(hidden_ref, grad_ref, gate_ref, up_ref, swish_ref, out_ref):
    pieces, _, _, rows = out_ref.shape
    for j, (left, right) in enumerate(
        ((hidden_ref, gate_ref), (hidden_ref, up_ref), (grad_ref, swish_ref))
    ):
        value = mm(right[...], left[...], ATB).astype(jnp.bfloat16)
        for k in range(pieces):
            out_ref[k, j] = value[:, k * rows : (k + 1) * rows]


def ffn_grads(hidden_b, grad_out, gate_grad, up_grad, swish_b):
    length, model = hidden_b.shape
    units = swish_b.shape[1]
    count = lax.axis_size("seq")
    rows = model // count
    pieces = max(2 * BLOCK // rows, 1)
    part = rows * pieces
    columns = pl.BlockSpec((length, part), lambda i: (0, i))
    full = pl.BlockSpec((length, units), lambda i: (0, 0))
    return pl.pallas_call(
        ffn_grads_kernel,
        grid=(model // part,),
        in_specs=[columns, columns, full, full, full],
        out_specs=pl.BlockSpec((pieces, 3, units, rows), lambda i: (i, 0, 0, 0)),
        out_shape=jax.ShapeDtypeStruct((count, 3, units, rows), jnp.bfloat16),
        compiler_params=pltpu.CompilerParams(vmem_limit_bytes=48 << 20),
        cost_estimate=cost(0),
        name="ffn_grads",
    )(hidden_b, grad_out, gate_grad, up_grad, swish_b)


def early_kernel(normed_ref, gate_grad_ref, gated_ref, stream_ref, gate_ref, out_ref):
    count, rows, width = out_ref.shape
    gate_ref[...] = mm(normed_ref[...], gate_grad_ref[...], ATB).astype(jnp.bfloat16)
    heads = gated_ref.shape[1] // DV
    share = DV // count
    halves = stream_ref.shape[1] // width
    for h in range(heads):
        value = mm(gated_ref[:, h * DV : (h + 1) * DV], stream_ref[...], ATB).astype(jnp.bfloat16)
        for i in range(count):
            for j in range(halves):
                at = (h * halves + j) * share
                out_ref[i, at : at + share] = value[
                    i * share : (i + 1) * share, j * width : (j + 1) * width
                ]


def early_grads(normed_b, gate_grad, gated_b, stream_b):
    count = lax.axis_size("seq")
    model, width = stream_b.shape[1], gate_grad.shape[1]
    return pl.pallas_call(
        early_kernel,
        in_specs=[VMEM] * 4,
        out_specs=[VMEM] * 2,
        out_shape=[
            jax.ShapeDtypeStruct((model, width), jnp.bfloat16),
            jax.ShapeDtypeStruct((count, model // count, width), jnp.bfloat16),
        ],
        compiler_params=pltpu.CompilerParams(vmem_limit_bytes=40 << 20),
        cost_estimate=cost(0),
        name="early_grads",
    )(normed_b, gate_grad, gated_b, stream_b)


def rms_apply(values, gain):
    return values * lax.rsqrt(jnp.mean(values * values, axis=-1, keepdims=True) + EPSILON) * gain


def product(left, right, dims=((1,), (0,))):
    return lax.dot_general(left, right, (dims, ((), ())), preferred_element_type=jnp.float32)


def shards(
    block_input,
    norm1_gain,
    w_in,
    w_ba,
    conv_weight,
    decay_log,
    gnorm_gain,
    w_out,
    norm2_gain,
    w_up,
    w_down,
    grad_out,
):
    model = block_input.shape[1]
    heads = w_in.shape[1]
    span = w_in.shape[2]
    channels = conv_weight.shape[0]
    f32 = jnp.float32
    bf16 = jnp.bfloat16

    tail_rows = shifted(block_input[-16:], "seq", 1)
    tokens_wide = block_input.astype(f32)
    _, pull_first = jax.vjp(rms_apply, tokens_wide, norm1_gain)
    w_in_flat = w_in.reshape(model, heads * span)
    w_ba_flat = w_ba.reshape(model, 2 * heads)
    taps = jnp.transpose(conv_weight, (1, 2, 0))
    normed_b, projected, halo, mix, mix_t, *front = delta_front(
        block_input, tail_rows, norm1_gain, w_in_flat, w_ba, taps, decay_log
    )
    carried, maps = carried_forward(front[-1])
    layer_outputs, gated_b, states, fresh = delta_outer(front, carried, projected, gnorm_gain)
    w_out_rows = lax.optimization_barrier(w_out.reshape(w_out.shape[0], -1))
    w_out_flat = jnp.concatenate(
        [w_out_rows[:, h * model : (h + 1) * model] for h in range(heads)], 0
    )
    mixed = head_sum(product(gated_b, w_out_flat))
    hidden, hidden_b, swish_b, gate_b, up_b, second_part, gain_second = feed_forward(
        block_input, mixed, norm2_gain, jnp.transpose(w_up, (1, 2, 0)), w_down.T, grad_out
    )
    ffn_parts = ffn_grads(hidden_b, grad_out, gate_b, up_b, swish_b)
    second_b, ffn_parts = lax.optimization_barrier((second_part, ffn_parts))
    ffn_share = lax.psum_scatter(ffn_parts, "seq", scatter_dimension=0, tiled=True)
    _, pull_second = jax.vjp(rms_apply, hidden, norm2_gain)
    second_total = head_sum(second_b).astype(f32)
    hidden_grad, _ = pull_second(second_total)
    gain_second = jnp.sum(gain_second[:, 0], 0)
    stream = grad_out.astype(f32) + hidden_grad
    stream_b = stream.astype(bf16)
    gated_grad = product(stream_b, w_out_flat, ((1,), (1,)))
    back, gate_grad, gain_gated, feed = delta_gate(
        gated_grad, layer_outputs, projected, gnorm_gain, front
    )
    gate_columns, out_rows = early_grads(normed_b, gate_grad, gated_b, stream_b)
    bits = powers(lax.axis_size("seq"))
    shares = [
        Share(gate_columns, bits),
        Share(out_rows.reshape(gate_columns.shape), bits[1:] + bits[:1]),
    ]
    feed = begin(shares, feed)
    ffn_part = product(swish_b, w_down, ((1,), (1,)))
    later, ffn_total = carried_back(feed, maps, ffn_part)
    result = hidden + ffn_total.astype(f32)
    later = proceed(shares, later)
    back_outs = delta_back(
        projected, halo, mix, mix_t, taps, decay_log, front, states, fresh, back, later, gate_grad
    )
    proj_grad, tail, edge, mix_grad, small_grad = proceed(shares, back_outs)
    back_edge = shifted(edge, "seq", -1)
    fixed = (tail + back_edge).astype(bf16)
    for h in range(heads):
        proj_grad = lax.dynamic_update_slice(
            proj_grad, fixed[h], (proj_grad.shape[0] - 16, h * span)
        )
    mixer_b = jnp.concatenate(
        [mix_grad[h, :, c : c + 1] for c in range(2) for h in range(heads)], 1
    ).astype(bf16)
    first_part = product(proj_grad, w_in_flat, ((1,), (1,)))
    first_part = first_part + product(mixer_b, w_ba_flat, ((1,), (1,)))
    qkv_grad = jnp.concatenate(
        [proj_grad[:, h * span : h * span + channels] for h in range(heads)], 1
    )
    in_weight_grad = product(normed_b, qkv_grad, ((0,), (0,))).astype(bf16)
    gate_weight_grad = product(mixer_b, normed_b, ((0,), (0,)))
    gain_first = pull_first(first_part)[1]
    first_part, ffn_share = lax.optimization_barrier((first_part.astype(bf16), ffn_share))
    while any(share.order for share in shares):
        first_part = proceed(shares, first_part)
    first_part = proceed(shares, first_part)
    gate_share, out_share = shares[0].blocks, shares[1].blocks
    input_grad, small, (in_share,) = final_sums(
        first_part,
        block_input,
        norm1_gain,
        stream,
        [gain_first, gain_second, jnp.sum(gain_gated[:, 0], 0)],
        [small_grad[:, CONV, 0], small_grad[:, :CONV], gate_weight_grad],
        [in_weight_grad],
    )
    ffn_share = ffn_share[0].astype(f32)
    up_share, down_share = jnp.transpose(ffn_share[:2], (2, 0, 1)), ffn_share[2].T
    gain_one, gain_two, gain_norm, decay_total, conv_total, gate_total = small
    in_share = jnp.stack(
        [
            jnp.concatenate(
                [
                    in_share[:, h * channels : (h + 1) * channels],
                    gate_share[:, h * DV : (h + 1) * DV],
                ],
                1,
            )
            for h in range(heads)
        ],
        1,
    )
    out_share = out_share.reshape(heads, -1, DV // lax.axis_size("seq"), heads * DV)
    out_share = jnp.transpose(out_share, (2, 0, 1, 3)).reshape((-1,) + w_out.shape[1:])
    count = lax.axis_size("seq")
    place = lax.axis_index("seq")

    def mine(whole, axis):
        share = whole.shape[axis] // count
        return lax.dynamic_slice_in_dim(whole, place * share, share, axis)

    return (
        result,
        input_grad,
        gain_one,
        in_share,
        mine(gate_total, 1).T.reshape(model // count, 2, heads),
        jnp.transpose(mine(conv_total, 2), (2, 0, 1)),
        decay_total,
        gain_norm,
        out_share,
        gain_two,
        up_share,
        down_share,
    )


def solution(mesh):
    return jax.shard_map(
        shards,
        mesh=mesh,
        in_specs=(
            P("seq", None),
            P(),
            P(None, "head", None),
            P(None, None, "head"),
            P(None, "head", None),
            P("head"),
            P(),
            P(None, "head", None),
            P(),
            P(None, None, "head"),
            P(None, "head"),
            P("seq", None),
        ),
        out_specs=(
            P("seq", None),
            P("seq", None),
            P(),
            P("seq", "head", None),
            P("seq", None, "head"),
            P("seq", "head", None),
            P("head"),
            P(),
            P("seq", "head", None),
            P(),
            P("seq", None, "head"),
            P("seq", "head"),
        ),
        check_vma=False,
    )
```

```python
import functools

import jax
import jax.numpy as jnp
from jax import lax
from jax.experimental import pallas as pl
from jax.experimental.pallas import tpu as pltpu
from jax.sharding import PartitionSpec as P

DK = 128
DV = 256
CONV = 4
STRETCH = 64


EPSILON = 1e-06
NEGATIVE = -1e30


def shifted(block, axis, distance):
    devices = range(lax.axis_size(axis))
    route = [(i - distance, i) for i in devices if i - distance in devices]
    return lax.ppermute(block, axis, route)


MESH = pl.DeviceIdType.MESH
PIECES = 8


def flipped(index, bit):
    mine = (index // bit) % 2
    return index + bit - 2 * bit * mine, mine


def powers(count):
    return [2**i for i in range(count.bit_length() - 1)]


def remote(src, dst, send_sem, recv_sem, axis, device):
    return pltpu.make_async_remote_copy(
        src_ref=src,
        dst_ref=dst,
        send_sem=send_sem,
        recv_sem=recv_sem,
        device_id={axis: device},
        device_id_type=MESH,
    )


def greet(partners):
    barrier = pltpu.get_barrier_semaphore()
    for axis, partner in partners:
        pl.semaphore_signal(barrier, inc=1, device_id={axis: partner}, device_id_type=MESH)
    pl.semaphore_wait(barrier, len(partners))


def together(tasks, paces=None):
    live = [(task, pace) for task, pace in zip(tasks, paces or [1] * len(tasks))]
    while live:
        for entry in list(live):
            task, pace = entry
            try:
                for _ in range(pace):
                    next(task)
            except StopIteration:
                live.remove(entry)


def bit_partners(axis, count):
    me = lax.axis_index(axis)
    return [(axis, flipped(me, bit)[0]) for bit in powers(count)]


def head_sum_scratch(count, whole):
    piece = whole[2:]
    steps = len(powers(count)) - 1
    dma = pltpu.SemaphoreType.DMA
    return [
        pltpu.VMEM((PIECES,) + piece, jnp.bfloat16),
        pltpu.VMEM((steps, PIECES) + piece, jnp.bfloat16),
        pltpu.VMEM((steps, PIECES) + piece, jnp.bfloat16),
        dma((PIECES,)),
        dma((PIECES,)),
        dma((steps, PIECES)),
        dma((steps, PIECES)),
        dma((PIECES,)),
        dma((PIECES,)),
    ]


def head_sum_task(count, x_ref, out_ref, scratch):
    first, held, sums, near_s, near_r, far_s, far_r, back_s, back_r = scratch
    me = lax.axis_index("head")
    bits = powers(count)
    partner, side = flipped(me, 1)
    peers = [flipped(me, bit)[0] for bit in bits[1:]]

    def send(src, dst, send_sem, recv_sem, device):
        copy = remote(src, dst, send_sem, recv_sem, "head", device)
        copy.start()
        return copy

    def add(left, right):
        return (left.astype(jnp.float32) + right.astype(jnp.float32)).astype(jnp.bfloat16)

    near = [
        send(x_ref.at[1 - side, k], first.at[k], near_s.at[k], near_r.at[k], partner)
        for k in range(PIECES)
    ]
    yield
    steps = len(peers)
    copies = []
    for k in range(PIECES):
        near[k].wait()
        sums[0, k] = add(x_ref[side, k], first[k])
        copies.append(
            send(sums.at[0, k], held.at[0, k], far_s.at[0, k], far_r.at[0, k], peers[0])
        )
    yield
    for step in range(steps):
        later = []
        for k in range(PIECES):
            copies[k].wait()
            total = add(sums[step, k], held[step, k])
            if step < steps - 1:
                sums[step + 1, k] = total
                later.append(
                    send(
                        sums.at[step + 1, k],
                        held.at[step + 1, k],
                        far_s.at[step + 1, k],
                        far_r.at[step + 1, k],
                        peers[step + 1],
                    )
                )
            else:
                out_ref[side, k] = total
                later.append(
                    send(
                        out_ref.at[side, k],
                        out_ref.at[side, k],
                        back_s.at[k],
                        back_r.at[k],
                        partner,
                    )
                )
            yield
        copies = later
    for copy in copies:
        copy.wait()


def head_whole(shape):
    rows, width = shape
    return (2, PIECES, rows // (2 * PIECES), width)


def head_sum_kernel(count, x_ref, out_ref, *scratch):
    greet(bit_partners("head", count))
    together([head_sum_task(count, x_ref, out_ref, scratch)])


VMEM = pl.BlockSpec(memory_space=pltpu.VMEM)


def head_sum(part):
    count = lax.axis_size("head")
    whole = head_whole(part.shape)
    total = pl.pallas_call(
        functools.partial(head_sum_kernel, count),
        out_shape=jax.ShapeDtypeStruct(whole, jnp.bfloat16),
        in_specs=[VMEM],
        out_specs=VMEM,
        scratch_shapes=head_sum_scratch(count, whole),
        compiler_params=pltpu.CompilerParams(
            collective_id=0, has_side_effects=True, vmem_limit_bytes=16 << 20
        ),
        cost_estimate=cost(0),
        name="head_sum",
    )(part.astype(jnp.bfloat16).reshape(whole))
    return total.reshape(part.shape)


def gather_scratch(count):
    dma = pltpu.SemaphoreType.DMA
    line = max(count // 2, 1)
    return [dma((line,)), dma((line,)), dma((line,)), dma((line,)), dma((2 * line,)), dma((2 * line,))]


def line_partners(count):
    me = lax.axis_index("seq")
    up, down = lax.rem(me + 2, count), lax.rem(me + count - 2, count)
    return [("seq", flipped(me, 1)[0]), ("seq", up), ("seq", down)]


def gather_task(count, out_ref, scratch):
    up_s, up_r, dn_s, dn_r, x_s, x_r = scratch
    me = lax.axis_index("seq")
    line = count // 2
    place, half = me // 2, lax.rem(me, 2)
    other, _ = flipped(me, 1)

    def hop(position, send_sem, recv_sem, device):
        block = out_ref.at[2 * position + half]
        return remote(block, block, send_sem, recv_sem, "seq", device)

    def up(step):
        return hop(place - (step - 1), up_s.at[step], up_r.at[step], me + 2)

    def down(step):
        return hop(place + (step - 1), dn_s.at[step], dn_r.at[step], me - 2)

    def came_up(step):
        return hop(place - step, up_s.at[step], up_r.at[step], me - 2)

    def came_down(step):
        return hop(place + step, dn_s.at[step], dn_r.at[step], me + 2)

    def across(number, position):
        return hop(position, x_s.at[number], x_r.at[number], other)

    def from_across(number, position):
        block = out_ref.at[2 * position + 1 - half]
        return remote(block, block, x_s.at[number], x_r.at[number], "seq", other)

    def sends_up(step):
        return (place + 1 < line) & (place - (step - 1) >= 0)

    def sends_down(step):
        return (place - 1 >= 0) & (place + (step - 1) < line)

    for step in range(1, line):
        if step > 1:
            @pl.when(place - (step - 1) >= 0)
            def _():
                came_up(step - 1).wait_recv()

        @pl.when(sends_up(step))
        def _():
            up(step).start()

        if step > 1:

            @pl.when(place + (step - 1) < line)
            def _():
                came_down(step - 1).wait_recv()

        @pl.when(sends_down(step))
        def _():
            down(step).start()

        if step == 1:
            across(0, place).start()
        else:

            @pl.when(place - (step - 1) >= 0)
            def _():
                across(2 * step - 3, place - (step - 1)).start()

            @pl.when(place + (step - 1) < line)
            def _():
                across(2 * step - 2, place + (step - 1)).start()

        yield
    last = line - 1

    @pl.when(place - last >= 0)
    def _():
        came_up(last).wait_recv()
        across(2 * last - 1, place - last).start()

    @pl.when(place + last < line)
    def _():
        came_down(last).wait_recv()
        across(2 * last, place + last).start()

    yield
    for step in range(1, line):

        @pl.when(sends_up(step))
        def _():
            up(step).wait_send()

        @pl.when(sends_down(step))
        def _():
            down(step).wait_send()

    across(0, place).wait_send()
    from_across(0, place).wait_recv()
    for step in range(1, line):

        @pl.when(place - step >= 0)
        def _():
            across(2 * step - 1, place - step).wait_send()
            from_across(2 * step - 1, place - step).wait_recv()

        @pl.when(place + step < line)
        def _():
            across(2 * step, place + step).wait_send()
            from_across(2 * step, place + step).wait_recv()


def carry_kernel(count, heads, x_ref, state_ref, all_ref, *scratch):
    me = lax.axis_index("seq")
    greet(line_partners(count))
    all_ref[me] = x_ref[...]
    together([gather_task(count, all_ref, scratch)])
    for h in range(heads):
        state = all_ref[0, h, :, DK:].astype(jnp.float32)
        state = jnp.where(me > 0, state, jnp.zeros_like(state))
        for source in range(1, count - 1):
            moved = jnp.dot(
                all_ref[source, h, :, :DK],
                state.astype(jnp.bfloat16),
                preferred_element_type=jnp.float32,
            ) + all_ref[source, h, :, DK:].astype(jnp.float32)
            state = jnp.where(source < me, moved, state)
        state_ref[h] = state


def carried_forward(part):
    count = lax.axis_size("seq")
    heads = part.shape[0]
    return pl.pallas_call(
        functools.partial(carry_kernel, count, heads),
        out_shape=[
            jax.ShapeDtypeStruct((heads, DK, DV), jnp.float32),
            jax.ShapeDtypeStruct((count,) + part.shape, jnp.bfloat16),
        ],
        in_specs=[VMEM],
        out_specs=[VMEM, VMEM],
        scratch_shapes=gather_scratch(count),
        compiler_params=pltpu.CompilerParams(
            collective_id=1, has_side_effects=True, vmem_limit_bytes=24 << 20
        ),
        cost_estimate=cost(0),
        name="carry_forward",
    )(part.astype(jnp.bfloat16))


def back_kernel(count, ranks, heads, x_ref, maps_ref, part_ref, state_ref, total_ref, all_ref, *scratch):
    me = lax.axis_index("seq")
    n = len(gather_scratch(count))
    greet(line_partners(count) + bit_partners("head", ranks))
    all_ref[me] = x_ref[...]
    gather = gather_task(count, all_ref, scratch[:n])
    total = head_sum_task(ranks, part_ref, total_ref, scratch[n:])
    next(gather)
    next(total)
    next(total)
    together([gather, total])
    for h in range(heads):
        state = all_ref[count - 1, h].astype(jnp.float32)
        state = jnp.where(me < count - 1, state, jnp.zeros_like(state))
        for source in range(count - 2, 0, -1):
            moved = lax.dot_general(
                maps_ref[source, h, :, :DK],
                state.astype(jnp.bfloat16),
                (((0,), (0,)), ((), ())),
                preferred_element_type=jnp.float32,
            ) + all_ref[source, h].astype(jnp.float32)
            state = jnp.where(source > me, moved, state)
        state_ref[h] = state


def carried_back(feed, maps, part):
    count = lax.axis_size("seq")
    ranks = lax.axis_size("head")
    heads = feed.shape[0]
    whole = head_whole(part.shape)
    state, total = pl.pallas_call(
        functools.partial(back_kernel, count, ranks, heads),
        out_shape=[
            jax.ShapeDtypeStruct((heads, DK, DV), jnp.float32),
            jax.ShapeDtypeStruct(whole, jnp.bfloat16),
        ],
        in_specs=[VMEM] * 3,
        out_specs=[VMEM] * 2,
        scratch_shapes=[pltpu.VMEM((count,) + feed.shape, jnp.bfloat16)]
        + gather_scratch(count)
        + head_sum_scratch(ranks, whole),
        compiler_params=pltpu.CompilerParams(
            collective_id=2, has_side_effects=True, vmem_limit_bytes=32 << 20
        ),
        cost_estimate=cost(0),
        name="carry_back",
    )(feed.astype(jnp.bfloat16), maps, part.astype(jnp.bfloat16).reshape(whole))
    return state, total.reshape(part.shape)


def share_works(count, shapes):
    bits = powers(count)
    works = []
    for a, (_, rows, width) in enumerate(shapes):
        half = rows // 2
        works.append((a, pl.ds(0, half), bits, (half, width)))
        works.append((a, pl.ds(half, half), bits[1:] + bits[:1], (half, width)))
    return works


def share_scratch(count, shapes):
    steps = len(powers(count))
    works = share_works(count, shapes)
    dma = pltpu.SemaphoreType.DMA
    return (
        [pltpu.VMEM((steps, count // 2) + work[3], jnp.bfloat16) for work in works]
        + [pltpu.VMEM((max(steps - 1, 1), count // 4) + work[3], jnp.bfloat16) for work in works]
        + [dma((len(works), steps, count // 2)), dma((len(works), steps, count // 2))]
    )


def share_task(count, x_refs, out_refs, scratch):
    works = share_works(count, [x.shape for x in x_refs])
    recv_refs, send_refs = scratch[: len(works)], scratch[len(works) : 2 * len(works)]
    send_sem, recv_sem = scratch[2 * len(works) :]
    me = lax.axis_index("seq")
    bits = powers(count)
    partners = {bit: flipped(me, bit)[0] for bit in bits}

    def block(relative):
        index = me
        for bit in bits:
            if relative & bit:
                index = flipped(index, bit)[0]
        return index

    def kept(order, step):
        used = sum(order[:step])
        return [r for r in range(count) if r & used == 0]

    def slot(order, step, relative):
        return kept(order, step + 1).index(relative)

    def partial_sum(number, relative, step):
        a, rows, order, _ = works[number]
        total = x_refs[a][block(relative), rows, :].astype(jnp.float32)
        for earlier in range(step):
            total = total + recv_refs[number][earlier, slot(order, earlier, relative)].astype(
                jnp.float32
            )
        return total

    pending = {}
    for step in range(len(bits) + 1):
        for number, (a, rows, order, _) in enumerate(works):
            for copy in pending.pop(number, []):
                copy.wait()
            if step == len(bits):
                out_refs[a][rows, :] = partial_sum(number, 0, step)
                continue
            bit = order[step]
            started = []
            for relative in kept(order, step):
                if not relative & bit:
                    continue
                place = slot(order, step, relative - bit)
                if step == 0:
                    source = x_refs[a].at[block(relative), rows, :]
                else:
                    send_refs[number][step - 1, place] = partial_sum(
                        number, relative, step
                    ).astype(jnp.bfloat16)
                    source = send_refs[number].at[step - 1, place]
                copy = remote(
                    source,
                    recv_refs[number].at[step, place],
                    send_sem.at[number, step, place],
                    recv_sem.at[number, step, place],
                    "seq",
                    partners[bit],
                )
                copy.start()
                started.append(copy)
            pending[number] = started
        yield


def small_scratch(count, ranks, rows, both):
    dma = pltpu.SemaphoreType.DMA
    near, far = len(powers(ranks)), len(powers(count))
    return [
        pltpu.VMEM((near, both, 128), jnp.float32),
        pltpu.VMEM((far, rows, 128), jnp.float32),
        pltpu.VMEM((near, both, 128), jnp.float32),
        pltpu.VMEM((far, rows, 128), jnp.float32),
        dma((near,)),
        dma((near,)),
        dma((far,)),
        dma((far,)),
    ]


def small_task(count, ranks, both, x_ref, out_ref, scratch):
    got_h, got_s, sent_h, sent_s, hs, hr, ss, sr = scratch
    total = x_ref[:both]
    for i, (axis, partner) in enumerate(bit_partners("head", ranks)):
        sent_h[i] = total
        copy = remote(sent_h.at[i], got_h.at[i], hs.at[i], hr.at[i], axis, partner)
        copy.start()
        yield
        copy.wait()
        total = sent_h[i] + got_h[i]
    for i, (axis, partner) in enumerate(bit_partners("seq", count)):
        if i == 0:
            sent_s[0, :both] = total
            sent_s[0, both:] = x_ref[both:]
        else:
            sent_s[i] = sent_s[i - 1] + got_s[i - 1]
        copy = remote(sent_s.at[i], got_s.at[i], ss.at[i], sr.at[i], axis, partner)
        copy.start()
        yield
        copy.wait()
    last = len(powers(count)) - 1
    out_ref[...] = sent_s[last] + got_s[last]


def input_task(before, total_ref, tokens_ref, gain_ref, stream_ref, grad_ref):
    yield from before
    for side in range(total_ref.shape[0]):
        for k in range(total_ref.shape[1]):
            tokens = tokens_ref[side, k].astype(jnp.float32)
            scale = lax.rsqrt(jnp.mean(tokens * tokens, axis=-1, keepdims=True) + EPSILON)
            normed = tokens * scale
            wide = total_ref[side, k].astype(jnp.float32) * gain_ref[...]
            along = jnp.mean(wide * normed, axis=-1, keepdims=True)
            grad_ref[side, k] = stream_ref[side, k] + scale * (wide - normed * along)
        yield


def last_task(bits, send_refs, keep_refs, out_refs, scratch):
    *got_refs, send_sem, recv_sem = scratch
    me = lax.axis_index("seq")
    copies = []
    for i, bit in enumerate(bits):
        partner, _ = flipped(me, bit)
        copy = remote(
            send_refs[i], got_refs[i], send_sem.at[i], recv_sem.at[i], "seq", partner
        )
        copy.start()
        copies.append(copy)
    yield
    for i, copy in enumerate(copies):
        copy.wait()
        out_refs[i][...] = keep_refs[i][...].astype(jnp.float32) + got_refs[i][...].astype(
            jnp.float32
        )


def final_kernel(count, ranks, both, arrays, bits, *refs):
    k = len(bits)
    ins, refs = refs[: arrays + 5 + 2 * k], refs[arrays + 5 + 2 * k :]
    send_refs, keep_refs = ins[arrays + 5 : arrays + 5 + k], ins[arrays + 5 + k :]
    last_outs, last_scratch = refs[arrays + 2 : arrays + 2 + k], refs[len(refs) - k - 2 :]
    refs = ins[: arrays + 5] + refs[: arrays + 2] + refs[arrays + 2 + k : len(refs) - k - 2]
    part_ref, small_ref, tokens_ref, gain_ref, stream_ref, *x_refs = refs[: arrays + 5]
    grad_ref, sum_ref, *out_refs = refs[arrays + 5 : 2 * arrays + 7]
    total_ref, *scratch = refs[2 * arrays + 7 :]
    n = len(head_sum_scratch(ranks, (1, 1, 8, 128)))
    m = 8
    greet(bit_partners("seq", count) + bit_partners("head", ranks))
    shares = share_task(count, x_refs, out_refs, scratch[n + m :])
    tokens = input_task(
        head_sum_task(ranks, part_ref, total_ref, scratch[:n]),
        total_ref, tokens_ref, gain_ref, stream_ref, grad_ref,
    )
    small = small_task(count, ranks, both, small_ref, sum_ref, scratch[n : n + m])
    last = last_task(bits, send_refs, keep_refs, last_outs, last_scratch)
    next(tokens)
    next(last)
    next(shares)
    next(small)
    next(tokens)
    next(small)
    together([shares, tokens, small, last], [1, PIECES + 1, 2, 1])


def final_sums(part, tokens, gain, stream, wide, narrow, grads, lasts):
    count = lax.axis_size("seq")
    ranks = lax.axis_size("head")
    whole = head_whole(part.shape)

    def padded(flat):
        size = -(-flat.shape[0] // 1024) * 1024
        return jnp.pad(flat, (0, size - flat.shape[0])).reshape(size // 128, 128)

    wide_flat = padded(jnp.concatenate([a.reshape(-1) for a in wide]))
    narrow_flat = padded(jnp.concatenate([a.reshape(-1) for a in narrow]))
    both = wide_flat.shape[0]
    small = jnp.concatenate([wide_flat, narrow_flat])
    blocks = [
        g.astype(jnp.bfloat16).reshape(count, g.shape[0] // count, g.shape[1]) for g in grads
    ]
    bits = [share.order[0] for share in lasts]
    total, summed, *shares = pl.pallas_call(
        functools.partial(final_kernel, count, ranks, both, len(grads), bits),
        out_shape=[
            jax.ShapeDtypeStruct(whole, jnp.float32),
            jax.ShapeDtypeStruct(small.shape, jnp.float32),
        ]
        + [jax.ShapeDtypeStruct(b.shape[1:], jnp.float32) for b in blocks]
        + [jax.ShapeDtypeStruct(share.send.shape, jnp.float32) for share in lasts],
        in_specs=[VMEM] * (len(grads) + 5 + 2 * len(lasts)),
        out_specs=[VMEM] * (len(grads) + 2 + len(lasts)),
        scratch_shapes=[pltpu.VMEM(whole, jnp.bfloat16)]
        + head_sum_scratch(ranks, whole)
        + small_scratch(count, ranks, small.shape[0], both)
        + share_scratch(count, [b.shape for b in blocks])
        + [pltpu.VMEM(share.send.shape, jnp.bfloat16) for share in lasts]
        + [pltpu.SemaphoreType.DMA((len(lasts),))] * 2,
        compiler_params=pltpu.CompilerParams(
            collective_id=3, has_side_effects=True, vmem_limit_bytes=56 << 20
        ),
        cost_estimate=cost(30),
        name="final_sums",
    )(
        part.astype(jnp.bfloat16).reshape(whole),
        small,
        tokens.reshape(whole),
        gain[None],
        stream.reshape(whole),
        *blocks,
        *[share.send for share in lasts],
        *[share.keep for share in lasts],
    )
    outs = []
    for flat, group in ((summed[:both].reshape(-1), wide), (summed[both:].reshape(-1), narrow)):
        at = 0
        for a in group:
            outs.append(flat[at : at + a.size].reshape(a.shape))
            at += a.size
    return total.reshape(part.shape), outs, shares


class Share:
    def __init__(self, grad, order):
        count = lax.axis_size("seq")
        self.bits = powers(count)[::-1]
        self.order = list(order)
        self.count = count
        rows = grad.shape[0] // count
        self.blocks = grad.astype(jnp.bfloat16).reshape((2,) * len(self.bits) + (rows, -1))

    def cut(self):
        bit = self.order[0]
        axis = self.bits.index(bit)
        mine = lax.rem(lax.axis_index("seq") // bit, 2)
        self.keep = lax.dynamic_index_in_dim(self.blocks, mine, axis, False)
        self.send = lax.dynamic_index_in_dim(self.blocks, 1 - mine, axis, False)

    def start(self):
        bit = self.order.pop(0)
        self.bits.remove(bit)
        route = [(i, i ^ bit) for i in range(self.count)]
        self.got = lax.ppermute(self.send, "seq", route)

    def add(self):
        total = self.keep.astype(jnp.float32) + self.got.astype(jnp.float32)
        self.blocks = total if not self.order else total.astype(jnp.bfloat16)


def begin(shares, beside):
    for share in shares:
        share.cut()
    beside, sends = lax.optimization_barrier((beside, [share.send for share in shares]))
    for share, send in zip(shares, sends):
        share.send = send
        share.start()
    return beside


def proceed(shares, beside):
    beside, got = lax.optimization_barrier((beside, [share.got for share in shares]))
    for share, g in zip(shares, got):
        share.got = g
        share.add()
    left = [share for share in shares if share.order]
    return begin(left, beside) if left else beside


BLOCK = 128


def mm(left, right, dims=((1,), (0,))):
    return lax.dot_general(
        left.astype(jnp.bfloat16),
        right.astype(jnp.bfloat16),
        (dims, ((), ())),
        preferred_element_type=jnp.float32,
    )


AB = ((1,), (0,))
ABT = ((1,), (1,))
ATB = ((0,), (0,))


def parts(x):
    high = x.astype(jnp.bfloat16)
    return high, (x - high.astype(jnp.float32)).astype(jnp.bfloat16)


def fine_parts(left, right, dims=AB):
    lh, ll = left
    rh, rl = right
    return mm(lh, rh, dims) + (mm(lh, rl, dims) + mm(ll, rh, dims))


def fine(left, right, dims=AB):
    return fine_parts(parts(left), parts(right), dims)


def places(width):
    rows = lax.broadcasted_iota(jnp.int32, (width, width), 0)
    columns = lax.broadcasted_iota(jnp.int32, (width, width), 1)
    return rows, columns


def sigmoid(x):
    return 1.0 / (1.0 + jnp.exp(-x))


def softplus(x):
    return jnp.maximum(x, 0.0) + jnp.log1p(jnp.exp(-jnp.abs(x)))


def conv_rows(proj_ref, halo_ref, i):
    channels = halo_ref.shape[1]
    main = proj_ref[i * BLOCK : (i + 1) * BLOCK, :channels].astype(jnp.float32)
    if i == 0:
        ahead = halo_ref[...].astype(jnp.float32)
    else:
        ahead = proj_ref[i * BLOCK - 16 : i * BLOCK, :channels].astype(jnp.float32)
    rows = jnp.concatenate([ahead, main], 0)
    start = rows.shape[0] - BLOCK - (CONV - 1)
    return [rows[start + t : start + t + BLOCK] for t in range(CONV)]


def mixing(rows, taps_ref):
    mixed = rows[0] * taps_ref[0:1]
    for t in range(1, CONV):
        mixed = mixed + rows[t] * taps_ref[t : t + 1]
    return mixed


def unit_features(rows, taps_ref):
    mixed = mixing(rows, taps_ref)
    gate = sigmoid(mixed)
    active = mixed * gate
    query, key, value = active[:, :DK], active[:, DK : 2 * DK], active[:, 2 * DK :]
    query_norm = lax.rsqrt(jnp.sum(query * query, axis=-1, keepdims=True) + EPSILON)
    key_norm = lax.rsqrt(jnp.sum(key * key, axis=-1, keepdims=True) + EPSILON)
    return mixed, gate, active, query_norm, key_norm


def unit_decays(mix_ref, mix_t_ref, rate, i):
    span = slice(i * BLOCK, (i + 1) * BLOCK)
    beta = sigmoid(mix_ref[span, 0:1])
    ld_column = -rate * softplus(mix_ref[span, 1:2])
    ld_row = -rate * softplus(mix_t_ref[1:2, span])
    rows, columns = places(BLOCK)
    cumul = jnp.sum(jnp.where(rows >= columns, ld_row, 0.0), axis=1, keepdims=True)
    cumul_row = jnp.sum(jnp.where(rows <= columns, ld_column, 0.0), axis=0, keepdims=True)
    last = jnp.sum(ld_row, axis=1, keepdims=True)
    decay = jnp.exp(jnp.where(rows >= columns, cumul - cumul_row, NEGATIVE))
    return beta, ld_column, cumul, last, decay


def inverse_all(lowers):
    width = lowers[0].shape[0]
    rows, columns = places(width)

    def pairs(size):
        return (rows // size == columns // size + 1) & ((rows // size) % 2 == 1)

    eye = (rows == columns).astype(jnp.float32)
    inverses = [eye - jnp.where(pairs(1), lower, 0.0) for lower in lowers]
    size = 2
    while size < width:
        mask = pairs(size)
        cut = [parts(jnp.where(mask, lower, 0.0)) for lower in lowers]
        held = [parts(inverse) for inverse in inverses]
        middle = [fine_parts(a, b) for a, b in zip(held, cut)]
        inverses = [
            inverse - fine_parts(parts(m), a) for inverse, m, a in zip(inverses, middle, held)
        ]
        size *= 2
    return inverses


def front_kernel(
    tokens_ref, tail_ref, gain_ref, w_ref, w_ba_ref, w_ba_t_ref, taps_ref, rate_ref,
    normed_ref, proj_ref, halo_ref, mix_ref, mix_t_ref, inv_ref, solved_ref, scores_ref, gq_ref, end_ref, last_ref, agg_ref,
):
    def normed_of(ref):
        wide = ref[...].astype(jnp.float32)
        scale = lax.rsqrt(jnp.mean(wide * wide, axis=-1, keepdims=True) + EPSILON)
        return (wide * scale * gain_ref[...]).astype(jnp.bfloat16)

    @pl.when(pl.program_id(0) == 0)
    def _():
        normed_ref[...] = normed_of(tokens_ref)

    normed = normed_ref[...]
    proj_ref[...] = mm(normed, w_ref[...]).astype(jnp.bfloat16)
    halo = mm(normed_of(tail_ref), w_ref[:, : halo_ref.shape[1]])
    halo_ref[...] = halo.astype(jnp.bfloat16)
    mix_ref[...] = mm(normed, w_ba_ref[...])
    mix_t_ref[...] = mm(w_ba_t_ref[...], normed, ABT)
    units = proj_ref.shape[0] // BLOCK
    rows, columns = places(BLOCK)
    strictly = rows > columns
    rate = jnp.exp(rate_ref[0:1, 0:1])
    kept = []
    for i in range(units):
        _, _, active, query_norm, key_norm = unit_features(
            conv_rows(proj_ref, halo_ref, i), taps_ref
        )
        query = active[:, :DK] * query_norm * DK ** (-0.5)
        key = active[:, DK : 2 * DK] * key_norm
        beta, _, cumul, last, decay = unit_decays(mix_ref, mix_t_ref, rate, i)
        split = parts(key)
        gram = fine_parts(split, split, ABT)
        lower = jnp.where(strictly, beta * decay * gram, 0.0)
        growth = jnp.exp(cumul)
        scores = decay * mm(query, key, ABT)
        span = slice(i * BLOCK, (i + 1) * BLOCK)
        scores_ref[span] = scores
        gq_ref[span] = growth * query
        key_end = jnp.exp(last - cumul) * key
        end_ref[span] = key_end
        sides = jnp.concatenate([(beta * growth) * key, beta * active[:, 2 * DK :]], axis=-1)
        finish = jnp.exp(last)
        last_ref[i : i + 1] = jnp.broadcast_to(finish, (1, 128))
        kept.append((lower, sides.astype(jnp.bfloat16), key_end, finish))
    inverses = inverse_all([unit[0] for unit in kept])
    total = None
    for i in range(units):
        span = slice(i * BLOCK, (i + 1) * BLOCK)
        _, sides, key_end, finish = kept[i]
        inverse = inverses[i].astype(jnp.bfloat16)
        inv_ref[span] = inverse
        solved = mm(inverse, sides)
        solved_ref[span] = solved
        if total is None:
            fresh = jnp.concatenate([-solved[:, :DK], solved[:, DK:]], axis=-1)
            eye = (rows == columns).astype(jnp.float32)
            base = jnp.concatenate([finish * eye, jnp.zeros((DK, DV), jnp.float32)], axis=-1)
        else:
            moved = fine(solved[:, :DK], total)
            fresh = jnp.concatenate([-moved[:, :DK], solved[:, DK:] - moved[:, DK:]], axis=-1)
            base = finish * total
        total = base + fine(key_end, fresh, ATB)
    agg_ref[0] = total.astype(jnp.bfloat16)


def per_head(width, rows):
    return pl.BlockSpec((rows, width), lambda h: (0, h))


def stacked(*shape):
    return pl.BlockSpec((1,) + shape, lambda h: (h,) + (0,) * len(shape))


def squeezed(*shape):
    return pl.BlockSpec((None,) + shape, lambda h: (h,) + (0,) * len(shape))


def cost(micros):
    return pl.CostEstimate(flops=int(micros * 1e9), bytes_accessed=1 << 20, transcendentals=0)


def local_call(kernel, heads, name, micros):
    def call(ins, outs, *arrays):
        return pl.pallas_call(
            kernel,
            grid=(heads,),
            in_specs=ins,
            out_specs=[spec for spec, _ in outs],
            out_shape=[shape for _, shape in outs],
            compiler_params=pltpu.CompilerParams(vmem_limit_bytes=48 << 20),
            cost_estimate=cost(micros),
            name=name,
        )(*arrays)

    return call


def delta_front(tokens, tail, gain, w_in_flat, w_ba, taps, decay_log):
    length, model = tokens.shape
    heads = taps.shape[0]
    channels = taps.shape[2]
    f32, bf16 = jnp.float32, jnp.bfloat16
    units = length // BLOCK
    shape = jax.ShapeDtypeStruct

    def side(width, kind):
        return per_head(width, length), shape((length, heads * width), kind)

    rate = jnp.broadcast_to(decay_log[:, None, None], (heads, 8, 128))
    span = channels + DV
    alone = pl.BlockSpec((length, model), lambda h: (0, 0))
    return local_call(front_kernel, heads, "delta_front", 0)(
        [
            alone,
            pl.BlockSpec(tail.shape, lambda h: (0, 0)),
            pl.BlockSpec((1, model), lambda h: (0, 0)),
            per_head(span, model),
            squeezed(model, 2),
            squeezed(2, model),
            squeezed(CONV, channels),
            squeezed(8, 128),
        ],
        [
            (alone, shape((length, model), bf16)),
            side(span, bf16),
            (squeezed(16, channels), shape((heads, 16, channels), bf16)),
            (squeezed(length, 2), shape((heads, length, 2), f32)),
            (squeezed(2, length), shape((heads, 2, length), f32)),
            side(BLOCK, bf16),
            side(DK + DV, f32),
            side(BLOCK, f32),
            side(DK, f32),
            side(DK, f32),
            (squeezed(units, 128), shape((heads, units, 128), f32)),
            (stacked(DK, DK + DV), shape((heads, DK, DK + DV), bf16)),
        ],
        tokens, tail, gain[None], w_in_flat, jnp.transpose(w_ba, (2, 0, 1)),
        jnp.transpose(w_ba, (2, 1, 0)), taps, rate,
    )


def outer_kernel(
    solved_ref, scores_ref, gq_ref, end_ref, last_ref, carried_ref, proj_ref, gain_ref,
    out_ref, gated_ref, state_ref, fresh_ref,
):
    units = solved_ref.shape[0] // BLOCK
    state = carried_ref[...]
    for i in range(units):
        span = slice(i * BLOCK, (i + 1) * BLOCK)
        narrow = state.astype(jnp.bfloat16)
        state_ref[i] = state
        fresh = solved_ref[span, DK:] - mm(solved_ref[span, :DK], narrow)
        fresh = fresh.astype(jnp.bfloat16)
        fresh_ref[span] = fresh
        out = mm(gq_ref[span], narrow) + mm(scores_ref[span], fresh)
        if i < units - 1:
            state = last_ref[i : i + 1, 0:1] * state + mm(end_ref[span], fresh, ATB)
        out_ref[span] = out
        gate = proj_ref[span, 2 * DK + DV :].astype(jnp.float32)
        normed = out * lax.rsqrt(jnp.mean(out * out, axis=-1, keepdims=True) + EPSILON)
        gated_ref[span] = (normed * gain_ref[...] * (gate * sigmoid(gate))).astype(jnp.bfloat16)


def delta_outer(front, carried, projected, gnorm_gain):
    inv, solved, scores, gq, end, last, agg = front
    length = solved.shape[0]
    heads = carried.shape[0]
    units = length // BLOCK
    f32, bf16 = jnp.float32, jnp.bfloat16
    shape = jax.ShapeDtypeStruct
    return local_call(outer_kernel, heads, "delta_outer", 0)(
        [
            per_head(DK + DV, length),
            per_head(BLOCK, length),
            per_head(DK, length),
            per_head(DK, length),
            squeezed(units, 128),
            squeezed(DK, DV),
            per_head(projected.shape[1] // heads, length),
            pl.BlockSpec((1, DV), lambda h: (0, 0)),
        ],
        [
            (per_head(DV, length), shape((length, heads * DV), f32)),
            (per_head(DV, length), shape((length, heads * DV), bf16)),
            (squeezed(units, DK, DV), shape((heads, units, DK, DV), f32)),
            (per_head(DV, length), shape((length, heads * DV), bf16)),
        ],
        solved, scores, gq, end, last, carried, projected, gnorm_gain[None],
    )


def gate_kernel(
    grad_ref, out_ref, proj_ref, gain_ref, solved_ref, scores_ref, gq_ref, end_ref, last_ref,
    back_ref, gate_grad_ref, gain_grad_ref, feed_ref,
):
    units = solved_ref.shape[0] // BLOCK
    gain = gain_ref[...]
    total = jnp.zeros((1, DV), jnp.float32)
    later = None
    for i in reversed(range(units)):
        span = slice(i * BLOCK, (i + 1) * BLOCK)
        gate = proj_ref[span, 2 * DK + DV :].astype(jnp.float32)
        out = out_ref[span]
        grad = grad_ref[span]
        scale = lax.rsqrt(jnp.mean(out * out, axis=-1, keepdims=True) + EPSILON)
        normed = out * scale
        sig = sigmoid(gate)
        silu = gate * sig
        gate_grad = grad * (normed * gain) * (sig * (1.0 + gate * (1.0 - sig)))
        gate_grad_ref[span] = gate_grad.astype(jnp.bfloat16)
        wide = grad * silu
        total = total + jnp.sum(wide * normed, axis=0, keepdims=True)
        wide = wide * gain
        back = scale * (wide - normed * jnp.mean(wide * normed, axis=-1, keepdims=True))
        back = back.astype(jnp.bfloat16)
        back_ref[span] = back
        fresh = mm(scores_ref[span], back, ATB)
        step = mm(gq_ref[span], back, ATB)
        if later is not None:
            fresh = fresh + fine(end_ref[span], later)
            step = step + last_ref[i : i + 1, 0:1] * later
        later = step - fine(solved_ref[span, :DK], fresh, ATB)
    gain_grad_ref[...] = jnp.broadcast_to(total, (8, DV))
    feed_ref[0] = later.astype(jnp.bfloat16)


def delta_gate(grad, out, projected, gnorm_gain, front):
    inv, solved, scores, gq, end, last, agg = front
    length = solved.shape[0]
    heads = agg.shape[0]
    units = length // BLOCK
    f32, bf16 = jnp.float32, jnp.bfloat16
    shape = jax.ShapeDtypeStruct
    return local_call(gate_kernel, heads, "delta_gate", 0)(
        [
            per_head(DV, length),
            per_head(DV, length),
            per_head(projected.shape[1] // heads, length),
            pl.BlockSpec((1, DV), lambda h: (0, 0)),
            per_head(DK + DV, length),
            per_head(BLOCK, length),
            per_head(DK, length),
            per_head(DK, length),
            squeezed(units, 128),
        ],
        [
            (per_head(DV, length), shape((length, heads * DV), bf16)),
            (per_head(DV, length), shape((length, heads * DV), bf16)),
            (squeezed(8, DV), shape((heads, 8, DV), f32)),
            (stacked(DK, DV), shape((heads, DK, DV), bf16)),
        ],
        grad, out, projected, gnorm_gain[None], solved, scores, gq, end, last,
    )


def back_terms_kernel(
    proj_ref, halo_ref, mix_ref, mix_t_ref, taps_ref, rate_ref,
    inv_ref, solved_ref, scores_ref, gq_ref, end_ref, last_ref, state_ref, fresh_ref,
    back_ref, later_ref, gate_grad_ref,
    proj_grad_ref, tail_ref, edge_ref, mix_grad_ref, small_ref,
):
    units = proj_ref.shape[0] // BLOCK
    channels = halo_ref.shape[1]
    rows, columns = places(BLOCK)
    strictly = rows > columns
    suffix = (rows <= columns).astype(jnp.bfloat16)
    rate = jnp.exp(rate_ref[0:1, 0:1])
    later = later_ref[...]
    follow = jnp.zeros((8, channels), jnp.float32)
    conv_total = [jnp.zeros((1, channels), jnp.float32) for _ in range(CONV)]
    decay_total = jnp.zeros((1, 1), jnp.float32)
    for i in reversed(range(units)):
        span = slice(i * BLOCK, (i + 1) * BLOCK)
        edged = conv_rows(proj_ref, halo_ref, i)
        mixed, gate, active, query_norm, key_norm = unit_features(edged, taps_ref)
        query_act, key_act, value = active[:, :DK], active[:, DK : 2 * DK], active[:, 2 * DK :]
        query = query_act * query_norm * DK ** (-0.5)
        key = key_act * key_norm
        beta, ld, cumul, last, decay = unit_decays(mix_ref, mix_t_ref, rate, i)
        growth = jnp.exp(cumul)
        key_b = key.astype(jnp.bfloat16)
        key_parts = parts(key)
        gram = fine_parts(key_parts, key_parts, ABT)
        finish = last_ref[i : i + 1, 0:1]
        key_end = end_ref[span]
        gq = gq_ref[span]
        scores = scores_ref[span]
        solved = solved_ref[span]
        solved_b = solved.astype(jnp.bfloat16)
        state = state_ref[i]
        state_b = state.astype(jnp.bfloat16)
        fresh = fresh_ref[span]
        back = back_ref[span]
        later_b = later.astype(jnp.bfloat16)

        fresh_grad = mm(scores, back, ATB) + fine(key_end, later)
        fresh_grad_b = fresh_grad.astype(jnp.bfloat16)
        scores_grad = mm(back, fresh, ABT)
        gq_grad = mm(back, state_b, ABT)
        end_grad = mm(fresh, later_b, ABT)
        wide_grad = -mm(fresh_grad_b, state_b, ABT)
        finish_grad = jnp.sum(
            jnp.sum(state * later, axis=0, keepdims=True),
            axis=1,
            keepdims=True,
        )
        later = mm(gq, back, ATB) + finish * later - fine(solved[:, :DK], fresh_grad, ATB)

        sides_grad = mm(
            inv_ref[span],
            jnp.concatenate([wide_grad.astype(jnp.bfloat16), fresh_grad_b], axis=-1),
            ATB,
        )
        lower_grad = jnp.where(strictly, -mm(sides_grad, solved_b, ABT) * decay, 0.0)
        key_side = sides_grad[:, :DK]
        value_side = sides_grad[:, DK:]
        key_dot = jnp.sum(key_side * key, axis=-1, keepdims=True)
        gram_part = lower_grad * gram
        beta_grad = (
            growth * key_dot
            + jnp.sum(value_side * value, axis=-1, keepdims=True)
            + jnp.sum(gram_part, axis=-1, keepdims=True)
        )
        gram_grad = (beta * lower_grad).astype(jnp.bfloat16)
        pair_grad = (scores_grad * decay).astype(jnp.bfloat16)
        end_part = end_grad * key_end
        cross = beta * gram_part + scores_grad * scores
        end_dot = jnp.sum(end_part, axis=-1, keepdims=True)
        single = (
            (beta * growth) * key_dot
            + jnp.sum(gq_grad * gq, axis=-1, keepdims=True)
            - end_dot
        )
        last_grad = jnp.sum(end_dot, axis=0, keepdims=True) + finish * finish_grad
        cross_parts = parts(cross)
        above = mm(suffix, cross_parts[0]) + mm(suffix, cross_parts[1])
        single_parts = parts(jnp.broadcast_to(single, (BLOCK, 128)))
        single_sum = mm(suffix, single_parts[0]) + mm(suffix, single_parts[1])
        ld_grad = (
            jnp.sum(jnp.where(columns < rows, above, 0.0), axis=-1, keepdims=True)
            + single_sum[:, 0:1]
            + last_grad
        )
        query_grad = growth * gq_grad + mm(pair_grad, key_b)
        key_grad = (
            (beta * growth) * key_side
            + jnp.exp(last - cumul) * end_grad
            + mm(gram_grad, key_b)
            + mm(gram_grad, key_b, ATB)
            + mm(pair_grad, query, ATB)
        )
        value_grad = beta * value_side

        decay_total = decay_total + jnp.sum(ld_grad * ld, axis=0, keepdims=True)
        mix_grad_ref[span, 0:1] = beta_grad * beta * (1.0 - beta)
        mix_grad_ref[span, 1:2] = ld_grad * (-rate) * sigmoid(mix_ref[span, 1:2])

        query_scaled = query_grad * DK ** (-0.5)
        query_dot = jnp.sum(query_scaled * query_act, axis=-1, keepdims=True)
        query_back = query_norm * (query_scaled - query_act * (query_norm * query_norm * query_dot))
        key_sum = jnp.sum(key_grad * key_act, axis=-1, keepdims=True)
        key_back = key_norm * (key_grad - key_act * (key_norm * key_norm * key_sum))
        active_grad = jnp.concatenate([query_back, key_back, value_grad], axis=-1)
        mixed_grad = active_grad * gate * (1.0 + mixed * (1.0 - gate))
        for t in range(CONV):
            conv_total[t] = conv_total[t] + jnp.sum(mixed_grad * edged[t], axis=0, keepdims=True)
        longer = jnp.concatenate([mixed_grad, follow], 0)
        grad = longer[CONV - 1 : CONV - 1 + BLOCK] * taps_ref[0:1]
        for t in range(1, CONV):
            begin = CONV - 1 - t
            grad = grad + longer[begin : begin + BLOCK] * taps_ref[t : t + 1]
        proj_grad_ref[span, :channels] = grad.astype(jnp.bfloat16)
        if i == units - 1:
            tail_ref[...] = grad[BLOCK - 16 :]
        follow = mixed_grad[:8]
    first = jnp.concatenate([jnp.zeros((16, channels), jnp.float32), follow], 0)
    spill = first[CONV - 1 : CONV - 1 + 16] * taps_ref[0:1]
    for t in range(1, CONV):
        begin = CONV - 1 - t
        spill = spill + first[begin : begin + 16] * taps_ref[t : t + 1]
    edge_ref[...] = spill
    proj_grad_ref[:, channels:] = gate_grad_ref[...]
    small_ref[0:CONV] = jnp.concatenate(conv_total, 0)
    small_ref[CONV : CONV + 1] = jnp.broadcast_to(decay_total, (1, channels))


def delta_back(projected, halo, mix, mix_t, taps, decay_log, front, states, fresh, back, later, gate_grad):
    inv, solved, scores, gq, end, last, agg = front
    length = projected.shape[0]
    heads = taps.shape[0]
    channels = taps.shape[2]
    units = length // BLOCK
    f32, bf16 = jnp.float32, jnp.bfloat16
    shape = jax.ShapeDtypeStruct
    rate = jnp.broadcast_to(decay_log[:, None, None], (heads, 8, 128))
    span = channels + DV
    return local_call(back_terms_kernel, heads, "delta_back", 10)(
        [
            per_head(span, length),
            squeezed(16, channels),
            squeezed(length, 2),
            squeezed(2, length),
            squeezed(CONV, channels),
            squeezed(8, 128),
            per_head(BLOCK, length),
            per_head(DK + DV, length),
            per_head(BLOCK, length),
            per_head(DK, length),
            per_head(DK, length),
            squeezed(units, 128),
            squeezed(units, DK, DV),
            per_head(DV, length),
            per_head(DV, length),
            squeezed(DK, DV),
            per_head(DV, length),
        ],
        [
            (per_head(span, length), shape((length, heads * span), bf16)),
            (squeezed(16, channels), shape((heads, 16, channels), f32)),
            (squeezed(16, channels), shape((heads, 16, channels), f32)),
            (squeezed(length, 2), shape((heads, length, 2), f32)),
            (squeezed(8, channels), shape((heads, 8, channels), f32)),
        ],
        projected, halo, mix, mix_t, taps, rate, inv, solved, scores, gq, end, last, states, fresh,
        back, later, gate_grad,
    )


def ffn_kernel(
    tokens_ref, mixed_ref, gain_ref, up_w_ref, down_w_ref, grad_ref,
    hidden_ref, hidden_b_ref, swish_ref, gate_grad_ref, up_grad_ref, second_ref, gain_grad_ref,
):
    hidden = tokens_ref[...].astype(jnp.float32) + mixed_ref[...].astype(jnp.float32)
    hidden_ref[...] = hidden
    normed = hidden * lax.rsqrt(jnp.mean(hidden * hidden, axis=-1, keepdims=True) + EPSILON)
    hidden_b = (normed * gain_ref[...]).astype(jnp.bfloat16)
    hidden_b_ref[...] = hidden_b
    gate = mm(hidden_b, up_w_ref[0], ABT)
    up = mm(hidden_b, up_w_ref[1], ABT)
    act = mm(grad_ref[...], down_w_ref[...], ABT)
    sig = sigmoid(gate)
    silu = gate * sig
    swish_ref[...] = (silu * up).astype(jnp.bfloat16)
    gate_grad = (act * up * (sig * (1.0 + gate * (1.0 - sig)))).astype(jnp.bfloat16)
    up_grad = (act * silu).astype(jnp.bfloat16)
    gate_grad_ref[...] = gate_grad
    up_grad_ref[...] = up_grad
    second = mm(gate_grad, up_w_ref[0]) + mm(up_grad, up_w_ref[1])
    second_ref[...] = second.astype(jnp.bfloat16)
    total = jnp.sum(second * normed, axis=0, keepdims=True)
    gain_grad_ref[...] = jnp.broadcast_to(total, gain_grad_ref.shape)


def feed_forward(tokens, mixed, gain, up_w, down_w, grad_out):
    length, model = tokens.shape
    units = down_w.shape[0]
    steps = length // (2 * BLOCK)
    f32, bf16 = jnp.float32, jnp.bfloat16
    shape = jax.ShapeDtypeStruct

    def rows(width):
        return pl.BlockSpec((2 * BLOCK, width), lambda i: (i, 0))

    def whole(array):
        return pl.BlockSpec(array.shape, lambda i: (0,) * array.ndim)

    return pl.pallas_call(
        ffn_kernel,
        grid=(steps,),
        in_specs=[
            rows(model), rows(model), whole(gain[None]), whole(up_w), whole(down_w), rows(model),
        ],
        out_specs=[
            rows(model), rows(model), rows(units), rows(units), rows(units), rows(model),
            pl.BlockSpec((None, 8, model), lambda i: (i, 0, 0)),
        ],
        out_shape=[
            shape((length, model), f32),
            shape((length, model), bf16),
            shape((length, units), bf16),
            shape((length, units), bf16),
            shape((length, units), bf16),
            shape((length, model), bf16),
            shape((steps, 8, model), f32),
        ],
        compiler_params=pltpu.CompilerParams(vmem_limit_bytes=48 << 20),
        cost_estimate=cost(0),
        name="feed_forward",
    )(tokens, mixed, gain[None], up_w, down_w, grad_out)


def ffn_grads_kernel(hidden_ref, grad_ref, gate_ref, up_ref, swish_ref, out_ref):
    pieces, _, _, rows = out_ref.shape
    for j, (left, right) in enumerate(
        ((hidden_ref, gate_ref), (hidden_ref, up_ref), (grad_ref, swish_ref))
    ):
        value = mm(right[...], left[...], ATB).astype(jnp.bfloat16)
        for k in range(pieces):
            out_ref[k, j] = value[:, k * rows : (k + 1) * rows]


def ffn_grads(hidden_b, grad_out, gate_grad, up_grad, swish_b):
    length, model = hidden_b.shape
    units = swish_b.shape[1]
    count = lax.axis_size("seq")
    rows = model // count
    pieces = max(2 * BLOCK // rows, 1)
    part = rows * pieces
    columns = pl.BlockSpec((length, part), lambda i: (0, i))
    full = pl.BlockSpec((length, units), lambda i: (0, 0))
    return pl.pallas_call(
        ffn_grads_kernel,
        grid=(model // part,),
        in_specs=[columns, columns, full, full, full],
        out_specs=pl.BlockSpec((pieces, 3, units, rows), lambda i: (i, 0, 0, 0)),
        out_shape=jax.ShapeDtypeStruct((count, 3, units, rows), jnp.bfloat16),
        compiler_params=pltpu.CompilerParams(vmem_limit_bytes=48 << 20),
        cost_estimate=cost(0),
        name="ffn_grads",
    )(hidden_b, grad_out, gate_grad, up_grad, swish_b)


def early_kernel(normed_ref, gate_grad_ref, gated_ref, stream_ref, gate_ref, out_ref):
    count, rows, width = out_ref.shape
    gate_ref[...] = mm(normed_ref[...], gate_grad_ref[...], ATB).astype(jnp.bfloat16)
    heads = gated_ref.shape[1] // DV
    share = DV // count
    halves = stream_ref.shape[1] // width
    for h in range(heads):
        value = mm(gated_ref[:, h * DV : (h + 1) * DV], stream_ref[...], ATB).astype(jnp.bfloat16)
        for i in range(count):
            for j in range(halves):
                at = (h * halves + j) * share
                out_ref[i, at : at + share] = value[
                    i * share : (i + 1) * share, j * width : (j + 1) * width
                ]


def early_grads(normed_b, gate_grad, gated_b, stream_b):
    count = lax.axis_size("seq")
    model, width = stream_b.shape[1], gate_grad.shape[1]
    return pl.pallas_call(
        early_kernel,
        in_specs=[VMEM] * 4,
        out_specs=[VMEM] * 2,
        out_shape=[
            jax.ShapeDtypeStruct((model, width), jnp.bfloat16),
            jax.ShapeDtypeStruct((count, model // count, width), jnp.bfloat16),
        ],
        compiler_params=pltpu.CompilerParams(vmem_limit_bytes=40 << 20),
        cost_estimate=cost(0),
        name="early_grads",
    )(normed_b, gate_grad, gated_b, stream_b)


def rms_apply(values, gain):
    return values * lax.rsqrt(jnp.mean(values * values, axis=-1, keepdims=True) + EPSILON) * gain


def product(left, right, dims=((1,), (0,))):
    return lax.dot_general(left, right, (dims, ((), ())), preferred_element_type=jnp.float32)


def shards(
    block_input,
    norm1_gain,
    w_in,
    w_ba,
    conv_weight,
    decay_log,
    gnorm_gain,
    w_out,
    norm2_gain,
    w_up,
    w_down,
    grad_out,
):
    model = block_input.shape[1]
    heads = w_in.shape[1]
    span = w_in.shape[2]
    channels = conv_weight.shape[0]
    f32 = jnp.float32
    bf16 = jnp.bfloat16

    tail_rows = shifted(block_input[-16:], "seq", 1)
    tokens_wide = block_input.astype(f32)
    _, pull_first = jax.vjp(rms_apply, tokens_wide, norm1_gain)
    w_in_flat = w_in.reshape(model, heads * span)
    w_ba_flat = w_ba.reshape(model, 2 * heads)
    taps = jnp.transpose(conv_weight, (1, 2, 0))
    normed_b, projected, halo, mix, mix_t, *front = delta_front(
        block_input, tail_rows, norm1_gain, w_in_flat, w_ba, taps, decay_log
    )
    carried, maps = carried_forward(front[-1])
    layer_outputs, gated_b, states, fresh = delta_outer(front, carried, projected, gnorm_gain)
    w_out_rows = lax.optimization_barrier(w_out.reshape(w_out.shape[0], -1))
    w_out_flat = jnp.concatenate(
        [w_out_rows[:, h * model : (h + 1) * model] for h in range(heads)], 0
    )
    mixed = head_sum(product(gated_b, w_out_flat))
    hidden, hidden_b, swish_b, gate_b, up_b, second_part, gain_second = feed_forward(
        block_input, mixed, norm2_gain, jnp.transpose(w_up, (1, 2, 0)), w_down.T, grad_out
    )
    ffn_parts = ffn_grads(hidden_b, grad_out, gate_b, up_b, swish_b)
    second_b, ffn_parts = lax.optimization_barrier((second_part, ffn_parts))
    ffn_share = lax.psum_scatter(ffn_parts, "seq", scatter_dimension=0, tiled=True)
    _, pull_second = jax.vjp(rms_apply, hidden, norm2_gain)
    second_total = head_sum(second_b).astype(f32)
    hidden_grad, _ = pull_second(second_total)
    gain_second = jnp.sum(gain_second[:, 0], 0)
    stream = grad_out.astype(f32) + hidden_grad
    stream_b = stream.astype(bf16)
    gated_grad = product(stream_b, w_out_flat, ((1,), (1,)))
    back, gate_grad, gain_gated, feed = delta_gate(
        gated_grad, layer_outputs, projected, gnorm_gain, front
    )
    gate_columns, out_rows = early_grads(normed_b, gate_grad, gated_b, stream_b)
    bits = powers(lax.axis_size("seq"))
    shares = [
        Share(gate_columns, bits),
        Share(out_rows.reshape(gate_columns.shape), bits[1:] + bits[:1]),
    ]
    ffn_part = product(swish_b, w_down, ((1,), (1,)))
    later, ffn_total = carried_back(feed, maps, ffn_part)
    result = hidden + ffn_total.astype(f32)
    later = begin(shares, later)
    back_outs = delta_back(
        projected, halo, mix, mix_t, taps, decay_log, front, states, fresh, back, later, gate_grad
    )
    proj_grad, tail, edge, mix_grad, small_grad = proceed(shares, back_outs)
    back_edge = shifted(edge, "seq", -1)
    fixed = (tail + back_edge).astype(bf16)
    for h in range(heads):
        proj_grad = lax.dynamic_update_slice(
            proj_grad, fixed[h], (proj_grad.shape[0] - 16, h * span)
        )
    mixer_b = jnp.concatenate(
        [mix_grad[h, :, c : c + 1] for c in range(2) for h in range(heads)], 1
    ).astype(bf16)
    first_part = product(proj_grad, w_in_flat, ((1,), (1,)))
    first_part = first_part + product(mixer_b, w_ba_flat, ((1,), (1,)))
    qkv_grad = jnp.concatenate(
        [proj_grad[:, h * span : h * span + channels] for h in range(heads)], 1
    )
    in_weight_grad = product(normed_b, qkv_grad, ((0,), (0,))).astype(bf16)
    gate_weight_grad = product(mixer_b, normed_b, ((0,), (0,)))
    gain_first = pull_first(first_part)[1]
    first_part, ffn_share = lax.optimization_barrier((first_part.astype(bf16), ffn_share))
    while len(shares[0].order) > 1:
        first_part = proceed(shares, first_part)
    first_part, got = lax.optimization_barrier((first_part, [share.got for share in shares]))
    for share, g in zip(shares, got):
        share.got = g
        share.add()
        share.cut()
    input_grad, small, (in_share, gate_share, out_share) = final_sums(
        first_part,
        block_input,
        norm1_gain,
        stream,
        [gain_first, gain_second, jnp.sum(gain_gated[:, 0], 0)],
        [small_grad[:, CONV, 0], small_grad[:, :CONV], gate_weight_grad],
        [in_weight_grad],
        shares,
    )
    ffn_share = ffn_share[0].astype(f32)
    up_share, down_share = jnp.transpose(ffn_share[:2], (2, 0, 1)), ffn_share[2].T
    gain_one, gain_two, gain_norm, decay_total, conv_total, gate_total = small
    in_share = jnp.stack(
        [
            jnp.concatenate(
                [
                    in_share[:, h * channels : (h + 1) * channels],
                    gate_share[:, h * DV : (h + 1) * DV],
                ],
                1,
            )
            for h in range(heads)
        ],
        1,
    )
    out_share = out_share.reshape(heads, -1, DV // lax.axis_size("seq"), heads * DV)
    out_share = jnp.transpose(out_share, (2, 0, 1, 3)).reshape((-1,) + w_out.shape[1:])
    count = lax.axis_size("seq")
    place = lax.axis_index("seq")

    def mine(whole, axis):
        share = whole.shape[axis] // count
        return lax.dynamic_slice_in_dim(whole, place * share, share, axis)

    return (
        result,
        input_grad,
        gain_one,
        in_share,
        mine(gate_total, 1).T.reshape(model // count, 2, heads),
        jnp.transpose(mine(conv_total, 2), (2, 0, 1)),
        decay_total,
        gain_norm,
        out_share,
        gain_two,
        up_share,
        down_share,
    )


def solution(mesh):
    return jax.shard_map(
        shards,
        mesh=mesh,
        in_specs=(
            P("seq", None),
            P(),
            P(None, "head", None),
            P(None, None, "head"),
            P(None, "head", None),
            P("head"),
            P(),
            P(None, "head", None),
            P(),
            P(None, None, "head"),
            P(None, "head"),
            P("seq", None),
        ),
        out_specs=(
            P("seq", None),
            P("seq", None),
            P(),
            P("seq", "head", None),
            P("seq", None, "head"),
            P("seq", "head", None),
            P("head"),
            P(),
            P("seq", "head", None),
            P(),
            P("seq", None, "head"),
            P("seq", "head"),
        ),
        check_vma=False,
    )
```
